32 devices in a mesh: mesh: 8 (over y, x, core), pts: 4 (over z).
Axes of the slice: x: 2, y: 2, z: 4, core: 2. Of those that a mesh axis runs over, the one named last changes fastest.
Arguments:
- features: float32 [7, 65536], P(None, ('mesh', 'pts')), may hold values from -6 to 6
- targets: float32 [4, 65536], P(None, ('mesh', 'pts')), may hold values from -6 to 6
- mesh_slot: int32 [65536], P(('mesh', 'pts')), may hold values from 0 to 4, as said below
- matrices: float32 [11, 256, 256], P(None, None, ('mesh', 'pts')), may hold values from -0.375 to 0.375
- matrices_moment: float32 [11, 256, 256], P(None, None, ('mesh', 'pts')), may hold values from -1.9073486e-05 to 1.9073486e-05
- matrices_second: float32 [11, 256, 256], P(None, None, ('mesh', 'pts')), may hold values from 7.166191e-12 to 2.839434e-11
- smalls: float32 [2, 5120], P(None, ('mesh', 'pts')), may hold values from -1 to 1
- smalls_moment: float32 [2, 5120], P(None, ('mesh', 'pts')), may hold values from -1.9073486e-05 to 1.9073486e-05
- smalls_second: float32 [2, 5120], P(None, ('mesh', 'pts')), may hold values from 7.166191e-12 to 2.839434e-11
- vectors: float32 [33, 256], P(None, ('mesh', 'pts')), may hold values from -2 to 2
- vectors_moment: float32 [33, 256], P(None, ('mesh', 'pts')), may hold values from -7.6293945e-05 to 7.6293945e-05
- vectors_second: float32 [33, 256], P(None, ('mesh', 'pts')), may hold values from 1.1357736e-10 to 4.597179e-10
Outputs:
- loss: float32 [], replicated
- grad_norm: float32 [], replicated
- matrices_moment_new: float32 [11, 256, 256], P(None, None, ('mesh', 'pts'))
- matrices_second_new: float32 [11, 256, 256], P(None, None, ('mesh', 'pts'))
- matrices_new: float32 [11, 256, 256], P(None, None, ('mesh', 'pts'))
- smalls_moment_new: float32 [2, 5120], P(None, ('mesh', 'pts'))
- smalls_second_new: float32 [2, 5120], P(None, ('mesh', 'pts'))
- smalls_new: float32 [2, 5120], P(None, ('mesh', 'pts'))
- vectors_moment_new: float32 [33, 256], P(None, ('mesh', 'pts'))
- vectors_second_new: float32 [33, 256], P(None, ('mesh', 'pts'))
- vectors_new: float32 [33, 256], P(None, ('mesh', 'pts'))
The draws below stay inside these ranges and needn't reach their ends.
Inputs may be any that keep to these rules, and one draw needn't show every extreme that they name: `mesh_slot`: within each group of 8192 slots, each of the 4 meshes occupies one contiguous run of slots with at least one point; the value 4 marks padding, found only at the group's end, on the group's last device. One mesh of each group has points on every device of the group; each of the others lies wholly within the slots of one device.
All inputs are finite; a program needn't handle non-finite values.
Results may differ from the reference program's by a relative error of at most 0.0015.
The reference program's roundings to bfloat16 on the way count: a program that leaves them out, or rounds other values in their place, can miss the bound.
Values may be sent and summed in bfloat16 or wider, within the bound.
No kernel may reach another device: no remote copies, remote signals or barrier semaphores. Data moves between devices by JAX's collectives and lax.ppermute only.
A program may use at most 192 MiB of HBM per device.

```python
import math
import jax
import jax.numpy as jnp
from jax import lax

D = 256
H = 8
DH = 32
S = 64
F_IN = 7
F_OUT = 4
LAYERS = 2
MESH_GRP = 4
STEP = 5
P_DEV = 2048
GROUP_PTS = 8192
MESHES = 32
POINTS = 65536
SMALLW = 5120
VROWS = 33
NPARAM = 739584


def draw_mesh_slot(key, part):
    groups = MESHES // MESH_GRP

    def one_group(sub_key):
        key_len, key_pad, key_perm = jax.random.split(sub_key, 3)
        sizes_small = jax.random.randint(key_len, (MESH_GRP - 1,), P_DEV // 8, P_DEV // 4 + 1)
        padding = jax.random.randint(key_pad, (), 1, P_DEV // 4 + 1)
        slot_order = jax.random.permutation(key_perm, MESH_GRP)
        bounds = jnp.cumsum(sizes_small)
        places = jnp.arange(GROUP_PTS)
        rank_idx = jnp.sum((places[:, None] >= bounds[None, :]).astype(jnp.int32), 1)
        labels = slot_order[rank_idx]
        return jnp.where(places >= GROUP_PTS - padding, MESH_GRP, labels).astype(jnp.int32)
    return jax.vmap(one_group)(jax.random.split(key, groups)).reshape(-1)


def draw_vectors(key, part):
    row_kinds = []
    for layer_idx in range(LAYERS):
        row_kinds = row_kinds + [1, 0, 0, 0, 0, 1, 0, 0, 0]
    row_kinds = row_kinds + [0, 0, 1, 0] + [2] * F_IN + [3] * F_OUT
    row_kind = jnp.array(row_kinds, jnp.int32)[:, None]
    full_shape = (len(row_kinds), D)
    jitter = jnp.clip(jax.random.normal(key, full_shape, jnp.float32), -4.0, 4.0)
    scaled = jnp.where(row_kind == 1, 1.0 + 0.2 * jitter, 0.2 * jitter)
    scaled = jnp.where(row_kind == 2, jitter * F_IN ** (-0.5), scaled)
    scaled = jnp.where(row_kind == 3, jitter * D ** (-0.5), scaled)
    return scaled.astype(jnp.float32)


def steps_of(own_key, extent, pieces, least, high):
    def one(position, parts):
        draws = jax.random.uniform(jax.random.fold_in(jax.random.fold_in(own_key, 6), position), (parts,), jnp.float32, least / len(pieces), high / len(pieces))
        return jnp.repeat(jnp.exp(draws), extent[position] // parts).reshape((-1,) + (1,) * (len(extent) - position - 1))

    gain = one(*pieces[0])
    for cut in pieces[1:]:
        gain = gain * one(*cut)
    return gain


def bell_draw(key, dims, deviation, limit, cuts=(), dtype=jnp.bfloat16):
    level = steps_of(key, dims, cuts, -0.22, 0.18) if cuts else 1.0
    result = jax.random.normal(key, dims, jnp.float32) * deviation * level
    return jnp.minimum(jnp.maximum(result, -limit), limit).astype(dtype)


def setup_inputs(seed: int = 0) -> dict:
    key_list = jax.random.split(jax.random.key(seed), 13)
    return {
        "features": bell_draw(key_list[0], (F_IN, POINTS), 1.0, 6.0, ((1, 32),), jnp.float32),
        "targets": bell_draw(key_list[1], (F_OUT, POINTS), 1.0, 6.0, ((1, 32),), jnp.float32),
        "mesh_slot": draw_mesh_slot(jax.random.fold_in(key_list[12], 71), 0),
        "matrices": bell_draw(key_list[3], (5 * LAYERS + 1, D, D), D ** -0.5, 0.375, ((2, 32),), jnp.float32),
        "matrices_moment": bell_draw(key_list[4], (5 * LAYERS + 1, D, D), (0.0011 / NPARAM ** 0.5), 1.9073486328125e-05, ((2, 32),), jnp.float32),
        "matrices_second": jnp.clip(jnp.exp(math.log(2.839434069812352e-11) - 1.3768156 * jax.random.uniform(key_list[5], (5 * LAYERS + 1, D, D), jnp.float32) ** steps_of(key_list[5], (5 * LAYERS + 1, D, D), ((2, 32),), -0.2, 0.2)), 7.1661908178366485e-12, 2.839434069812352e-11),
        "smalls": bell_draw(key_list[6], (LAYERS, SMALLW), DH ** -0.5, 1.0, ((1, 32),), jnp.float32),
        "smalls_moment": bell_draw(key_list[7], (LAYERS, SMALLW), (0.0011 / NPARAM ** 0.5), 1.9073486328125e-05, ((1, 32),), jnp.float32),
        "smalls_second": jnp.clip(jnp.exp(math.log(2.839434069812352e-11) - 1.3768156 * jax.random.uniform(key_list[8], (LAYERS, SMALLW), jnp.float32) ** steps_of(key_list[8], (LAYERS, SMALLW), ((1, 32),), -0.2, 0.2)), 7.1661908178366485e-12, 2.839434069812352e-11),
        "vectors": draw_vectors(jax.random.fold_in(key_list[12], 71), 0),
        "vectors_moment": bell_draw(key_list[10], (VROWS, D), (0.0044 / NPARAM ** 0.5), 7.62939453125e-05, ((1, 32),), jnp.float32),
        "vectors_second": jnp.clip(jnp.exp(math.log(4.597179026344378e-10) - 1.39812883 * jax.random.uniform(key_list[11], (VROWS, D), jnp.float32) ** steps_of(key_list[11], (VROWS, D), ((1, 32),), -0.2, 0.2)), 1.1357736279249409e-10, 4.597179026344378e-10),
    }


EPS_NORM = 1e-05
EPS_SLICE = 1e-05
EPS_LOSS = 1e-06
CLIP = 0.01
LEARN = 0.03
BETA_ONE = 0.9
BETA_TWO = 0.95
EPS_ADAM = 1e-08
DECAY = 0.1
HIGH = lax.Precision.HIGHEST

@jax.custom_vjp
def low(v):
    return lax.optimization_barrier(v.astype(jnp.bfloat16)).astype(jnp.float32)

@jax.custom_vjp
def low_back(v):
    return v

def low_keep(v):
    return (low(v), None)

def low_pass(kept, grad):
    return (grad,)

def back_keep(v):
    return (v, None)

def back_low(kept, grad):
    return (low(grad),)
low.defvjp(low_keep, low_pass)
low_back.defvjp(back_keep, back_low)

def layer_norm(values, gains, shifts):
    row_mean = lax.optimization_barrier(jnp.mean(values, -1, keepdims=True))
    centred = values - row_mean
    row_var = lax.optimization_barrier(jnp.mean(centred * centred, -1, keepdims=True))
    return centred * lax.rsqrt(row_var + EPS_NORM) * gains + shifts

def matmul(left, right):
    return low_back(jnp.dot(left, right, precision=HIGH))

def einsum_hi(form, *operands):
    return jnp.einsum(form, *operands, precision=HIGH)

def layer_fwd(hidden, weights, small, vec, onehot, valid):
    count = hidden.shape[0]
    normed = low(layer_norm(hidden, vec[0], vec[1]))
    x_mid = low(matmul(normed, weights[0]) + vec[2]).reshape(count, H, DH)
    f_mid = low(matmul(normed, weights[1]) + vec[3]).reshape(count, H, DH)
    logits = low_back(einsum_hi('phc,cs->phs', x_mid, small[:, :S]))
    probs = low(jax.nn.softmax(logits, -1) * valid[:, None, None])
    numer = low_back(einsum_hi('pm,phs,phc->mhsc', onehot, probs, f_mid))
    denom = einsum_hi('pm,phs->mhs', onehot, probs)
    tokens = low(numer / (denom[..., None] + EPS_SLICE))
    queries = low(low_back(einsum_hi('mhsc,cd->mhsd', tokens, small[:, S:S + DH])))
    keys_low = low(low_back(einsum_hi('mhsc,cd->mhsd', tokens, small[:, S + DH:S + 2 * DH])))
    values_low = low(low_back(einsum_hi('mhsc,cd->mhsd', tokens, small[:, S + 2 * DH:])))
    scores = low_back(einsum_hi('mhsd,mhtd->mhst', queries, keys_low) * DH ** (-0.5))
    attn = low(jax.nn.softmax(scores, -1))
    slice_out = low(low_back(einsum_hi('mhst,mhtd->mhsd', attn, values_low)))
    spread = low(low_back(einsum_hi('pm,phs,mhsc->phc', onehot, probs, slice_out))).reshape(count, D)
    hidden = hidden + matmul(spread, weights[2]) + vec[4]
    normed_two = low(layer_norm(hidden, vec[5], vec[6]))
    activ = low(jax.nn.gelu(matmul(normed_two, weights[3]) + vec[7]))
    return hidden + matmul(activ, weights[4]) + vec[8]

def group_loss(matrices, smalls, vectors, feat, targ, slot):
    mats_low = low(matrices)
    small_low = low(smalls).reshape(LAYERS, DH, S + 3 * DH)
    vec_low = low(vectors)
    onehot = (slot[:, None] == jnp.arange(MESH_GRP)[None, :]).astype(jnp.float32)
    valid = (slot < MESH_GRP).astype(jnp.float32)
    base = 9 * LAYERS
    w_in = vec_low[base + 4:base + 4 + F_IN]
    w_head = vec_low[base + 4 + F_IN:base + 4 + F_IN + F_OUT].T
    inputs = low(feat.T)
    embed_act = low(jax.nn.gelu(matmul(inputs, w_in) + vec_low[base]))
    hidden = matmul(embed_act, mats_low[5 * LAYERS]) + vec_low[base + 1]
    for layer_idx in range(LAYERS):
        hidden = layer_fwd(hidden, mats_low[5 * layer_idx:5 * layer_idx + 5], small_low[layer_idx], vec_low[9 * layer_idx:9 * layer_idx + 9], onehot, valid)
    head_in = low(layer_norm(hidden, vec_low[base + 2], vec_low[base + 3]))
    predict = matmul(head_in, w_head)
    truth = targ.T
    differ = predict - truth
    err_sum = jnp.dot(lax.optimization_barrier(jnp.sum(differ * differ, 1)), onehot, precision=HIGH)
    tgt_sum = jnp.dot(lax.optimization_barrier(jnp.sum(truth * truth, 1)), onehot, precision=HIGH)
    relative = jnp.sqrt(err_sum + EPS_LOSS) / jnp.sqrt(tgt_sum + EPS_LOSS)
    return jnp.sum(relative) / MESHES

def adamw(weight, moment, second, grad, factor):
    clipped = grad * factor
    moment = BETA_ONE * moment + (1.0 - BETA_ONE) * clipped
    second = BETA_TWO * second + (1.0 - BETA_TWO) * clipped * clipped
    moment_hat = moment / (1.0 - BETA_ONE ** STEP)
    second_hat = second / (1.0 - BETA_TWO ** STEP)
    updated = weight - LEARN * (moment_hat / (jnp.sqrt(second_hat) + EPS_ADAM) + DECAY * weight)
    return (moment, second, updated)

def reference(features, targets, mesh_slot, matrices, matrices_moment, matrices_second, smalls, smalls_moment, smalls_second, vectors, vectors_moment, vectors_second):
    groups = MESHES // MESH_GRP
    feat_all = features.reshape(F_IN, groups, GROUP_PTS).transpose(1, 0, 2)
    targ_all = targets.reshape(F_OUT, groups, GROUP_PTS).transpose(1, 0, 2)
    slot_all = mesh_slot.reshape(groups, GROUP_PTS)

    def one_group(carry, item):
        feat, targ, slot = item
        value, pullback = jax.vjp(lambda a, b, c: group_loss(a, b, c, feat, targ, slot), matrices, smalls, vectors)
        grads = pullback(jnp.ones_like(value))
        return ((carry[0] + value, tuple((c + g for c, g in zip(carry[1], grads)))), None)
    start = (jnp.zeros((), jnp.float32), (jnp.zeros_like(matrices), jnp.zeros_like(smalls), jnp.zeros_like(vectors)))
    (loss, grads), _ = lax.scan(one_group, start, (feat_all, targ_all, slot_all))
    squares = sum((jnp.sum(g * g) for g in grads))
    grad_norm = jnp.sqrt(squares)
    factor = jnp.minimum(1.0, CLIP / grad_norm)
    mat_out = adamw(matrices, matrices_moment, matrices_second, grads[0], factor)
    small_out = adamw(smalls, smalls_moment, smalls_second, grads[1], factor)
    vec_out = adamw(vectors, vectors_moment, vectors_second, grads[2], factor)
    return (loss, grad_norm, mat_out[0], mat_out[1], mat_out[2], small_out[0], small_out[1], small_out[2], vec_out[0], vec_out[1], vec_out[2])
```

```python
import jax
import jax.numpy as jnp
from jax import lax
from jax.sharding import PartitionSpec as P

D = 256
H = 8
DH = 32
S = 64
F_IN = 7
F_OUT = 4
LAYERS = 2
MESH_GRP = 4
STEP = 5


EPS_NORM = 1e-05
EPS_SLICE = 1e-05
EPS_LOSS = 1e-06
CLIP = 0.01
LEARN = 0.03
BETA_ONE = 0.9
BETA_TWO = 0.95
EPS_ADAM = 1e-08
DECAY = 0.1
BF = jnp.bfloat16
F32 = jnp.float32


ALL = ("mesh", "pts")


def swap(value, axis, mask):
    size = lax.axis_size(axis)
    return lax.ppermute(value, axis, [(i, i ^ mask) for i in range(size)])


def xor_order(pieces, index):
    step = 1
    while step < len(pieces):
        bit = (index & step) != 0
        pieces = [jnp.where(bit, pieces[j ^ step], pieces[j]) for j in range(len(pieces))]
        step *= 2
    return pieces


def bit_groups(size):
    bits = size.bit_length() - 1
    groups, low = [], 1
    while low < bits:
        width = min(2, bits - low)
        groups.append((low, width))
        low += width
    return groups


def gather_all(block):
    mesh_size, pts_size = lax.axis_size("mesh"), lax.axis_size("pts")
    me = lax.axis_index("mesh")
    tail = block.shape
    held = lax.all_to_all(jnp.broadcast_to(block[None], (pts_size,) + tail), "pts", 0, 0)
    held = held[None]
    for low, width in bit_groups(mesh_size):
        parts = [held] + [swap(held, "mesh", k << low) for k in range(1, 1 << width)]
        held = jnp.stack(xor_order(parts, (me >> low) & ((1 << width) - 1)))
        held = held.reshape((-1,) + held.shape[2:])
    other = swap(held, "mesh", 1)
    held = jnp.stack(xor_order([held, other], me & 1), 1)
    return held.reshape((mesh_size * pts_size,) + tail)


def scatter_sum(blocks):
    mesh_size, pts_size = lax.axis_size("mesh"), lax.axis_size("pts")
    me = lax.axis_index("mesh")
    tail = blocks.shape[1:]
    held = blocks.reshape((mesh_size // 2, 2, pts_size) + tail)
    odd = (me & 1) != 0
    keep = jnp.where(odd, held[:, 1], held[:, 0])
    send = jnp.where(odd, held[:, 0], held[:, 1])
    held = keep + swap(send, "mesh", 1)
    for low, width in reversed(bit_groups(mesh_size)):
        count = 1 << width
        held = held.reshape((count, -1, pts_size) + tail)
        pieces = xor_order([held[j] for j in range(count)], (me >> low) & (count - 1))
        total = pieces[0]
        for k in range(1, count):
            total = total + swap(pieces[k], "mesh", k << low)
        held = total
    held = held.reshape((pts_size,) + tail)
    return jnp.sum(lax.all_to_all(held, "pts", 0, 0), 0)


def pts_sum(value):
    size = lax.axis_size("pts")
    terms = [value.astype(F32)] + [swap(value, "pts", k).astype(F32) for k in range(1, size)]
    while len(terms) > 1:
        terms = [terms[i] + terms[i + 1] for i in range(0, len(terms), 2)]
    return terms[0]


def all_sum(values):
    count = lax.axis_size("mesh") * lax.axis_size("pts")
    wide = jnp.broadcast_to(values[None, :, None], (count,) + values.shape + (128,))
    return jnp.sum(lax.all_to_all(wide, ALL, 0, 0)[:, :, 0], 0)


def layer_norm(values, gains, shifts):
    row_mean = jnp.mean(values, -1, keepdims=True)
    centred = values - row_mean
    row_var = jnp.mean(centred * centred, -1, keepdims=True)
    return centred * lax.rsqrt(row_var + EPS_NORM) * gains + shifts


def matmul(left, right):
    return jnp.dot(left, right, preferred_element_type=F32)


def matmul_back(left, right, grad):
    grad_low = grad.astype(BF)
    return (matmul(grad_low, right.T), matmul(left.T, grad_low))


def einsum_low(form, first, second):
    return jnp.einsum(form, first, second, preferred_element_type=F32)


def per_mesh_sum(first, second, share):
    parts = einsum_low("mhsc,mhsd->mcd", first, second)
    return jnp.sum(parts * share[:, None, None], 0)


def layer_forward(hidden, weights, small, vec, onehot, valid):
    count = hidden.shape[0]
    normed = layer_norm(hidden, vec[0], vec[1]).astype(BF)
    x_low = (matmul(normed, weights[0]) + vec[2]).astype(BF).reshape(count, H, DH)
    f_low = (matmul(normed, weights[1]) + vec[3]).astype(BF).reshape(count, H, DH)
    logits = einsum_low("phc,cs->phs", x_low, small[:, :S])
    probs = jax.nn.softmax(logits, -1)
    w_low = (probs * valid[:, None, None]).astype(BF)
    routed = onehot[:, :, None, None] * w_low[:, None]
    numer = einsum_low("pmhs,phc->mhsc", routed, f_low)
    denom = einsum_low("pm,phs->mhs", onehot, w_low)
    both = pts_sum(jnp.concatenate([numer, denom[..., None]], -1).astype(BF))
    numer, denom = both[..., :DH], both[..., DH]
    tokens = (numer / (denom[..., None] + EPS_SLICE)).astype(BF)
    queries = einsum_low("mhsc,cd->mhsd", tokens, small[:, S : S + DH]).astype(BF)
    keys_low = einsum_low("mhsc,cd->mhsd", tokens, small[:, S + DH : S + 2 * DH]).astype(BF)
    values_low = einsum_low("mhsc,cd->mhsd", tokens, small[:, S + 2 * DH :]).astype(BF)
    scores = einsum_low("mhsd,mhtd->mhst", queries, keys_low) * DH ** (-0.5)
    attn = jax.nn.softmax(scores, -1)
    attn_low = attn.astype(BF)
    slice_out = einsum_low("mhst,mhtd->mhsd", attn_low, values_low).astype(BF)
    spread_low = einsum_low("pmhs,mhsc->phc", routed, slice_out).astype(BF).reshape(count, D)
    hidden_mid = hidden + matmul(spread_low, weights[2]) + vec[4]
    normed_two = layer_norm(hidden_mid, vec[5], vec[6]).astype(BF)
    pre_act = matmul(normed_two, weights[3]) + vec[7]
    activ = jax.nn.gelu(pre_act).astype(BF)
    hidden_out = hidden_mid + matmul(activ, weights[4]) + vec[8]
    saved = (
        hidden,
        normed,
        x_low,
        f_low,
        probs,
        routed,
        numer,
        denom,
        tokens,
        queries,
        keys_low,
        values_low,
        attn,
        attn_low,
        slice_out,
        spread_low,
        hidden_mid,
        normed_two,
        pre_act,
        activ,
    )
    return (hidden_out, saved)


def layer_backward(grad_out, saved, weights, small, vec, onehot_f, valid, share):
    (
        hidden,
        normed,
        x_low,
        f_low,
        probs,
        routed,
        numer,
        denom,
        tokens,
        queries,
        keys_low,
        values_low,
        attn,
        attn_low,
        slice_out,
        spread_low,
        hidden_mid,
        normed_two,
        pre_act,
        activ,
    ) = saved
    count = hidden.shape[0]
    d_activ, d_wfour = matmul_back(activ, weights[4], grad_out)
    d_pre = jax.vjp(jax.nn.gelu, pre_act)[1](d_activ)[0]
    d_normtwo, d_wthree = matmul_back(normed_two, weights[3], d_pre)
    d_mid, d_gfive, d_bsix = jax.vjp(layer_norm, hidden_mid, vec[5], vec[6])[1](d_normtwo)
    d_mid = d_mid + grad_out
    d_spread, d_wtwo = matmul_back(spread_low, weights[2], d_mid)
    d_spread_low = d_spread.reshape(count, H, DH).astype(BF)
    d_slice = einsum_low("pmhs,phc->mhsc", routed, d_spread_low)
    d_slice = pts_sum(d_slice.astype(BF)).astype(BF)
    d_route = einsum_low("phc,mhsc->pmhs", d_spread_low, slice_out)
    d_attn = einsum_low("mhsd,mhtd->mhst", d_slice, values_low)
    d_values = einsum_low("mhst,mhsd->mhtd", attn_low, d_slice).astype(BF)
    d_scores = (attn * (d_attn - jnp.sum(d_attn * attn, -1, keepdims=True))).astype(BF)
    d_queries = (einsum_low("mhst,mhtd->mhsd", d_scores, keys_low) * DH ** (-0.5)).astype(BF)
    d_keys = (einsum_low("mhst,mhsd->mhtd", d_scores, queries) * DH ** (-0.5)).astype(BF)
    d_tokens = (
        einsum_low("mhsd,cd->mhsc", d_queries, small[:, S : S + DH])
        + einsum_low("mhsd,cd->mhsc", d_keys, small[:, S + DH : S + 2 * DH])
        + einsum_low("mhsd,cd->mhsc", d_values, small[:, S + 2 * DH :])
    )
    d_wq = per_mesh_sum(tokens, d_queries, share)
    d_wk = per_mesh_sum(tokens, d_keys, share)
    d_wv = per_mesh_sum(tokens, d_values, share)
    inverse = 1.0 / (denom + EPS_SLICE)
    d_numer_low = (d_tokens * inverse[..., None]).astype(BF)
    d_denom = -jnp.sum(d_tokens * numer, -1) * inverse * inverse
    d_route = d_route + einsum_low("mhsc,phc->pmhs", d_numer_low, f_low) + d_denom[None]
    d_probs = jnp.sum(d_route * onehot_f[:, :, None, None], 1) * valid[:, None, None]
    d_fmid = einsum_low("pmhs,mhsc->phc", routed, d_numer_low).reshape(count, D)
    d_logits = (probs * (d_probs - jnp.sum(d_probs * probs, -1, keepdims=True))).astype(BF)
    d_xmid = einsum_low("phs,cs->phc", d_logits, small[:, :S]).reshape(count, D)
    d_wslice = einsum_low("phc,phs->cs", x_low, d_logits)
    d_norm_a, d_wzero = matmul_back(normed, weights[0], d_xmid)
    d_norm_b, d_wone = matmul_back(normed, weights[1], d_fmid)
    d_hidden, d_gzero, d_bone = jax.vjp(layer_norm, hidden, vec[0], vec[1])[1](d_norm_a + d_norm_b)
    d_hidden = d_hidden + d_mid
    d_weights = jnp.stack([d_wzero, d_wone, d_wtwo, d_wthree, d_wfour])
    d_small = jnp.concatenate([d_wslice, d_wq, d_wk, d_wv], 1).reshape(-1)
    d_vec = jnp.stack(
        [
            d_gzero,
            d_bone,
            jnp.sum(d_xmid, 0),
            jnp.sum(d_fmid, 0),
            jnp.sum(d_mid, 0),
            d_gfive,
            d_bsix,
            jnp.sum(d_pre, 0),
            jnp.sum(grad_out, 0),
        ]
    )
    return (d_hidden, d_weights, d_small, d_vec)


def adamw(weight, moment, second, grad, factor):
    clipped = grad * factor
    moment = BETA_ONE * moment + (1.0 - BETA_ONE) * clipped
    second = BETA_TWO * second + (1.0 - BETA_TWO) * clipped * clipped
    moment_hat = moment / (1.0 - BETA_ONE**STEP)
    second_hat = second / (1.0 - BETA_TWO**STEP)
    updated = weight - LEARN * (moment_hat / (jnp.sqrt(second_hat) + EPS_ADAM) + DECAY * weight)
    return (moment, second, updated)


def per_device(
    features,
    targets,
    mesh_slot,
    matrices,
    matrices_moment,
    matrices_second,
    smalls,
    smalls_moment,
    smalls_second,
    vectors,
    vectors_moment,
    vectors_second,
):
    devices = lax.axis_size("mesh") * lax.axis_size("pts")
    cols, width = matrices.shape[2], smalls.shape[1]
    count_mats, count_vecs = matrices.shape[0], vectors.shape[0]
    mat_rows = count_mats * cols
    pad_rows = -(mat_rows + cols + LAYERS) % 8
    block = jnp.concatenate(
        [
            matrices.astype(BF).transpose(0, 2, 1).reshape(mat_rows, D),
            jnp.pad(vectors.astype(BF).T, ((0, 0), (0, D - count_vecs))),
            jnp.pad(smalls.astype(BF), ((0, pad_rows), (0, D - width))),
        ]
    )
    whole = gather_all(block)
    all_mats = (
        whole[:, :mat_rows]
        .reshape(devices, count_mats, cols, D)
        .transpose(1, 3, 0, 2)
        .reshape(count_mats, D, D)
    )
    all_vecs = whole[:, mat_rows : mat_rows + cols, :count_vecs].reshape(D, count_vecs).T
    first = mat_rows + cols
    all_small = whole[:, first : first + LAYERS, :width].transpose(1, 0, 2)
    all_small = all_small.reshape(LAYERS, DH, S + 3 * DH)
    vec_full = all_vecs.astype(F32)
    onehot_f = (mesh_slot[:, None] == jnp.arange(MESH_GRP)[None, :]).astype(F32)
    onehot_b = onehot_f.astype(BF)
    valid = (mesh_slot < MESH_GRP).astype(F32)
    point_devs = lax.axis_size("pts")
    share = jnp.full((MESH_GRP,), 1.0 / point_devs, F32)
    base = 9 * LAYERS
    w_in = all_vecs[base + 4 : base + 4 + F_IN]
    w_head = all_vecs[base + 4 + F_IN : base + 4 + F_IN + F_OUT].T
    inputs = features.T.astype(BF)
    embed_pre = matmul(inputs, w_in) + vec_full[base]
    embed_act = jax.nn.gelu(embed_pre).astype(BF)
    hidden = matmul(embed_act, all_mats[5 * LAYERS]) + vec_full[base + 1]
    saves = []
    for layer_idx in range(LAYERS):
        hidden, saved = layer_forward(
            hidden,
            all_mats[5 * layer_idx : 5 * layer_idx + 5],
            all_small[layer_idx],
            vec_full[9 * layer_idx : 9 * layer_idx + 9],
            onehot_b,
            valid,
        )
        saves.append(saved)
    head_low = layer_norm(hidden, vec_full[base + 2], vec_full[base + 3]).astype(BF)
    predict = matmul(head_low, w_head)
    truth = targets.T
    differ = predict - truth
    err_part = jnp.sum(onehot_f * jnp.sum(differ * differ, 1)[:, None], 0)
    tgt_part = jnp.sum(onehot_f * jnp.sum(truth * truth, 1)[:, None], 0)
    sums = pts_sum(jnp.broadcast_to(jnp.concatenate([err_part, tgt_part])[:, None], (8, 128)))
    err_sum, tgt_sum = sums[:4, 0], sums[4:, 0]
    err_root = jnp.sqrt(err_sum + EPS_LOSS)
    tgt_root = jnp.sqrt(tgt_sum + EPS_LOSS)
    meshes_all = MESH_GRP * lax.axis_size("mesh")
    group_loss = jnp.sum(err_root / tgt_root) / meshes_all
    row_weight = jnp.sum(onehot_f * (1.0 / (err_root * tgt_root))[None, :], 1) / meshes_all
    d_predict = differ * row_weight[:, None]
    d_head, d_whead = matmul_back(head_low, w_head, d_predict)
    d_hidden, d_hgain, d_hbias = jax.vjp(
        layer_norm, hidden, vec_full[base + 2], vec_full[base + 3]
    )[1](d_head)
    grads_mats = [None] * LAYERS
    grads_small = [None] * LAYERS
    grads_vec = [None] * LAYERS
    for layer_idx in reversed(range(LAYERS)):
        d_hidden, grads_mats[layer_idx], grads_small[layer_idx], grads_vec[layer_idx] = (
            layer_backward(
                d_hidden,
                saves[layer_idx],
                all_mats[5 * layer_idx : 5 * layer_idx + 5],
                all_small[layer_idx],
                vec_full[9 * layer_idx : 9 * layer_idx + 9],
                onehot_f,
                valid,
                share,
            )
        )
    d_act, d_wembed = matmul_back(embed_act, all_mats[5 * LAYERS], d_hidden)
    d_embed = jax.vjp(jax.nn.gelu, embed_pre)[1](d_act)[0]
    d_win = matmul(inputs.T, d_embed.astype(BF))
    d_mats = jnp.concatenate(grads_mats + [d_wembed[None]], 0)
    d_smalls = jnp.stack(grads_small)
    d_vecs = jnp.concatenate(
        grads_vec
        + [
            jnp.stack([jnp.sum(d_embed, 0), jnp.sum(d_hidden, 0), d_hgain, d_hbias]),
            d_win,
            d_whead.T,
        ],
        0,
    )
    grads = jnp.concatenate(
        [
            d_mats.reshape(count_mats, D, devices, cols)
            .transpose(2, 0, 3, 1)
            .reshape(devices, mat_rows, D),
            jnp.pad(d_vecs.T.reshape(devices, cols, count_vecs), ((0, 0), (0, 0), (0, D - count_vecs))),
            jnp.pad(
                d_smalls.reshape(LAYERS, devices, width).transpose(1, 0, 2),
                ((0, 0), (0, pad_rows), (0, D - width)),
            ),
        ],
        1,
    )
    own = scatter_sum(grads)
    red_mats = own[:mat_rows].reshape(count_mats, cols, D).transpose(0, 2, 1)
    red_vecs = own[mat_rows:first, :count_vecs].T
    red_small = own[first : first + LAYERS, :width]
    squares = (
        jnp.sum(red_mats * red_mats) + jnp.sum(red_small * red_small) + jnp.sum(red_vecs * red_vecs)
    )
    totals = all_sum(jnp.stack([squares, group_loss / point_devs]))
    loss_total = totals[1]
    grad_norm = jnp.sqrt(totals[0])
    factor = jnp.minimum(1.0, CLIP / grad_norm)
    mat_out = adamw(matrices, matrices_moment, matrices_second, red_mats, factor)
    small_out = adamw(smalls, smalls_moment, smalls_second, red_small, factor)
    vec_out = adamw(vectors, vectors_moment, vectors_second, red_vecs, factor)
    return (
        loss_total,
        grad_norm,
        mat_out[0],
        mat_out[1],
        mat_out[2],
        small_out[0],
        small_out[1],
        small_out[2],
        vec_out[0],
        vec_out[1],
        vec_out[2],
    )


def solution(mesh):
    return jax.shard_map(
        per_device,
        mesh=mesh,
        in_specs=(
            P(None, ("mesh", "pts")),
            P(None, ("mesh", "pts")),
            P(("mesh", "pts")),
            P(None, None, ("mesh", "pts")),
            P(None, None, ("mesh", "pts")),
            P(None, None, ("mesh", "pts")),
            P(None, ("mesh", "pts")),
            P(None, ("mesh", "pts")),
            P(None, ("mesh", "pts")),
            P(None, ("mesh", "pts")),
            P(None, ("mesh", "pts")),
            P(None, ("mesh", "pts")),
        ),
        out_specs=(
            P(),
            P(),
            P(None, None, ("mesh", "pts")),
            P(None, None, ("mesh", "pts")),
            P(None, None, ("mesh", "pts")),
            P(None, ("mesh", "pts")),
            P(None, ("mesh", "pts")),
            P(None, ("mesh", "pts")),
            P(None, ("mesh", "pts")),
            P(None, ("mesh", "pts")),
            P(None, ("mesh", "pts")),
        ),
        check_vma=False,
    )
```

```python
import functools
import jax
import jax.numpy as jnp
from jax import lax
from jax.experimental import pallas as pl
from jax.experimental.pallas import tpu as pltpu
from jax.sharding import PartitionSpec as P

D = 256
H = 8
DH = 32
S = 64
HS = H * S
F_IN = 7
F_OUT = 4
LAYERS = 2
MESH_GRP = 4
STEP = 5
CHUNK = 512
ND_ROWS = 40


EPS_NORM = 1e-05
EPS_SLICE = 1e-05
EPS_LOSS = 1e-06
CLIP = 0.01
LEARN = 0.03
BETA_ONE = 0.9
BETA_TWO = 0.95
EPS_ADAM = 1e-08
DECAY = 0.1
BF = jnp.bfloat16
F32 = jnp.float32
I32 = jnp.int32
ALL = ("mesh", "pts")
BASE = 9 * LAYERS


def dot(left, right):
    return jnp.dot(left, right, preferred_element_type=F32)


def dot_nt(left, right):
    return lax.dot_general(left, right, (((1,), (1,)), ((), ())), preferred_element_type=F32)


def dot_tn(left, right):
    return lax.dot_general(left, right, (((0,), (0,)), ((), ())), preferred_element_type=F32)


def low(value):
    return value.astype(BF)


def block_mask():
    rows = lax.broadcasted_iota(I32, (D, HS), 0) // DH
    cols = lax.broadcasted_iota(I32, (D, HS), 1) // S
    return rows == cols


def spread_blocks(compact):
    tall = jnp.concatenate([compact] * H, 0)
    return jnp.where(block_mask(), tall, jnp.zeros_like(tall))


def fold_blocks(full):
    lanes = lax.broadcasted_iota(I32, (DH, HS), 1) // S
    total = jnp.zeros((DH, HS), F32)
    for head in range(H):
        total = jnp.where(lanes == head, full[head * DH : (head + 1) * DH], total)
    return total


def pick_matrix():
    rows = lax.broadcasted_iota(I32, (S, HS), 0)
    cols = lax.broadcasted_iota(I32, (S, HS), 1) % S
    return (rows == cols).astype(F32).astype(BF)


def norm_stats(hidden):
    row_mean = jnp.sum(hidden, 0, keepdims=True) * (1.0 / D)
    centred = hidden - row_mean
    row_var = jnp.sum(centred * centred, 0, keepdims=True) * (1.0 / D)
    return centred, lax.rsqrt(row_var + EPS_NORM)


def norm_apply(hidden, gain, shift):
    centred, scale = norm_stats(hidden)
    return low(centred * scale * gain + shift)


def norm_back(grad, unit, scale, gain):
    inner = grad * gain
    first = jnp.sum(inner, 0, keepdims=True) * (1.0 / D)
    second = jnp.sum(inner * unit, 0, keepdims=True) * (1.0 / D)
    return scale * (inner - first - unit * second)


ROOT = 0.7978845608028654
CUBIC = 0.044715


def gelu(value):
    return 0.5 * value * (1.0 + jnp.tanh(ROOT * (value + CUBIC * (value * value * value))))


def gelu_both(value):
    square = value * value
    bend = jnp.tanh(ROOT * (value + CUBIC * (square * value)))
    half = 0.5 * (1.0 + bend)
    slope = half + 0.5 * value * (1.0 - bend * bend) * (ROOT * (1.0 + 3.0 * CUBIC * square))
    return value * half, slope


def lane_fold(value):
    total = value[:, :128]
    for start in range(128, value.shape[1], 128):
        total = total + value[:, start : start + 128]
    return total


def columns(sums):
    lanes = lax.broadcasted_iota(I32, (D, 128), 1)
    total = jnp.zeros((D, 128), F32)
    for index, value in sums:
        total = jnp.where(lanes == index, jnp.sum(value, 1, keepdims=True), total)
    return total


def slice_matrix(small):
    wide = jnp.concatenate([small[:, :S], small[:, :S]], 1)
    return spread_blocks(jnp.concatenate([wide] * (HS // (2 * S)), 1))


def slice_forward(num_den, small):
    tokens = low(num_den[:DH] / (num_den[DH : DH + 1] + EPS_SLICE))
    mixed = low(dot_tn(small[:, S:], tokens))
    pick = pick_matrix()
    keys = low(dot_nt(pick, spread_blocks(mixed[DH : 2 * DH])))
    values = low(dot_nt(spread_blocks(mixed[2 * DH :]), pick))
    scores = dot(keys, spread_blocks(mixed[:DH])) * DH ** (-0.5)
    scores = scores - jnp.max(scores, 0, keepdims=True)
    raised = jnp.exp(scores)
    attn = raised / jnp.sum(raised, 0, keepdims=True)
    full = dot(values, low(attn))
    routed = low(jnp.where(block_mask(), full, jnp.zeros_like(full)))
    return routed, attn, tokens, mixed


def widen(tall):
    pair = jnp.concatenate([tall, tall], 1)
    return fold_blocks(jnp.concatenate([pair] * (HS // (2 * S)), 1))


def slice_backward(d_slice, num_den, attn, tokens, mixed, small):
    attn_low = low(attn)
    pick = pick_matrix()
    d_full = spread_blocks(d_slice)
    query_full = spread_blocks(mixed[:DH])
    values = low(dot_nt(pick, spread_blocks(mixed[2 * DH :])))
    keys = low(dot_nt(spread_blocks(mixed[DH : 2 * DH]), pick))
    d_attn = dot(values, d_full)
    d_values = low(widen(dot_nt(d_full, attn_low)))
    d_scores = low(attn * (d_attn - jnp.sum(d_attn * attn, 0, keepdims=True)))
    scale = DH ** (-0.5)
    d_queries = low(fold_blocks(dot(keys, d_scores)) * scale)
    d_keys = low(widen(dot_nt(query_full, d_scores)) * scale)
    d_mixed = jnp.concatenate([d_queries, d_keys, d_values], 0)
    d_tokens = dot(small[:, S:], d_mixed)
    d_weight = dot_nt(tokens, d_mixed)
    inverse = 1.0 / (num_den[DH : DH + 1] + EPS_SLICE)
    d_num = low(d_tokens * inverse)
    d_den = -jnp.sum(d_tokens * num_den[:DH], 0, keepdims=True) * inverse * inverse
    return spread_blocks(d_num), d_den, d_weight


def first_step():
    return pl.program_id(0) == 0


def last_step():
    return pl.program_id(0) == pl.num_programs(0) - 1


def is_mesh(slot, mesh_id):
    return (slot == mesh_id).astype(F32)


def front(hidden, vec, layer, wx, wf, slices, slot, here, x_ref, f_ref, probs_ref, w_ref, sums):
    at = 9 * layer
    u = norm_apply(hidden, vec[:, at : at + 1], vec[:, at + 1 : at + 2])
    x_low = low(dot(wx, u) + vec[:, at + 2 : at + 3])
    f_low = low(dot(wf, u) + vec[:, at + 3 : at + 4])
    x_ref[...] = x_low
    f_ref[...] = f_low
    width = hidden.shape[1]
    logits = dot(slices, x_low).reshape(H, S, width)
    raised = jnp.exp(logits - jnp.max(logits, 1, keepdims=True))
    probs = raised * (1.0 / jnp.sum(raised, 1, keepdims=True))
    valid = (slot < MESH_GRP).astype(F32)
    probs_ref[...] = probs.reshape(HS, width)
    w_low = low(probs * valid[None]).reshape(HS, width)
    w_ref[...] = w_low
    for mesh_id in range(MESH_GRP):

        @pl.when(here[pl.program_id(0), mesh_id] != 0)
        def _():
            mine = is_mesh(slot, mesh_id)
            rows = jnp.concatenate(
                [low(f_low.astype(F32) * mine), low(jnp.broadcast_to(mine, (16, width)))], 0
            )
            sums[mesh_id] = sums[mesh_id] + dot_nt(rows, w_low)


def front_finish(sums, big, nd_ref, send_ref):
    for mesh_id in range(MESH_GRP):
        full = sums[mesh_id]
        both = jnp.concatenate([fold_blocks(full[:D]), full[D : D + ND_ROWS - DH]], 0)
        nd_ref[mesh_id] = both
    send_ref[...] = low(nd_ref[big])


def back_half(w_low, slot, here, routed, mix, hidden, vec, layer, wo, w1, w2):
    mix[...] = jnp.zeros_like(mix)
    for mesh_id in range(MESH_GRP):

        @pl.when(here[pl.program_id(0), mesh_id] != 0)
        def _():
            mix[...] = mix[...] + dot(routed[mesh_id], w_low) * is_mesh(slot, mesh_id)

    at = 9 * layer
    y_low = low(mix[...])
    middle = hidden + dot(wo, y_low) + vec[:, at + 4 : at + 5]
    u2 = norm_apply(middle, vec[:, at + 5 : at + 6], vec[:, at + 6 : at + 7])
    pre = dot(w1, u2) + vec[:, at + 7 : at + 8]
    out = middle + dot(w2, low(gelu(pre))) + vec[:, at + 8 : at + 9]
    return y_low, middle, pre, out


def head_half(grad, vec, layer, pre, middle, y_low, w_low, slot, here, w1, w2, wo, sums, cols, keep):
    at = 9 * layer
    grad_low = low(grad)
    activ, slope = gelu_both(pre)
    d_pre = dot(w2, grad_low) * slope
    d_pre_low = low(d_pre)
    d_norm = dot(w1, d_pre_low)
    centred, scale = norm_stats(middle)
    unit = centred * scale
    gain = vec[:, at + 5 : at + 6]
    d_mid = norm_back(d_norm, unit, scale, gain) + grad
    d_mid_low = low(d_mid)
    d_y = low(dot(wo, d_mid_low))
    cols[0] = cols[0] + lane_fold(d_mid)
    cols[1] = cols[1] + lane_fold(d_norm * unit)
    cols[2] = cols[2] + lane_fold(d_norm)
    cols[3] = cols[3] + lane_fold(d_pre)
    cols[4] = cols[4] + lane_fold(grad)
    keep[0][...] = grad_low
    keep[1][...] = low(activ)
    keep[2][...] = d_pre_low
    keep[3][...] = low(unit * gain + vec[:, at + 6 : at + 7])
    keep[4][...] = d_mid_low
    keep[5][...] = d_y
    keep[6][...] = d_mid
    for mesh_id in range(MESH_GRP):

        @pl.when(here[pl.program_id(0), mesh_id] != 0)
        def _():
            mine = is_mesh(slot, mesh_id)
            sums[mesh_id] = sums[mesh_id] + dot_nt(low(d_y.astype(F32) * mine), w_low)


def head_finish(sums, big, ds_ref, send_ref):
    for mesh_id in range(MESH_GRP):
        ds_ref[mesh_id] = low(fold_blocks(sums[mesh_id]))
    send_ref[...] = ds_ref[big]


def tail_half(vec, layer, hidden, x_low, f_low, probs, w_low, d_y, d_mid, slot, here,
              both, d_num, d_den, slices, wx, wf, route, mix, slope_sum, cols, d_wx, d_wf):
    width = hidden.shape[1]
    at = 9 * layer
    route[...] = jnp.zeros_like(route)
    mix[...] = jnp.zeros_like(mix)
    for mesh_id in range(MESH_GRP):

        @pl.when(here[pl.program_id(0), mesh_id] != 0)
        def _():
            mine = is_mesh(slot, mesh_id)
            pair = jnp.concatenate([d_y, f_low], 0)
            through = dot(both[mesh_id], pair) + d_den[mesh_id][:, :1]
            route[...] = route[...] + through * mine
            mix[...] = mix[...] + dot(d_num[mesh_id], w_low) * mine

    d_probs = route[...].reshape(H, S, width)
    probs = probs.reshape(H, S, width)
    spread = jnp.sum(d_probs * probs, 1, keepdims=True)
    d_logits = low(probs * (d_probs - spread)).reshape(HS, width)
    d_x = dot(slices, d_logits)
    d_f = mix[...]
    slope_sum[...] = slope_sum[...] + dot_nt(x_low, d_logits)
    d_x_low, d_f_low = low(d_x), low(d_f)
    d_norm = dot(wx, d_x_low) + dot(wf, d_f_low)
    centred, scale = norm_stats(hidden)
    unit = centred * scale
    gain = vec[:, at : at + 1]
    u = low(unit * gain + vec[:, at + 1 : at + 2])
    d_wx[...] = d_wx[...] + dot_nt(d_x_low, u)
    d_wf[...] = d_wf[...] + dot_nt(d_f_low, u)
    cols[0] = cols[0] + lane_fold(d_norm * unit)
    cols[1] = cols[1] + lane_fold(d_norm)
    cols[2] = cols[2] + lane_fold(d_x)
    cols[3] = cols[3] + lane_fold(d_f)
    return norm_back(d_norm, unit, scale, gain) + d_mid


def zero(*refs):
    for ref in refs:
        ref[...] = jnp.zeros_like(ref)


def embed_kernel(here, big, feat, slot, vec, we1, we2, wx, wf, small,
                 h_ref, x_ref, f_ref, probs_ref, w_ref, nd_ref, send_ref, sums, slices):
    @pl.when(first_step())
    def _():
        zero(sums)
        slices[...] = slice_matrix(small[...]).T

    e1 = dot(we1[...], low(feat[...])) + vec[:, BASE : BASE + 1]
    hidden = dot(we2[...], low(gelu(e1))) + vec[:, BASE + 1 : BASE + 2]
    h_ref[...] = hidden
    front(hidden, vec, 0, wx[...], wf[...], slices[...], slot[...], here,
          x_ref, f_ref, probs_ref, w_ref, sums)

    @pl.when(last_step())
    def _():
        front_finish(sums, big[0], nd_ref, send_ref)


def small_kernel(there, big, nd_ref, small, routed_ref, attn_ref, tokens_ref, mixed_ref):
    for mesh_id in range(MESH_GRP):

        @pl.when((there[mesh_id] != 0) & (big[0] != mesh_id))
        def _():
            routed, attn, tokens, mixed = slice_forward(nd_ref[mesh_id], small[...])
            routed_ref[mesh_id] = routed
            attn_ref[mesh_id] = attn
            tokens_ref[mesh_id] = tokens
            mixed_ref[mesh_id] = mixed


def sum_parts(parts):
    terms = [part[...].astype(F32) for part in parts]
    while len(terms) > 1:
        terms = [terms[i] + terms[i + 1] for i in range(0, len(terms), 2)]
    return terms[0]


def middle_start(parts, small, big, routed_in, routed, routed_ref, nd_ref, attn_ref, tokens_ref, mixed_ref):
    routed[...] = routed_in[...]
    total = sum_parts(parts)
    mine, attn, tokens, mixed = slice_forward(total, small[...])
    routed[big] = mine
    routed_ref[...] = mine
    nd_ref[...] = total
    attn_ref[...] = attn
    tokens_ref[...] = tokens
    mixed_ref[...] = mixed


def middle_kernel(npts, here, big, *refs):
    parts, refs = refs[:npts], refs[npts:]
    (routed_in, w_in, h_in, slot, vec, wo, w1, w2, wx, wf, small, small_next,
     routed_ref, ndb_ref, attn_ref, tokens_ref, mixed_ref,
     y_ref, m_ref, p_ref, h_ref, x_ref, f_ref, probs_ref, w_ref, nd_ref, send_ref,
     routed, mix, sums, slices) = refs

    @pl.when(first_step())
    def _():
        zero(sums)
        slices[...] = slice_matrix(small_next[...]).T
        middle_start(parts, small, big[0], routed_in, routed,
                     routed_ref, ndb_ref, attn_ref, tokens_ref, mixed_ref)

    y_low, middle, pre, out = back_half(w_in[...], slot[...], here, routed, mix, h_in[...], vec, 0,
                                        wo[...], w1[...], w2[...])
    y_ref[...] = y_low
    m_ref[...] = middle
    p_ref[...] = pre
    h_ref[...] = out
    front(out, vec, 1, wx[...], wf[...], slices[...], slot[...], here,
          x_ref, f_ref, probs_ref, w_ref, sums)

    @pl.when(last_step())
    def _():
        front_finish(sums, big[0], nd_ref, send_ref)


def head_kernel(npts, here, big, *refs):
    parts, refs = refs[:npts], refs[npts:]
    (routed_in, w_in, h_in, slot, target, vec, wo, w1, w2, whd, small,
     routed_ref, ndb_ref, attn_ref, tokens_ref, mixed_ref,
     y_ref, m_ref, p_ref, h_ref, diff_ref, loss_ref,
     routed, mix, acc) = refs

    @pl.when(first_step())
    def _():
        zero(acc)
        middle_start(parts, small, big[0], routed_in, routed,
                     routed_ref, ndb_ref, attn_ref, tokens_ref, mixed_ref)

    y_low, middle, pre, out = back_half(w_in[...], slot[...], here, routed, mix, h_in[...], vec, 1,
                                        wo[...], w1[...], w2[...])
    y_ref[...] = y_low
    m_ref[...] = middle
    p_ref[...] = pre
    h_ref[...] = out
    uh = norm_apply(out, vec[:, BASE + 2 : BASE + 3], vec[:, BASE + 3 : BASE + 4])
    truth = target[...]
    differ = dot_tn(whd[...], uh) - truth
    diff_ref[...] = differ
    width = truth.shape[1]
    ids = lax.broadcasted_iota(I32, (MESH_GRP, width), 0)
    member = (ids == slot[...]).astype(F32)
    squares = jnp.sum(differ * differ, 0, keepdims=True)
    sizes = jnp.sum(truth * truth, 0, keepdims=True)
    acc[...] = acc[...] + lane_fold(jnp.concatenate([member * squares, member * sizes], 0))

    @pl.when(last_step())
    def _():
        loss_ref[...] = jnp.broadcast_to(jnp.sum(acc[...], 1, keepdims=True), loss_ref.shape)


def loss_kernel(npts, groups, here, big, *refs):
    parts, refs = refs[:npts], refs[npts:]
    (diff, slot, h_in, pre, middle, y_in, w_in, vec, whd, w1t, w2t, wot,
     rel_ref, whd_ref, col_ref, ds_ref, send_ref, k0, k1, k2, k3, k4, k5, k6,
     coef, cols, sums, w1, w2, wo) = refs

    @pl.when(first_step())
    def _():
        zero(cols, sums, whd_ref)
        w1[...] = w1t[...].T
        w2[...] = w2t[...].T
        wo[...] = wot[...].T
        total = sum_parts(parts)
        err_root = jnp.sqrt(total[:MESH_GRP] + EPS_LOSS)
        tgt_root = jnp.sqrt(total[MESH_GRP:] + EPS_LOSS)
        rel_ref[...] = jnp.concatenate([err_root / tgt_root, jnp.zeros_like(err_root)], 0)
        scale = 1.0 / (err_root * tgt_root) * (1.0 / (MESH_GRP * groups))
        coef[...] = jnp.concatenate([scale, jnp.zeros_like(scale)], 0)

    width = slot.shape[1]
    ids = lax.broadcasted_iota(I32, (MESH_GRP, width), 0)
    member = (ids == slot[...]).astype(F32)
    row = jnp.sum(member * coef[:MESH_GRP, :1], 0, keepdims=True)
    d_pred = low(diff[...] * row)
    d_head = dot(whd[...], d_pred)
    centred, scale = norm_stats(h_in[...])
    unit = centred * scale
    gain = vec[:, BASE + 2 : BASE + 3]
    uh = low(unit * gain + vec[:, BASE + 3 : BASE + 4])
    whd_ref[...] = whd_ref[...] + dot_nt(uh, d_pred)
    cols[5] = cols[5] + lane_fold(d_head * unit)
    cols[6] = cols[6] + lane_fold(d_head)
    grad = norm_back(d_head, unit, scale, gain)
    head_half(grad, vec, 1, pre[...], middle[...], y_in[...], w_in[...], slot[...], here,
              w1[...], w2[...], wo[...], sums, cols, (k0, k1, k2, k3, k4, k5, k6))

    @pl.when(last_step())
    def _():
        head_finish(sums, big[0], ds_ref, send_ref)
        at = 9
        col_ref[...] = columns([(at + 4 + j, cols[j]) for j in range(5)]
                               + [(BASE + 2, cols[5]), (BASE + 3, cols[6])])


def weights_kernel(g_low, activ, d_pre, u2, d_mid, y_low, w2_ref, w1_ref, wo_ref):
    @pl.when(first_step())
    def _():
        zero(w2_ref, w1_ref, wo_ref)

    w2_ref[...] = w2_ref[...] + dot_nt(g_low[...], activ[...])
    w1_ref[...] = w1_ref[...] + dot_nt(d_pre[...], u2[...])
    wo_ref[...] = wo_ref[...] + dot_nt(d_mid[...], y_low[...])


def small_back_kernel(there, big, ds_in, nd_ref, attn, tokens, mixed, routed, small,
                      both_ref, dn_ref, den_ref, dw_ref):
    zero(dw_ref)
    for mesh_id in range(MESH_GRP):

        @pl.when((there[mesh_id] != 0) & (big[0] != mesh_id))
        def _():
            dn, den, dw = slice_backward(ds_in[mesh_id], nd_ref[mesh_id], attn[mesh_id],
                                         tokens[mesh_id], mixed[mesh_id], small[...])
            place_back(both_ref, dn_ref, den_ref, mesh_id, routed[mesh_id], dn, den)
            dw_ref[...] = dw_ref[...] + dw


def place_back(both_ref, dn_ref, den_ref, at, routed, dn, den):
    both_ref[at] = jnp.concatenate([routed, dn], 0).T
    dn_ref[at] = dn
    den_ref[at] = jnp.broadcast_to(den, (128, HS)).T


def tail_start(npts, parts, small, big, ndb, attn, tokens, mixed, routed_big, both_in, dn_in, den_in, dw_in,
               both, dn, den, dw_ref):
    both[...] = both_in[...]
    dn[...] = dn_in[...]
    den[...] = den_in[...]
    total = low(sum_parts(parts))
    d_num, d_den, d_weight = slice_backward(total, ndb[...], attn[...], tokens[...], mixed[...], small[...])
    place_back(both, dn, den, big, routed_big[...], d_num, d_den)
    dw_ref[...] = dw_in[...] + d_weight * (1.0 / npts)


TAIL_INS = 25


def turn_kernel(npts, here, big, *refs):
    parts, refs = refs[:npts], refs[npts:]
    (both_in, dn_in, den_in, dw_in, ndb, attn, tokens, mixed, routed_big, small,
     h_in, x_in, f_in, probs, w_in, d_y, d_mid, slot, vec, wxt, wft,
     pre, middle, y_in, w_prev, w1t, w2t, wot,
     dw_ref, slope_ref, wx_ref, wf_ref, col_ref, ds_ref, send_ref, k0, k1, k2, k3, k4, k5, k6,
     both, dn, den, slices, route, mix, slope_sum, cols, cols_next, sums, wx, wf, w1, w2, wo) = refs

    @pl.when(first_step())
    def _():
        zero(slope_sum, cols, cols_next, sums, wx_ref, wf_ref)
        slices[...] = slice_matrix(small[...])
        wx[...] = wxt[...].T
        wf[...] = wft[...].T
        w1[...] = w1t[...].T
        w2[...] = w2t[...].T
        wo[...] = wot[...].T
        tail_start(npts, parts, small, big[0], ndb, attn, tokens, mixed, routed_big,
                   both_in, dn_in, den_in, dw_in, both, dn, den, dw_ref)

    grad = tail_half(vec, 1, h_in[...], x_in[...], f_in[...], probs[...], w_in[...], d_y[...], d_mid[...],
                     slot[...], here, both, dn, den, slices[...], wx[...], wf[...], route, mix,
                     slope_sum, cols, wx_ref, wf_ref)
    head_half(grad, vec, 0, pre[...], middle[...], y_in[...], w_prev[...], slot[...], here,
              w1[...], w2[...], wo[...], sums, cols_next, (k0, k1, k2, k3, k4, k5, k6))

    @pl.when(last_step())
    def _():
        head_finish(sums, big[0], ds_ref, send_ref)
        slope_ref[...] = fold_blocks(slope_sum[...])
        col_ref[...] = columns([(9 + j, cols[j]) for j in range(4)]
                               + [(4 + j, cols_next[j]) for j in range(5)])


def end_kernel(npts, here, big, *refs):
    parts, refs = refs[:npts], refs[npts:]
    (both_in, dn_in, den_in, dw_in, ndb, attn, tokens, mixed, routed_big, small,
     h_in, x_in, f_in, probs, w_in, d_y, d_mid, slot, vec, wxt, wft,
     feat, we1, we2t,
     dw_ref, slope_ref, wx_ref, wf_ref, col_ref, we2_ref, we1_ref,
     both, dn, den, slices, route, mix, slope_sum, cols, cols_next, wx, wf, we2) = refs

    @pl.when(first_step())
    def _():
        zero(slope_sum, cols, cols_next, wx_ref, wf_ref, we2_ref, we1_ref)
        slices[...] = slice_matrix(small[...])
        wx[...] = wxt[...].T
        wf[...] = wft[...].T
        we2[...] = we2t[...].T
        tail_start(npts, parts, small, big[0], ndb, attn, tokens, mixed, routed_big,
                   both_in, dn_in, den_in, dw_in, both, dn, den, dw_ref)

    grad = tail_half(vec, 0, h_in[...], x_in[...], f_in[...], probs[...], w_in[...], d_y[...], d_mid[...],
                     slot[...], here, both, dn, den, slices[...], wx[...], wf[...], route, mix,
                     slope_sum, cols, wx_ref, wf_ref)
    feat_low = low(feat[...])
    activ, slope = gelu_both(dot(we1[...], feat_low) + vec[:, BASE : BASE + 1])
    grad_low = low(grad)
    d_embed = dot(we2[...], grad_low) * slope
    we2_ref[...] = we2_ref[...] + dot_nt(grad_low, low(activ))
    we1_ref[...] = we1_ref[...] + dot_nt(low(d_embed), feat_low)
    cols_next[0] = cols_next[0] + lane_fold(d_embed)
    cols_next[1] = cols_next[1] + lane_fold(grad)

    @pl.when(last_step())
    def _():
        slope_ref[...] = fold_blocks(slope_sum[...])
        col_ref[...] = columns([(j, cols[j]) for j in range(4)]
                               + [(BASE, cols_next[0]), (BASE + 1, cols_next[1])])


def call(kernel, name, scalars, ins, outs, scratch, steps, flops=10**9):
    def spec(shape, chunked):
        if chunked:
            return pl.BlockSpec(shape[:-1] + (CHUNK,), lambda i, *_: (0,) * (len(shape) - 1) + (i,))
        return pl.BlockSpec(shape, lambda i, *_: (0,) * len(shape))

    moved = sum(a.size * a.dtype.itemsize for a, _ in ins)
    return pl.pallas_call(
        kernel,
        grid_spec=pltpu.PrefetchScalarGridSpec(
            num_scalar_prefetch=len(scalars),
            grid=(steps,),
            in_specs=[spec(a.shape, chunked) for a, chunked in ins],
            out_specs=[spec(s, chunked) for s, _, chunked in outs],
            scratch_shapes=[pltpu.VMEM(s, t) for s, t in scratch],
        ),
        out_shape=[jax.ShapeDtypeStruct(s, t) for s, t, _ in outs],
        compiler_params=pltpu.CompilerParams(
            dimension_semantics=("arbitrary",), vmem_limit_bytes=56 * 2**20
        ),
        cost_estimate=pl.CostEstimate(flops=flops, bytes_accessed=moved, transcendentals=0),
        name=name,
    )(*scalars, *[a for a, _ in ins])


def swap(value, axis, mask):
    size = lax.axis_size(axis)
    return lax.ppermute(value, axis, [(i, i ^ mask) for i in range(size)])


def xor_order(pieces, index):
    step = 1
    while step < len(pieces):
        bit = (index & step) != 0
        pieces = [jnp.where(bit, pieces[j ^ step], pieces[j]) for j in range(len(pieces))]
        step *= 2
    return pieces


def bit_groups(size):
    bits = size.bit_length() - 1
    groups, low = [], 1
    while low < bits:
        width = min(2, bits - low)
        groups.append((low, width))
        low += width
    return groups


def gather_all(block):
    mesh_size, pts_size = lax.axis_size("mesh"), lax.axis_size("pts")
    me = lax.axis_index("mesh")
    tail = block.shape
    held = lax.all_to_all(jnp.broadcast_to(block[None], (pts_size,) + tail), "pts", 0, 0)
    held = held[None]
    for low, width in bit_groups(mesh_size):
        parts = [held] + [swap(held, "mesh", k << low) for k in range(1, 1 << width)]
        held = jnp.stack(xor_order(parts, (me >> low) & ((1 << width) - 1)))
        held = held.reshape((-1,) + held.shape[2:])
    other = swap(held, "mesh", 1)
    held = jnp.stack(xor_order([held, other], me & 1), 1)
    return held.reshape((mesh_size * pts_size,) + tail)


def scatter_sum(blocks):
    mesh_size, pts_size = lax.axis_size("mesh"), lax.axis_size("pts")
    me = lax.axis_index("mesh")
    tail = blocks.shape[1:]
    held = blocks.reshape((mesh_size // 2, 2, pts_size) + tail)
    odd = (me & 1) != 0
    keep = jnp.where(odd, held[:, 1], held[:, 0])
    send = jnp.where(odd, held[:, 0], held[:, 1])
    held = keep + swap(send, "mesh", 1)
    for low, width in reversed(bit_groups(mesh_size)):
        count = 1 << width
        held = held.reshape((count, -1, pts_size) + tail)
        pieces = xor_order([held[j] for j in range(count)], (me >> low) & (count - 1))
        total = pieces[0]
        for k in range(1, count):
            total = total + swap(pieces[k], "mesh", k << low)
        held = total
    held = held.reshape((pts_size,) + tail)
    return jnp.sum(lax.all_to_all(held, "pts", 0, 0), 0)


def all_sum(values):
    count = lax.axis_size("mesh") * lax.axis_size("pts")
    wide = jnp.broadcast_to(values[None, :, None], (count,) + values.shape + (128,))
    return jnp.sum(lax.all_to_all(wide, ALL, 0, 0)[:, :, 0], 0)


def adamw(weight, moment, second, grad, factor):
    clipped = grad * factor
    moment = BETA_ONE * moment + (1.0 - BETA_ONE) * clipped
    second = BETA_TWO * second + (1.0 - BETA_TWO) * clipped * clipped
    moment_hat = moment / (1.0 - BETA_ONE**STEP)
    second_hat = second / (1.0 - BETA_TWO**STEP)
    updated = weight - LEARN * (moment_hat / (jnp.sqrt(second_hat) + EPS_ADAM) + DECAY * weight)
    return (moment, second, updated)


def per_device(
    features,
    targets,
    mesh_slot,
    matrices,
    matrices_moment,
    matrices_second,
    smalls,
    smalls_moment,
    smalls_second,
    vectors,
    vectors_moment,
    vectors_second,
):
    groups, npts = lax.axis_size("mesh"), lax.axis_size("pts")
    devices = groups * npts
    cols, width = matrices.shape[2], smalls.shape[1]
    count_mats, count_vecs = matrices.shape[0], vectors.shape[0]
    points = mesh_slot.shape[0]
    steps = points // CHUNK
    mat_rows = count_mats * cols
    pad_rows = -(mat_rows + cols + LAYERS) % 8
    first = mat_rows + cols
    block = jnp.concatenate(
        [
            matrices.astype(BF).transpose(0, 2, 1).reshape(mat_rows, D),
            jnp.pad(vectors.astype(BF).T, ((0, 0), (0, D - count_vecs))),
            jnp.pad(smalls.astype(BF), ((0, pad_rows), (0, D - width))),
        ]
    )
    whole = gather_all(block)
    mats = (
        whole[:, :mat_rows]
        .reshape(devices, count_mats, cols, D)
        .transpose(1, 0, 2, 3)
        .reshape(count_mats, D, D)
    )
    vec_low = whole[:, mat_rows:first, :128].reshape(D, 128)
    vec = vec_low.astype(F32)
    we1 = vec_low[:, BASE + 4 : BASE + 4 + F_IN]
    whd = vec_low[:, BASE + 4 + F_IN : BASE + 4 + F_IN + F_OUT]
    small = (
        whole[:, first : first + LAYERS, :width].transpose(1, 0, 2).reshape(LAYERS, DH, S + 3 * DH)
    )

    slot = mesh_slot[None]
    ids = jnp.arange(MESH_GRP)
    member = mesh_slot.reshape(steps, CHUNK)[:, :, None] == ids
    here = jnp.any(member, 1).astype(I32)
    there = jnp.any(here != 0, 0).astype(I32)
    big = jnp.where(lax.axis_index("pts") == 0, mesh_slot[points - 1], mesh_slot[0])[None]
    scalars = (here, big)

    wide = (D, points)
    tall = (HS, points)
    acts = [(wide, BF, True), (wide, BF, True), (tall, F32, True), (tall, BF, True)]
    nd_out = [((MESH_GRP, ND_ROWS, HS), F32, False), ((ND_ROWS, HS), BF, False)]
    one_out = [((D, HS), BF, False), ((ND_ROWS, HS), F32, False), ((S, HS), F32, False),
               ((DH, HS), BF, False), ((3 * DH, HS), BF, False)]
    square = ((D, D), F32, False)
    sums = ((MESH_GRP, D + 16, HS), F32)
    turn_sums = ((MESH_GRP, D, HS), F32)

    def exchange(value):
        return [value] + [swap(value, "pts", k) for k in range(1, npts)]

    def whole_in(*arrays):
        return [(a, False) for a in arrays]

    def parts_in(*arrays):
        return [(a, True) for a in arrays]

    h0, x0, f0, probs0, w0, nd0, send = call(
        embed_kernel, "embed", scalars,
        parts_in(features, slot) + whole_in(vec, we1, mats[10], mats[0], mats[1], small[0]),
        [(wide, F32, True)] + acts + nd_out,
        [sums, ((HS, D), BF)], steps,
    )

    def small_call(nd, layer):
        return call(
            small_kernel, "small_fwd", (there, big), whole_in(nd, small[layer]),
            [((MESH_GRP, D, HS), BF, False), ((MESH_GRP, S, HS), F32, False),
             ((MESH_GRP, DH, HS), BF, False), ((MESH_GRP, 3 * DH, HS), BF, False)],
            [], 1,
        )

    parts = exchange(send)
    few0 = small_call(nd0, 0)
    res = call(
        functools.partial(middle_kernel, npts), "middle", scalars,
        whole_in(*parts, few0[0]) + parts_in(w0, h0, slot)
        + whole_in(vec, mats[2], mats[3], mats[4], mats[5], mats[6], small[0], small[1]),
        one_out + [(wide, BF, True), (wide, F32, True), (wide, F32, True), (wide, F32, True)]
        + acts + nd_out,
        [((MESH_GRP, D, HS), BF), ((D, CHUNK), F32), sums, ((HS, D), BF)], steps,
    )
    one0, (y0, m0, p0, h1, x1, f1, probs1, w1, nd1, send) = res[:5], res[5:]

    parts = exchange(send)
    few1 = small_call(nd1, 1)
    res = call(
        functools.partial(head_kernel, npts), "head", scalars,
        whole_in(*parts, few1[0]) + parts_in(w1, h1, slot, targets)
        + whole_in(vec, mats[7], mats[8], mats[9], whd, small[1]),
        one_out + [(wide, BF, True), (wide, F32, True), (wide, F32, True), (wide, F32, True),
                   ((F_OUT, points), F32, True), ((8, 128), F32, False)],
        [((MESH_GRP, D, HS), BF), ((D, CHUNK), F32), ((8, 128), F32)], steps,
    )
    one1, (y1, m1, p1, h2, diff, loss_part) = res[:5], res[5:]

    keeps = [(wide, BF, True)] * 6 + [(wide, F32, True)]
    ds_out = [((MESH_GRP, DH, HS), BF, False), ((DH, HS), BF, False)]
    vec_cols = ((D, 128), F32, False)
    parts = exchange(loss_part)
    res = call(
        functools.partial(loss_kernel, npts, groups), "loss_bwd", scalars,
        whole_in(*parts) + parts_in(diff, slot, h2, p1, m1, y1, w1)
        + whole_in(vec, whd, mats[8], mats[9], mats[7]),
        [((8, 128), F32, False), ((D, F_OUT), F32, False), vec_cols] + ds_out + keeps,
        [((8, 128), F32), ((7, D, 128), F32), turn_sums] + [((D, D), BF)] * 3, steps,
    )
    rel, g_whd, cols_a, ds1, send = res[:5]
    keep1 = res[5:]

    def weights_call(keep, y_low):
        return call(
            weights_kernel, "weights", (), parts_in(*keep[:5], y_low), [square] * 3, [], steps,
        )

    def small_back(ds, nd, few, layer):
        return call(
            small_back_kernel, "small_bwd", (there, big),
            whole_in(ds, nd, few[1], few[2], few[3], few[0], small[layer]),
            [((MESH_GRP, HS, HS), BF, False), ((MESH_GRP, D, HS), BF, False),
             ((MESH_GRP, HS, 128), F32, False), ((DH, 3 * DH), F32, False)],
            [], 1,
        )

    tail_scratch = [((MESH_GRP, HS, HS), BF), ((MESH_GRP, D, HS), BF), ((MESH_GRP, HS, 128), F32),
                    ((D, HS), BF), ((HS, CHUNK), F32), ((D, CHUNK), F32), ((D, HS), F32)]
    tail_out = [((DH, 3 * DH), F32, False), ((DH, HS), F32, False), square, square, vec_cols]

    parts = exchange(send)
    g_w2b, g_w1b, g_wob = weights_call(keep1, y1)
    back1 = small_back(ds1, nd1, few1, 1)
    res = call(
        functools.partial(turn_kernel, npts), "turn", scalars,
        whole_in(*parts, *back1, one1[1], one1[2], one1[3], one1[4], one1[0], small[1])
        + parts_in(h1, x1, f1, probs1, w1, keep1[5], keep1[6], slot)
        + whole_in(vec, mats[5], mats[6]) + parts_in(p0, m0, y0, w0)
        + whole_in(mats[3], mats[4], mats[2]),
        tail_out + ds_out + keeps,
        tail_scratch + [((4, D, 128), F32), ((5, D, 128), F32), turn_sums] + [((D, D), BF)] * 5,
        steps,
    )
    dw1, slope1, g_wxb, g_wfb, cols_b, ds0, send = res[:7]
    keep0 = res[7:]

    parts = exchange(send)
    g_w2a, g_w1a, g_woa = weights_call(keep0, y0)
    back0 = small_back(ds0, nd0, few0, 0)
    dw0, slope0, g_wxa, g_wfa, cols_c, g_we2, g_we1 = call(
        functools.partial(end_kernel, npts), "end", scalars,
        whole_in(*parts, *back0, one0[1], one0[2], one0[3], one0[4], one0[0], small[0])
        + parts_in(h0, x0, f0, probs0, w0, keep0[5], keep0[6], slot)
        + whole_in(vec, mats[0], mats[1]) + parts_in(features) + whole_in(we1, mats[10]),
        tail_out + [square, ((D, F_IN), F32, False)],
        tail_scratch + [((4, D, 128), F32), ((2, D, 128), F32)] + [((D, D), BF)] * 3,
        steps,
    )

    grads_mats = jnp.stack([g_wxa, g_wfa, g_woa, g_w1a, g_w2a, g_wxb, g_wfb, g_wob, g_w1b, g_w2b, g_we2])
    grads_cols = (cols_a + cols_b + cols_c)[:, : BASE + 4]
    grads_vecs = jnp.concatenate([grads_cols, g_we1, g_whd], 1)

    def small_grad(slope, mixed):
        return jnp.concatenate([slope.reshape(DH, H, S).sum(1), mixed], 1).reshape(-1)

    grads_small = jnp.stack([small_grad(slope0, dw0), small_grad(slope1, dw1)])
    grads = jnp.concatenate(
        [
            grads_mats.reshape(count_mats, devices, cols, D).transpose(1, 0, 2, 3).reshape(devices, mat_rows, D),
            jnp.pad(grads_vecs.reshape(devices, cols, count_vecs), ((0, 0), (0, 0), (0, D - count_vecs))),
            jnp.pad(grads_small.reshape(LAYERS, devices, width).transpose(1, 0, 2),
                    ((0, 0), (0, pad_rows), (0, D - width))),
        ],
        1,
    )
    own = scatter_sum(grads)
    red_mats = own[:mat_rows].reshape(count_mats, cols, D).transpose(0, 2, 1)
    red_vecs = own[mat_rows:first, :count_vecs].T
    red_small = own[first : first + LAYERS, :width]
    squares = (
        jnp.sum(red_mats * red_mats) + jnp.sum(red_small * red_small) + jnp.sum(red_vecs * red_vecs)
    )
    group_loss = jnp.sum(rel[:MESH_GRP, 0]) / (MESH_GRP * devices)
    totals = all_sum(jnp.stack([squares, group_loss]))
    grad_norm = jnp.sqrt(totals[0])
    factor = jnp.minimum(1.0, CLIP / grad_norm)
    mat_out = adamw(matrices, matrices_moment, matrices_second, red_mats, factor)
    small_out = adamw(smalls, smalls_moment, smalls_second, red_small, factor)
    vec_out = adamw(vectors, vectors_moment, vectors_second, red_vecs, factor)
    return (totals[1], grad_norm) + mat_out + small_out + vec_out


def solution(mesh):
    both = ("mesh", "pts")
    cube, flat = P(None, None, both), P(None, both)
    return jax.shard_map(
        per_device,
        mesh=mesh,
        in_specs=(flat, flat, P(both), cube, cube, cube, flat, flat, flat, flat, flat, flat),
        out_specs=(P(), P(), cube, cube, cube, flat, flat, flat, flat, flat, flat),
        check_vma=False,
    )
```

```python
import functools
import jax
import jax.numpy as jnp
from jax import lax
from jax.experimental import pallas as pl
from jax.experimental.pallas import tpu as pltpu
from jax.sharding import PartitionSpec as P

D = 256
H = 8
DH = 32
S = 64
HS = H * S
F_IN = 7
F_OUT = 4
LAYERS = 2
MESH_GRP = 4
STEP = 5
SUB = 512
ND_ROWS = 40


EPS_NORM = 1e-05
EPS_SLICE = 1e-05
EPS_LOSS = 1e-06
CLIP = 0.01
LEARN = 0.03
BETA_ONE = 0.9
BETA_TWO = 0.95
EPS_ADAM = 1e-08
DECAY = 0.1
BF = jnp.bfloat16
F32 = jnp.float32
I32 = jnp.int32
ALL = ("mesh", "pts")
BASE = 9 * LAYERS


def dot(left, right):
    return jnp.dot(left, right, preferred_element_type=F32)


def dot_nt(left, right):
    return lax.dot_general(left, right, (((1,), (1,)), ((), ())), preferred_element_type=F32)


def dot_tn(left, right):
    return lax.dot_general(left, right, (((0,), (0,)), ((), ())), preferred_element_type=F32)


def low(value):
    return value.astype(BF)


def block_mask():
    rows = lax.broadcasted_iota(I32, (D, HS), 0) // DH
    cols = lax.broadcasted_iota(I32, (D, HS), 1) // S
    return rows == cols


def spread_blocks(compact):
    tall = jnp.concatenate([compact] * H, 0)
    return jnp.where(block_mask(), tall, jnp.zeros_like(tall))


def fold_blocks(full):
    lanes = lax.broadcasted_iota(I32, (DH, HS), 1) // S
    total = jnp.zeros((DH, HS), F32)
    for head in range(H):
        total = jnp.where(lanes == head, full[head * DH : (head + 1) * DH], total)
    return total


def pick_matrix():
    rows = lax.broadcasted_iota(I32, (S, HS), 0)
    cols = lax.broadcasted_iota(I32, (S, HS), 1) % S
    return (rows == cols).astype(F32).astype(BF)


def norm_stats(hidden):
    row_mean = jnp.sum(hidden, 0, keepdims=True) * (1.0 / D)
    centred = hidden - row_mean
    row_var = jnp.sum(centred * centred, 0, keepdims=True) * (1.0 / D)
    return centred, lax.rsqrt(row_var + EPS_NORM)


def norm_apply(hidden, gain, shift):
    centred, scale = norm_stats(hidden)
    return low(centred * scale * gain + shift)


def norm_back(grad, unit, scale, gain):
    inner = grad * gain
    first = jnp.sum(inner, 0, keepdims=True) * (1.0 / D)
    second = jnp.sum(inner * unit, 0, keepdims=True) * (1.0 / D)
    return scale * (inner - first - unit * second)


ROOT = 0.7978845608028654
CUBIC = 0.044715


def gelu(value):
    return 0.5 * value * (1.0 + jnp.tanh(ROOT * (value + CUBIC * (value * value * value))))


def gelu_both(value):
    square = value * value
    bend = jnp.tanh(ROOT * (value + CUBIC * (square * value)))
    half = 0.5 * (1.0 + bend)
    slope = half + 0.5 * value * (1.0 - bend * bend) * (ROOT * (1.0 + 3.0 * CUBIC * square))
    return value * half, slope


def lane_fold(value):
    total = value[:, :128]
    for start in range(128, value.shape[1], 128):
        total = total + value[:, start : start + 128]
    return total


def columns(sums):
    lanes = lax.broadcasted_iota(I32, (D, 128), 1)
    total = jnp.zeros((D, 128), F32)
    for index, value in sums:
        total = jnp.where(lanes == index, jnp.sum(value, 1, keepdims=True), total)
    return total


def slice_matrix(small):
    wide = jnp.concatenate([small[:, :S], small[:, :S]], 1)
    return spread_blocks(jnp.concatenate([wide] * (HS // (2 * S)), 1))


def slice_forward(num_den, small):
    tokens = low(num_den[:DH] / (num_den[DH : DH + 1] + EPS_SLICE))
    mixed = low(dot_tn(small[:, S:], tokens))
    pick = pick_matrix()
    keys = low(dot_nt(pick, spread_blocks(mixed[DH : 2 * DH])))
    values = low(dot_nt(spread_blocks(mixed[2 * DH :]), pick))
    scores = dot(keys, spread_blocks(mixed[:DH])) * DH ** (-0.5)
    scores = scores - jnp.max(scores, 0, keepdims=True)
    raised = jnp.exp(scores)
    attn = raised / jnp.sum(raised, 0, keepdims=True)
    full = dot(values, low(attn))
    routed = low(jnp.where(block_mask(), full, jnp.zeros_like(full)))
    return routed, attn, tokens, mixed


def widen(tall):
    pair = jnp.concatenate([tall, tall], 1)
    return fold_blocks(jnp.concatenate([pair] * (HS // (2 * S)), 1))


def slice_backward(d_slice, num_den, attn, tokens, mixed, small):
    attn_low = low(attn)
    pick = pick_matrix()
    d_full = spread_blocks(d_slice)
    query_full = spread_blocks(mixed[:DH])
    values = low(dot_nt(pick, spread_blocks(mixed[2 * DH :])))
    keys = low(dot_nt(spread_blocks(mixed[DH : 2 * DH]), pick))
    d_attn = dot(values, d_full)
    d_values = low(widen(dot_nt(d_full, attn_low)))
    d_scores = low(attn * (d_attn - jnp.sum(d_attn * attn, 0, keepdims=True)))
    scale = DH ** (-0.5)
    d_queries = low(fold_blocks(dot(keys, d_scores)) * scale)
    d_keys = low(widen(dot_nt(query_full, d_scores)) * scale)
    d_mixed = jnp.concatenate([d_queries, d_keys, d_values], 0)
    d_tokens = dot(small[:, S:], d_mixed)
    d_weight = dot_nt(tokens, d_mixed)
    inverse = 1.0 / (num_den[DH : DH + 1] + EPS_SLICE)
    d_num = low(d_tokens * inverse)
    d_den = -jnp.sum(d_tokens * num_den[:DH], 0, keepdims=True) * inverse * inverse
    return spread_blocks(d_num), d_den, d_weight


def is_mesh(slot, mesh_id):
    return (slot == mesh_id).astype(F32)


def columns_at(vec, index):
    return vec[:, index : index + 1]


def sum_parts(parts):
    terms = [part[...].astype(F32) for part in parts]
    while len(terms) > 1:
        terms = [terms[i] + terms[i + 1] for i in range(0, len(terms), 2)]
    return terms[0]


def put(grads_ref, row, value):
    devices, rows, _ = grads_ref.shape
    cols = rows // 12
    grads_ref[:, row * cols : (row + 1) * cols, :] = value.reshape(devices, cols, D)


def put_columns(grads_ref, sums, fresh=False):
    devices, rows, _ = grads_ref.shape
    cols = rows // 12
    value = columns(sums).reshape(devices, cols, 128)
    if not fresh:
        value = value + grads_ref[:, 11 * cols :, :128]
    grads_ref[:, 11 * cols :, :128] = value


def start_copies(sources, targets, sems, first):
    copies = [
        pltpu.make_async_copy(a, b, sems.at[first + j]) for j, (a, b) in enumerate(zip(sources, targets))
    ]
    for copy in copies:
        copy.start()
    return copies


def finish_copies(copies):
    for copy in copies:
        copy.wait()


def each_local(info, visit):
    for mesh_id in range(MESH_GRP):

        @pl.when(info[1 + mesh_id] != 0)
        def _():
            visit(mesh_id)


def local_blocks(info, mesh_id, visit):
    def step(index, carry):
        visit(pl.ds(pl.multiple_of(index * SUB, SUB), SUB))
        return carry

    lax.fori_loop(info[5 + mesh_id], info[9 + mesh_id], step, 0)


def front(hidden, vec, layer, mats, small, slot, info, w_ref, nd_ref, send_ref, acc, stage, far, sems):
    x_ref, f_ref, probs_ref = stage
    base = 9 * layer
    width = hidden.shape[1]
    u = norm_apply(hidden, columns_at(vec, base), columns_at(vec, base + 1))
    pair = dot(mats[5 * layer : 5 * layer + 2].reshape(2 * D, D), u)
    x_low = low(pair[:D] + columns_at(vec, base + 2))
    f_low = low(pair[D:] + columns_at(vec, base + 3))
    x_ref[...] = x_low
    f_ref[...] = f_low
    copies = start_copies(stage[:2], far[:2], sems, 0)
    logits = dot(slice_matrix(small[layer]).T, x_low).reshape(H, S, width)
    raised = jnp.exp(logits - jnp.max(logits, 1, keepdims=True))
    valid = (slot[...] < MESH_GRP).astype(F32)
    probs = (raised * (valid[None] / jnp.sum(raised, 1, keepdims=True))).reshape(HS, width)
    probs_ref[...] = probs
    copies = copies + start_copies(stage[2:], far[2:], sems, 2)
    w_low = low(probs)
    w_ref[...] = w_low

    def rows_of(features, mine):
        ones = jnp.broadcast_to(mine, (16, mine.shape[1]))
        return jnp.concatenate([low(features.astype(F32) * mine), low(ones)], 0)

    def compact(full):
        return jnp.concatenate([fold_blocks(full[:D]), full[D : D + ND_ROWS - DH]], 0)

    send_ref[...] = low(compact(dot_nt(rows_of(f_low, is_mesh(slot[...], info[0])), w_low)))

    def visit(mesh_id):
        acc[...] = jnp.zeros_like(acc)

        def add(part):
            acc[...] = acc[...] + dot_nt(rows_of(f_ref[:, part], is_mesh(slot[:, part], mesh_id)), w_ref[:, part])

        local_blocks(info, mesh_id, add)
        nd_ref[mesh_id] = compact(acc[...])

    each_local(info, visit)
    return copies


def back_half(w_in, slot, info, routed, routed_big, mix, hidden, vec, layer, mats):
    base = 9 * layer
    mix[...] = dot(routed_big[...], w_in[...]) * is_mesh(slot[...], info[0])

    def visit(mesh_id):
        def add(part):
            mix[:, part] = mix[:, part] + dot(routed[mesh_id], w_in[:, part]) * is_mesh(slot[:, part], mesh_id)

        local_blocks(info, mesh_id, add)

    each_local(info, visit)
    y_low = low(mix[...])
    middle = hidden + dot(mats[5 * layer + 2], y_low) + columns_at(vec, base + 4)
    u2 = norm_apply(middle, columns_at(vec, base + 5), columns_at(vec, base + 6))
    pre = dot(mats[5 * layer + 3], u2) + columns_at(vec, base + 7)
    out = middle + dot(mats[5 * layer + 4], low(gelu(pre))) + columns_at(vec, base + 8)
    return y_low, middle, out


def head_half(grad, vec, layer, mats, middle, probs, y_low, slot, info, grads_ref, ds_ref, send_ref, acc, keep):
    base = 9 * layer
    grad_low = low(grad)
    centred, scale = norm_stats(middle)
    unit = centred * scale
    gain = columns_at(vec, base + 5)
    u2 = low(unit * gain + columns_at(vec, base + 6))
    activ, slope = gelu_both(dot(mats[5 * layer + 3], u2) + columns_at(vec, base + 7))
    d_pre = dot_tn(mats[5 * layer + 4], grad_low) * slope
    d_pre_low = low(d_pre)
    d_norm = dot_tn(mats[5 * layer + 3], d_pre_low)
    d_mid = norm_back(d_norm, unit, scale, gain) + grad
    d_mid_low = low(d_mid)
    d_y = low(dot_tn(mats[5 * layer + 2], d_mid_low))
    d_y_ref, d_mid_ref = keep
    d_y_ref[...] = d_y
    d_mid_ref[...] = d_mid
    put(grads_ref, 5 * layer + 4, dot_nt(grad_low, low(activ)))
    put(grads_ref, 5 * layer + 3, dot_nt(d_pre_low, u2))
    put(grads_ref, 5 * layer + 2, dot_nt(d_mid_low, y_low))
    own = low(d_y.astype(F32) * is_mesh(slot[...], info[0]))
    send_ref[...] = low(fold_blocks(dot_nt(own, low(probs[...]))))

    def visit(mesh_id):
        acc[...] = jnp.zeros_like(acc)

        def add(part):
            mine = low(d_y_ref[:, part].astype(F32) * is_mesh(slot[:, part], mesh_id))
            acc[...] = acc[...] + dot_nt(mine, low(probs[:, part]))

        local_blocks(info, mesh_id, add)
        ds_ref[mesh_id] = low(fold_blocks(acc[...]))

    each_local(info, visit)
    return [(base + 4, lane_fold(d_mid)), (base + 5, lane_fold(d_norm * unit)),
            (base + 6, lane_fold(d_norm)), (base + 7, lane_fold(d_pre)), (base + 8, lane_fold(grad))]


def tail_half(vec, layer, mats, small, hidden, x_in, f_in, probs_in, d_y, d_mid, slot, info,
              back, back_big, route, mix, slope_ref, grads_ref):
    width = hidden.shape[1]
    base = 9 * layer
    both_big, num_big, den_big = back_big
    both, d_num, d_den = back
    mine = is_mesh(slot[...], info[0])
    pair = jnp.concatenate([d_y[...], f_in[...]], 0)
    route[...] = (dot(both_big, pair) + den_big) * mine
    mix[...] = dot(num_big, low(probs_in[...])) * mine

    def visit(mesh_id):
        def add(part):
            here = is_mesh(slot[:, part], mesh_id)
            piece = jnp.concatenate([d_y[:, part], f_in[:, part]], 0)
            route[:, part] = route[:, part] + (dot(both[mesh_id], piece) + d_den[mesh_id][:, :1]) * here
            mix[:, part] = mix[:, part] + dot(d_num[mesh_id], low(probs_in[:, part])) * here

        local_blocks(info, mesh_id, add)

    each_local(info, visit)
    d_probs = route[...].reshape(H, S, width)
    probs = probs_in[...].reshape(H, S, width)
    spread = jnp.sum(d_probs * probs, 1, keepdims=True)
    d_logits = low(probs * (d_probs - spread)).reshape(HS, width)
    d_x = dot(slice_matrix(small[layer]), d_logits)
    d_f = mix[...]
    slope_ref[...] = fold_blocks(dot_nt(x_in[...], d_logits))
    d_pair = jnp.concatenate([low(d_x), low(d_f)], 0)
    d_norm = dot_tn(mats[5 * layer : 5 * layer + 2].reshape(2 * D, D), d_pair)
    centred, scale = norm_stats(hidden)
    unit = centred * scale
    gain = columns_at(vec, base)
    u = low(unit * gain + columns_at(vec, base + 1))
    grads = dot_nt(d_pair, u)
    put(grads_ref, 5 * layer, grads[:D])
    put(grads_ref, 5 * layer + 1, grads[D:])
    sums = [(base, lane_fold(d_norm * unit)), (base + 1, lane_fold(d_norm)),
            (base + 2, lane_fold(d_x)), (base + 3, lane_fold(d_f))]
    return norm_back(d_norm, unit, scale, gain) + d_mid[...], sums


def embed_kernel(info, feat, slot, vec, we1, mats, small,
                 h_ref, w_ref, nd_ref, send_ref, h_far, x_far, f_far, probs_far,
                 acc, x_ref, f_ref, probs_ref, sems):
    e1 = dot(we1[...], low(feat[...])) + columns_at(vec, BASE)
    hidden = dot(mats[5 * LAYERS], low(gelu(e1))) + columns_at(vec, BASE + 1)
    h_ref[...] = hidden
    copies = start_copies([h_ref], [h_far], sems, 3)
    copies = copies + front(hidden, vec, 0, mats, small, slot, info, w_ref, nd_ref, send_ref, acc,
                            (x_ref, f_ref, probs_ref), (x_far, f_far, probs_far), sems)
    finish_copies(copies)


def small_kernel(layer, info, nd_ref, small, routed_ref, routed_far, attn_far, tokens_far, mixed_far,
                 attn_ref, tokens_ref, mixed_ref, sems):
    stage = (routed_ref, attn_ref, tokens_ref, mixed_ref)
    far = (routed_far, attn_far, tokens_far, mixed_far)

    def copies(mesh_id):
        return [
            pltpu.make_async_copy(a.at[mesh_id], b.at[mesh_id], sems.at[4 * mesh_id + j])
            for j, (a, b) in enumerate(zip(stage, far))
        ]

    def visit(mesh_id):
        for ref, value in zip(stage, slice_forward(nd_ref[mesh_id], small[layer])):
            ref[mesh_id] = value
        for copy in copies(mesh_id):
            copy.start()

    each_local(info, visit)
    each_local(info, lambda mesh_id: finish_copies(copies(mesh_id)))


def share_start(parts, small, stage, far, sems, first):
    total = sum_parts(parts)
    for ref, value in zip(stage, slice_forward(total, small) + (total,)):
        ref[...] = value
    return start_copies(stage, far, sems, first)


def middle_kernel(npts, info, *refs):
    parts, refs = refs[:npts], refs[npts:]
    (routed, w_in, h_in, slot, vec, mats, small,
     h_ref, w_ref, nd_ref, send_ref, *refs) = refs
    share_far, (y_far, m_far, h_far, x_far, f_far, probs_far), refs = refs[:5], refs[5:11], refs[11:]
    share, (y_ref, m_ref, x_ref, f_ref, probs_ref, mix, acc, sems) = refs[:5], refs[5:]
    copies = share_start(parts, small[0], share, share_far, sems, 6)
    y_low, middle, out = back_half(w_in, slot, info, routed, share[0], mix, h_in[...], vec, 0, mats)
    y_ref[...] = y_low
    m_ref[...] = middle
    h_ref[...] = out
    copies = copies + start_copies((h_ref, y_ref, m_ref), (h_far, y_far, m_far), sems, 3)
    copies = copies + front(out, vec, 1, mats, small, slot, info, w_ref, nd_ref, send_ref, acc,
                            (x_ref, f_ref, probs_ref), (x_far, f_far, probs_far), sems)
    finish_copies(copies)


def head_kernel(npts, info, *refs):
    parts, refs = refs[:npts], refs[npts:]
    (routed, w_in, h_in, slot, target, vec, mats, whd, small,
     y_ref, m_ref, h_ref, diff_ref, loss_ref, *refs) = refs
    share_far, share, (mix, sems) = refs[:5], refs[5:10], refs[10:]
    copies = share_start(parts, small[1], share, share_far, sems, 0)
    y_low, middle, out = back_half(w_in, slot, info, routed, share[0], mix, h_in[...], vec, 1, mats)
    y_ref[...] = y_low
    m_ref[...] = middle
    h_ref[...] = out
    uh = norm_apply(out, columns_at(vec, BASE + 2), columns_at(vec, BASE + 3))
    truth = target[...]
    differ = dot_tn(whd[...], uh) - truth
    diff_ref[...] = differ
    ids = lax.broadcasted_iota(I32, differ.shape, 0)
    member = (ids == slot[...]).astype(F32)
    squares = jnp.sum(differ * differ, 0, keepdims=True)
    sizes = jnp.sum(truth * truth, 0, keepdims=True)
    both = lane_fold(jnp.concatenate([member * squares, member * sizes], 0))
    loss_ref[...] = jnp.broadcast_to(jnp.sum(both, 1, keepdims=True), loss_ref.shape)
    finish_copies(copies)


def loss_kernel(npts, groups, info, *refs):
    parts, refs = refs[:npts], refs[npts:]
    diff, slot, h_in, vec, whd, grad_ref, rel_ref, grads_ref = refs
    total = sum_parts(parts)
    err_root = jnp.sqrt(total[:MESH_GRP] + EPS_LOSS)
    tgt_root = jnp.sqrt(total[MESH_GRP:] + EPS_LOSS)
    rel_ref[...] = jnp.concatenate([err_root / tgt_root, jnp.zeros_like(err_root)], 0)
    coef = (1.0 / (err_root * tgt_root) * (1.0 / (MESH_GRP * groups)))[:, :1]
    ids = lax.broadcasted_iota(I32, diff.shape, 0)
    member = (ids == slot[...]).astype(F32)
    d_pred = low(diff[...] * jnp.sum(member * coef, 0, keepdims=True))
    d_head = dot(whd[...], d_pred)
    centred, scale = norm_stats(h_in[...])
    unit = centred * scale
    gain = columns_at(vec, BASE + 2)
    g_whd = dot_nt(low(unit * gain + columns_at(vec, BASE + 3)), d_pred)
    put_columns(grads_ref, [(BASE + 2, lane_fold(d_head * unit)), (BASE + 3, lane_fold(d_head))]
                + [(BASE + 4 + F_IN + j, g_whd[:, j : j + 1]) for j in range(F_OUT)], True)
    grad_ref[...] = norm_back(d_head, unit, scale, gain)


def half_kernel(layer, info, grad, middle, probs, y_low, slot, vec, mats, grads_ref,
                ds_ref, send_ref, d_y_ref, d_mid_ref, acc):
    sums = head_half(grad[...], vec, layer, mats, middle[...], probs, y_low[...], slot, info, grads_ref,
                     ds_ref, send_ref, acc, (d_y_ref, d_mid_ref))
    put_columns(grads_ref, sums)


def small_back_kernel(layer, info, ds_in, nd_ref, attn, tokens, mixed, routed, small,
                      both_ref, dn_ref, den_ref, dw_ref):
    dw_ref[...] = jnp.zeros_like(dw_ref)

    def visit(mesh_id):
        dn, den, dw = slice_backward(ds_in[mesh_id], nd_ref[mesh_id], attn[mesh_id],
                                     tokens[mesh_id], mixed[mesh_id], small[layer])
        both_ref[mesh_id] = jnp.concatenate([routed[mesh_id], dn], 0).T
        dn_ref[mesh_id] = dn
        den_ref[mesh_id] = jnp.broadcast_to(den, (128, HS)).T
        dw_ref[...] = dw_ref[...] + dw

    each_local(info, visit)


def tail_start(npts, parts, small, ndb, attn, tokens, mixed, routed_big, dw_in, dw_ref):
    total = low(sum_parts(parts))
    d_num, d_den, d_weight = slice_backward(total, ndb[...], attn[...], tokens[...], mixed[...], small)
    dw_ref[...] = dw_in[...] + d_weight * (1.0 / npts)
    both = jnp.concatenate([routed_big[...], d_num], 0).T
    return both, d_num, jnp.broadcast_to(d_den, (128, HS)).T[:, :1]


def tail_kernel(npts, layer, info, *refs):
    parts, refs = refs[:npts], refs[npts:]
    (both_in, dn_in, den_in, dw_in, ndb, attn, tokens, mixed, routed_big, small,
     h_in, x_in, f_in, probs, d_y, d_mid, slot, vec, mats, grads_ref,
     grad_ref, dw_ref, slope_ref, route, mix) = refs
    back_big = tail_start(npts, parts, small[layer], ndb, attn, tokens, mixed, routed_big, dw_in, dw_ref)
    grad, sums = tail_half(vec, layer, mats, small, h_in[...], x_in, f_in, probs, d_y, d_mid, slot, info,
                           (both_in, dn_in, den_in), back_big, route, mix, slope_ref, grads_ref)
    grad_ref[...] = grad
    put_columns(grads_ref, sums)


def end_kernel(npts, info, *refs):
    parts, refs = refs[:npts], refs[npts:]
    (both_in, dn_in, den_in, dw_in, ndb, attn, tokens, mixed, routed_big, small,
     h_in, x_in, f_in, probs, d_y, d_mid, slot, vec, mats, feat, we1, grads_ref,
     dw_ref, slope_ref, route, mix) = refs
    back_big = tail_start(npts, parts, small[0], ndb, attn, tokens, mixed, routed_big, dw_in, dw_ref)
    grad, sums = tail_half(vec, 0, mats, small, h_in[...], x_in, f_in, probs, d_y, d_mid, slot, info,
                           (both_in, dn_in, den_in), back_big, route, mix, slope_ref, grads_ref)
    feat_low = low(feat[...])
    activ, slope = gelu_both(dot(we1[...], feat_low) + columns_at(vec, BASE))
    grad_low = low(grad)
    d_embed = dot_tn(mats[5 * LAYERS], grad_low) * slope
    put(grads_ref, 5 * LAYERS, dot_nt(grad_low, low(activ)))
    g_we1 = dot_nt(low(d_embed), feat_low)
    put_columns(grads_ref, sums + [(BASE, lane_fold(d_embed)), (BASE + 1, lane_fold(grad))]
                + [(BASE + 4 + j, g_we1[:, j : j + 1]) for j in range(F_IN)])


def split_kernel(odd, grads, few, keep_ref, send_ref):
    rows = grads.shape[3]
    for ref, index in ((keep_ref, odd[0]), (send_ref, 1 - odd[0])):
        ref[:, :, :rows] = grads[:, index]
        ref[:, :, rows:] = few[:, index]


LIMITS = dict(embed=14, small_fwd=5, middle=20, head=8, loss=8, half=18, small_bwd=4, tail=16, end=14, split=4)


def call(kernel, name, info, ins, outs, scratch=(), held=None, far=(), sems=0):
    near = len(outs)
    outs = list(outs) + list(far)
    held = {} if held is None else held
    names = list(held)
    plain = [a for a in ins if not isinstance(a, str)]
    inside = pl.BlockSpec(memory_space=pltpu.VMEM)
    table = [] if info is None else [info]
    first, second = len(table) + len(plain), len(table) + len(plain) + len(names)

    def body(*refs):
        rest = iter(refs[len(table) : first])
        kept = dict(zip(names, refs[first:second]))
        order = [kept[a] if isinstance(a, str) else next(rest) for a in ins]
        after = refs[second + len(outs) + len(names) :]
        kernel(*refs[: len(table)], *order, *refs[second : second + len(outs)], *after)

    res = pl.pallas_call(
        body,
        in_specs=[pl.BlockSpec(memory_space=pltpu.SMEM)] * len(table) + [inside] * (second - len(table)),
        out_specs=[inside] * near + [pl.BlockSpec(memory_space=pltpu.HBM)] * len(far) + [inside] * len(names),
        out_shape=[jax.ShapeDtypeStruct(s, t) for s, t in outs]
        + [jax.ShapeDtypeStruct(held[n].shape, held[n].dtype) for n in names],
        input_output_aliases={first + j: len(outs) + j for j in range(len(names))},
        scratch_shapes=[pltpu.VMEM(s, t) for s, t in scratch]
        + ([pltpu.SemaphoreType.DMA((sems,))] if sems else []),
        compiler_params=pltpu.CompilerParams(vmem_limit_bytes=LIMITS[name] * 2**20),
        cost_estimate=pl.CostEstimate(flops=1000, bytes_accessed=1000, transcendentals=0),
        name=name,
    )(*table, *plain, *[held[n] for n in names])
    held.update(zip(names, res[len(outs) :]))
    return res[: len(outs)]


def swap(value, axis, mask):
    size = lax.axis_size(axis)
    return lax.ppermute(value, axis, [(i, i ^ mask) for i in range(size)])


def xor_order(pieces, index):
    step = 1
    while step < len(pieces):
        bit = (index & step) != 0
        pieces = [jnp.where(bit, pieces[j ^ step], pieces[j]) for j in range(len(pieces))]
        step *= 2
    return pieces


def bit_groups(size):
    bits = size.bit_length() - 1
    groups, low = [], 1
    while low < bits:
        width = min(2, bits - low)
        groups.append((low, width))
        low += width
    return groups


def gather_all(block):
    mesh_size, pts_size = lax.axis_size("mesh"), lax.axis_size("pts")
    me = lax.axis_index("mesh")
    tail = block.shape
    held = lax.all_to_all(jnp.broadcast_to(block[None], (pts_size,) + tail), "pts", 0, 0)
    held = held[None]
    for low, width in bit_groups(mesh_size):
        parts = [held] + [swap(held, "mesh", k << low) for k in range(1, 1 << width)]
        held = jnp.stack(xor_order(parts, (me >> low) & ((1 << width) - 1)))
        held = held.reshape((-1,) + held.shape[2:])
    other = swap(held, "mesh", 1)
    held = jnp.stack(xor_order([held, other], me & 1), 1)
    return held.reshape((mesh_size * pts_size,) + tail)


def scatter_sum(keep, send):
    mesh_size, pts_size = lax.axis_size("mesh"), lax.axis_size("pts")
    me = lax.axis_index("mesh")
    tail = keep.shape[2:]
    held = keep + swap(send, "mesh", 1)
    for low, width in reversed(bit_groups(mesh_size)):
        count = 1 << width
        held = held.reshape((count, -1, pts_size) + tail)
        pieces = xor_order([held[j] for j in range(count)], (me >> low) & (count - 1))
        total = pieces[0]
        for k in range(1, count):
            total = total + swap(pieces[k], "mesh", k << low)
        held = total
    held = held.reshape((pts_size,) + tail)
    return jnp.sum(lax.all_to_all(held, "pts", 0, 0), 0)


def all_sum(values):
    count = lax.axis_size("mesh") * lax.axis_size("pts")
    wide = jnp.broadcast_to(values[None, :, None], (count,) + values.shape + (128,))
    return jnp.sum(lax.all_to_all(wide, ALL, 0, 0)[:, :, 0], 0)


def adamw(weight, moment, second, grad, factor):
    clipped = grad * factor
    moment = BETA_ONE * moment + (1.0 - BETA_ONE) * clipped
    second = BETA_TWO * second + (1.0 - BETA_TWO) * clipped * clipped
    moment_hat = moment / (1.0 - BETA_ONE**STEP)
    second_hat = second / (1.0 - BETA_TWO**STEP)
    updated = weight - LEARN * (moment_hat / (jnp.sqrt(second_hat) + EPS_ADAM) + DECAY * weight)
    return (moment, second, updated)


def per_device(
    features,
    targets,
    mesh_slot,
    matrices,
    matrices_moment,
    matrices_second,
    smalls,
    smalls_moment,
    smalls_second,
    vectors,
    vectors_moment,
    vectors_second,
):
    groups, npts = lax.axis_size("mesh"), lax.axis_size("pts")
    devices = groups * npts
    cols, width = matrices.shape[2], smalls.shape[1]
    count_mats, count_vecs = matrices.shape[0], vectors.shape[0]
    points = mesh_slot.shape[0]
    mat_rows = count_mats * cols
    pad_rows = -(mat_rows + cols + LAYERS) % 8
    few_rows = LAYERS + pad_rows
    first = mat_rows + cols
    block = jnp.concatenate(
        [
            matrices.astype(BF).transpose(0, 2, 1).reshape(mat_rows, D),
            jnp.pad(vectors.astype(BF).T, ((0, 0), (0, D - count_vecs))),
            jnp.pad(smalls.astype(BF), ((0, pad_rows), (0, D - width))),
        ]
    )
    whole = gather_all(block)
    mats = (
        whole[:, :mat_rows]
        .reshape(devices, count_mats, cols, D)
        .transpose(1, 0, 2, 3)
        .reshape(count_mats, D, D)
    )
    vec_low = whole[:, mat_rows:first, :128].reshape(D, 128)
    vec = vec_low.astype(F32)
    we1 = vec_low[:, BASE + 4 : BASE + 4 + F_IN]
    whd = vec_low[:, BASE + 4 + F_IN : BASE + 4 + F_IN + F_OUT]
    small = (
        whole[:, first : first + LAYERS, :width].transpose(1, 0, 2).reshape(LAYERS, DH, S + 3 * DH)
    )

    slot = mesh_slot[None]
    big = jnp.where(lax.axis_index("pts") == 0, mesh_slot[points - 1], mesh_slot[0])
    ids = jnp.arange(MESH_GRP)
    blocks = points // SUB
    member = jnp.any(mesh_slot.reshape(blocks, SUB)[:, :, None] == ids, 1)
    order = jnp.arange(blocks)[:, None]
    starts = jnp.min(jnp.where(member, order, blocks), 0)
    ends = jnp.max(jnp.where(member, order + 1, 0), 0)
    local = jnp.any(member, 0) & (ids != big)
    info = jnp.concatenate([big[None], local.astype(I32), starts, ends]).astype(I32)

    wide = (D, points)
    tall = (HS, points)

    def exchange(value):
        return [value] + [swap(value, "pts", k) for k in range(1, npts)]

    held = {}

    def hold(**values):
        held.update(values)

    acc = ((D + 16, HS), F32)
    share = [((D, HS), BF), ((S, HS), F32), ((DH, HS), BF), ((3 * DH, HS), BF), ((ND_ROWS, HS), F32)]
    acts = [(wide, BF), (wide, BF), (tall, F32)]
    nears = [(wide, F32), (tall, BF), ((MESH_GRP, ND_ROWS, HS), F32), ((ND_ROWS, HS), BF)]
    few_out = [((MESH_GRP, D, HS), BF), ((MESH_GRP, S, HS), F32),
               ((MESH_GRP, DH, HS), BF), ((MESH_GRP, 3 * DH, HS), BF)]

    def small_call(nd, layer):
        routed, *rest = call(
            functools.partial(small_kernel, layer), "small_fwd", info, (nd, small),
            few_out[:1], few_out[1:], None, few_out, 4 * MESH_GRP,
        )
        return routed, rest

    h0, w0, nd0, send, *acts0 = call(
        embed_kernel, "embed", info, (features, slot, vec, we1, mats, small),
        nears, [acc] + acts, None, [(wide, F32)] + acts, 4,
    )
    parts = exchange(send)
    routed, few0 = small_call(nd0, 0)
    h1, w1, nd1, send, *rest = call(
        functools.partial(middle_kernel, npts), "middle", info,
        (*parts, routed, w0, h0, slot, vec, mats, small),
        nears, share + [(wide, BF), (wide, F32)] + acts + [(wide, F32), acc], None,
        share + [(wide, BF), (wide, F32), (wide, F32)] + acts, 11,
    )
    share0, (y0, m0, *acts1) = rest[:5], rest[5:]

    parts = exchange(send)
    routed, few1 = small_call(nd1, 1)
    y1, m1, h2, diff, loss_part, *share1 = call(
        functools.partial(head_kernel, npts), "head", info,
        (*parts, routed, w1, h1, slot, targets, vec, mats, whd, small),
        [(wide, BF), (wide, F32), (wide, F32), ((F_OUT, points), F32), ((8, 128), F32)],
        share + [(wide, F32)], None, share, 5,
    )
    hold(y1=y1, m1=m1)

    keeps = [(wide, BF), (wide, F32)]
    ds_out = [((MESH_GRP, DH, HS), BF), ((DH, HS), BF)]
    parts = exchange(loss_part)
    grad2, rel, grads = call(
        functools.partial(loss_kernel, npts, groups), "loss", info,
        (*parts, diff, slot, h2, vec, whd),
        [(wide, F32), ((8, 128), F32), ((devices, 12 * cols, D), F32)], [], held,
    )
    hold(grads=grads)

    def half_call(layer, grad, middle, probs, y_low):
        res = call(
            functools.partial(half_kernel, layer), "half", info,
            (grad, middle, probs, y_low, slot, vec, mats, "grads"), ds_out + keeps, [((D, HS), F32)], held,
        )
        return res[0], res[1], res[2:]

    def small_back(layer, ds, nd, few):
        return call(
            functools.partial(small_back_kernel, layer), "small_bwd", info,
            (ds, nd, few[1], few[2], few[3], few[0], small),
            [((MESH_GRP, HS, HS), BF), ((MESH_GRP, D, HS), BF),
             ((MESH_GRP, HS, 128), F32), ((DH, 3 * DH), F32)],
        )

    tail_scratch = [(tall, F32), (wide, F32)]
    tail_out = [((DH, 3 * DH), F32), ((DH, HS), F32)]

    def tail_ins(parts, back, keep, share, acts):
        return (*parts, *back, share[4], share[1], share[2], share[3], share[0], small, *acts, *keep, slot, vec, mats)

    ds, send, keep = half_call(1, grad2, held.pop("m1"), acts1[3], held.pop("y1"))
    parts = exchange(send)
    back = small_back(1, ds, nd1, few1)
    grad1, dw1, slope1 = call(
        functools.partial(tail_kernel, npts, 1), "tail", info,
        (*tail_ins(parts, back, keep, share1, acts1), "grads"), [(wide, F32)] + tail_out, tail_scratch, held,
    )
    hold(dw1=dw1, slope1=slope1)
    ds, send, keep = half_call(0, grad1, m0, acts0[3], y0)
    parts = exchange(send)
    back = small_back(0, ds, nd0, few0)
    dw0, slope0 = call(
        functools.partial(end_kernel, npts), "end", info,
        (*tail_ins(parts, back, keep, share0, acts0), features, we1, "grads"), tail_out, tail_scratch, held,
    )

    def small_grad(slope, mixed):
        return jnp.concatenate([slope.reshape(DH, H, S).sum(1), mixed], 1).reshape(devices, width)

    few = jnp.pad(
        jnp.stack([small_grad(slope0, dw0), small_grad(held["slope1"], held["dw1"])], 1),
        ((0, 0), (0, few_rows - LAYERS), (0, D - width)),
    )
    odd = (lax.axis_index("mesh") & 1)[None].astype(I32)
    halves = (groups // 2, 2, npts)
    total_rows = 12 * cols + few_rows
    keep, send = call(
        split_kernel, "split", odd,
        (held["grads"].reshape(halves + (12 * cols, D)), few.reshape(halves + (few_rows, D))),
        [((groups // 2, npts, total_rows, D), F32)] * 2,
    )
    own = scatter_sum(keep, send)
    first = 12 * cols
    red_mats = own[:mat_rows].reshape(count_mats, cols, D).transpose(0, 2, 1)
    red_vecs = own[mat_rows:first, :count_vecs].T
    red_small = own[first : first + LAYERS, :width]
    squares = (
        jnp.sum(red_mats * red_mats) + jnp.sum(red_small * red_small) + jnp.sum(red_vecs * red_vecs)
    )
    group_loss = jnp.sum(rel[:MESH_GRP, 0]) / (MESH_GRP * devices)
    totals = all_sum(jnp.stack([squares, group_loss]))
    grad_norm = jnp.sqrt(totals[0])
    factor = jnp.minimum(1.0, CLIP / grad_norm)
    mat_out = adamw(matrices, matrices_moment, matrices_second, red_mats, factor)
    small_out = adamw(smalls, smalls_moment, smalls_second, red_small, factor)
    vec_out = adamw(vectors, vectors_moment, vectors_second, red_vecs, factor)
    return (totals[1], grad_norm) + mat_out + small_out + vec_out


def solution(mesh):
    both = ("mesh", "pts")
    cube, flat = P(None, None, both), P(None, both)
    return jax.shard_map(
        per_device,
        mesh=mesh,
        in_specs=(flat, flat, P(both), cube, cube, cube, flat, flat, flat, flat, flat, flat),
        out_specs=(P(), P(), cube, cube, cube, flat, flat, flat, flat, flat, flat),
        check_vma=False,
    )
```

```python
import functools
import jax
import jax.numpy as jnp
from jax import lax
from jax.experimental import pallas as pl
from jax.experimental.pallas import tpu as pltpu
from jax.sharding import PartitionSpec as P

D = 256
H = 8
DH = 32
S = 64
HS = H * S
F_IN = 7
F_OUT = 4
LAYERS = 2
MESH_GRP = 4
STEP = 5
LOCALS = MESH_GRP - 1
WINDOW = 640
ND_ROWS = 40


EPS_NORM = 1e-05
EPS_SLICE = 1e-05
EPS_LOSS = 1e-06
CLIP = 0.01
LEARN = 0.03
BETA_ONE = 0.9
BETA_TWO = 0.95
EPS_ADAM = 1e-08
DECAY = 0.1
BF = jnp.bfloat16
F32 = jnp.float32
I32 = jnp.int32
ALL = ("mesh", "pts")
BASE = 9 * LAYERS


def dot(left, right):
    return jnp.dot(left, right, preferred_element_type=F32)


def dot_nt(left, right):
    return lax.dot_general(left, right, (((1,), (1,)), ((), ())), preferred_element_type=F32)


def dot_tn(left, right):
    return lax.dot_general(left, right, (((0,), (0,)), ((), ())), preferred_element_type=F32)


def low(value):
    return value.astype(BF)


def block_mask():
    rows = lax.broadcasted_iota(I32, (D, HS), 0) // DH
    cols = lax.broadcasted_iota(I32, (D, HS), 1) // S
    return rows == cols


def spread_blocks(compact):
    tall = jnp.concatenate([compact] * H, 0)
    return jnp.where(block_mask(), tall, jnp.zeros_like(tall))


def fold_blocks(full):
    lanes = lax.broadcasted_iota(I32, (DH, HS), 1) // S
    total = jnp.zeros((DH, HS), F32)
    for head in range(H):
        total = jnp.where(lanes == head, full[head * DH : (head + 1) * DH], total)
    return total


def pick_matrix():
    rows = lax.broadcasted_iota(I32, (S, HS), 0)
    cols = lax.broadcasted_iota(I32, (S, HS), 1) % S
    return (rows == cols).astype(F32).astype(BF)


def norm_stats(hidden):
    row_mean = jnp.sum(hidden, 0, keepdims=True) * (1.0 / D)
    centred = hidden - row_mean
    row_var = jnp.sum(centred * centred, 0, keepdims=True) * (1.0 / D)
    return centred, lax.rsqrt(row_var + EPS_NORM)


def norm_apply(hidden, gain, shift):
    centred, scale = norm_stats(hidden)
    return low(centred * scale * gain + shift)


def norm_back(grad, unit, scale, gain):
    inner = grad * gain
    first = jnp.sum(inner, 0, keepdims=True) * (1.0 / D)
    second = jnp.sum(inner * unit, 0, keepdims=True) * (1.0 / D)
    return scale * (inner - first - unit * second)


ROOT = 0.7978845608028654
CUBIC = 0.044715


def gelu(value):
    return 0.5 * value * (1.0 + jnp.tanh(ROOT * (value + CUBIC * (value * value * value))))


def gelu_both(value):
    square = value * value
    bend = jnp.tanh(ROOT * (value + CUBIC * (square * value)))
    half = 0.5 * (1.0 + bend)
    slope = half + 0.5 * value * (1.0 - bend * bend) * (ROOT * (1.0 + 3.0 * CUBIC * square))
    return value * half, slope


def lane_fold(value):
    total = value[:, :128]
    for start in range(128, value.shape[1], 128):
        total = total + value[:, start : start + 128]
    return total


def columns(sums):
    lanes = lax.broadcasted_iota(I32, (D, 128), 1)
    total = jnp.zeros((D, 128), F32)
    for index, value in sums:
        total = jnp.where(lanes == index, jnp.sum(value, 1, keepdims=True), total)
    return total


def slice_matrix(small):
    wide = jnp.concatenate([small[:, :S], small[:, :S]], 1)
    return spread_blocks(jnp.concatenate([wide] * (HS // (2 * S)), 1))


def slice_forward(num_dens, small):
    pick, mask = pick_matrix(), block_mask()
    tokens = [low(nd[:DH] / (nd[DH : DH + 1] + EPS_SLICE)) for nd in num_dens]
    mixed = [low(dot_tn(small[:, S:], t)) for t in tokens]
    keys = [low(dot_nt(pick, spread_blocks(m[DH : 2 * DH]))) for m in mixed]
    values = [low(dot_nt(spread_blocks(m[2 * DH :]), pick)) for m in mixed]
    scores = [dot(k, spread_blocks(m[:DH])) * DH ** (-0.5) for k, m in zip(keys, mixed)]
    raised = [jnp.exp(s - jnp.max(s, 0, keepdims=True)) for s in scores]
    attn = [r * (1.0 / jnp.sum(r, 0, keepdims=True)) for r in raised]
    full = [dot(v, low(a)) for v, a in zip(values, attn)]
    routed = [low(jnp.where(mask, f, jnp.zeros_like(f))) for f in full]
    return list(zip(routed, attn, tokens, mixed))


def widen(tall):
    pair = jnp.concatenate([tall, tall], 1)
    return fold_blocks(jnp.concatenate([pair] * (HS // (2 * S)), 1))


def slice_backward(d_slices, num_dens, attns, tokens, mixed, small):
    pick = pick_matrix()
    scale = DH ** (-0.5)
    lows = [low(a) for a in attns]
    d_full = [spread_blocks(d) for d in d_slices]
    query_full = [spread_blocks(m[:DH]) for m in mixed]
    values = [low(dot_nt(pick, spread_blocks(m[2 * DH :]))) for m in mixed]
    keys = [low(dot_nt(spread_blocks(m[DH : 2 * DH]), pick)) for m in mixed]
    d_attn = [dot(v, d) for v, d in zip(values, d_full)]
    d_values = [low(widen(dot_nt(d, a))) for d, a in zip(d_full, lows)]
    d_scores = [low(a * (d - jnp.sum(d * a, 0, keepdims=True))) for a, d in zip(attns, d_attn)]
    d_queries = [low(fold_blocks(dot(k, d)) * scale) for k, d in zip(keys, d_scores)]
    d_keys = [low(widen(dot_nt(q, d)) * scale) for q, d in zip(query_full, d_scores)]
    d_mixed = [jnp.concatenate(group, 0) for group in zip(d_queries, d_keys, d_values)]
    d_tokens = [dot(small[:, S:], d) for d in d_mixed]
    d_weight = [dot_nt(t, d) for t, d in zip(tokens, d_mixed)]
    inverse = [1.0 / (nd[DH : DH + 1] + EPS_SLICE) for nd in num_dens]
    d_num = [spread_blocks(low(d * i)) for d, i in zip(d_tokens, inverse)]
    d_den = [
        -jnp.sum(d * nd[:DH], 0, keepdims=True) * i * i for d, nd, i in zip(d_tokens, num_dens, inverse)
    ]
    return list(zip(d_num, d_den, d_weight))


def is_mesh(slot, mesh_id):
    return (slot == mesh_id).astype(F32)


def columns_at(vec, index):
    return vec[:, index : index + 1]


def sum_parts(parts):
    terms = [part[...].astype(F32) for part in parts]
    while len(terms) > 1:
        terms = [terms[i] + terms[i + 1] for i in range(0, len(terms), 2)]
    return terms[0]


def window(info, place, index, width):
    start = info[5 + place] + index * WINDOW
    at = pl.multiple_of(jnp.minimum(start, width - WINDOW), 128)
    return start, pl.ds(at, WINDOW)


def inside_of(info, place, slot, start, part):
    lanes = lax.broadcasted_iota(I32, (1, WINDOW), 1) + part.start
    mesh_id = info[2 + place]
    first = jnp.where(start == info[5 + place], 0, start)
    return ((slot[:, part] == mesh_id) & (lanes >= first)).astype(F32)


def each_window(info, slot, value, store):
    width = slot.shape[1]

    @pl.when(info[1] != 0)
    def _():
        found = []
        for place in range(LOCALS):
            start, part = window(info, place, 0, width)
            found.append((part, value(place, part, inside_of(info, place, slot, start, part))))
        for place, (part, result) in enumerate(found):
            store(place, part, result)
        for place in range(LOCALS):

            def step(index, carry):
                start, part = window(info, place, index, width)
                store(place, part, value(place, part, inside_of(info, place, slot, start, part)))
                return carry

            lax.fori_loop(1, info[8 + place], step, 0)


def any_local(info, visit):
    @pl.when(info[1] != 0)
    def _():
        visit()


LATE = (0, 1, 5 * LAYERS)
EARLY = tuple(m for m in range(5 * LAYERS + 1) if m not in LATE)
SMALL_AT = 64
UNIT = 40


def put(early_ref, late_ref, matrix, value):
    ref, row = (late_ref, LATE.index(matrix)) if matrix in LATE else (early_ref, EARLY.index(matrix))
    devices, cols = ref.shape[0], D // ref.shape[0]
    ref[:, row * cols : (row + 1) * cols, :] = value.reshape(devices, cols, D)


def put_columns(late_ref, sums, fresh=False):
    devices, cols = late_ref.shape[0], D // late_ref.shape[0]
    value = columns(sums).reshape(devices, cols, 128)
    if not fresh:
        value = value + late_ref[:, len(LATE) * cols :, :128]
    late_ref[:, len(LATE) * cols :, :128] = value


def small_grad(slope, mixed):
    total = slope[:, :S]
    for head in range(1, H):
        total = total + slope[:, head * S : (head + 1) * S]
    return jnp.concatenate([total, mixed], 1)


def small_units(width, rows):
    step = min(width, UNIT)
    for k in range(LAYERS * width // step):
        yield k * step // width, k * step % width, k * step // UNIT, k * step % UNIT, step


def start_copies(sources, targets, sems, first):
    copies = [
        pltpu.make_async_copy(a, b, sems.at[first + j]) for j, (a, b) in enumerate(zip(sources, targets))
    ]
    for copy in copies:
        copy.start()
    return copies


def finish_copies(copies):
    for copy in copies:
        copy.wait()


def front(hidden, vec, layer, mats, small, slot, info, w_ref, nd_ref, send_ref, stage, far, sems):
    x_ref, f_ref, probs_ref = stage
    base = 9 * layer
    width = hidden.shape[1]
    u = norm_apply(hidden, columns_at(vec, base), columns_at(vec, base + 1))
    pair = dot(mats[5 * layer : 5 * layer + 2].reshape(2 * D, D), u)
    x_low = low(pair[:D] + columns_at(vec, base + 2))
    f_low = low(pair[D:] + columns_at(vec, base + 3))
    x_ref[...] = x_low
    f_ref[...] = f_low
    copies = start_copies(stage[:2], far[:2], sems, 0)
    logits = dot(slice_matrix(small[layer]).T, x_low).reshape(H, S, width)
    raised = jnp.exp(logits - jnp.max(logits, 1, keepdims=True))
    valid = (slot[...] < MESH_GRP).astype(F32)
    probs = (raised * (valid[None] / jnp.sum(raised, 1, keepdims=True))).reshape(HS, width)
    probs_ref[...] = probs
    copies = copies + start_copies(stage[2:], far[2:], sems, 2)
    w_low = low(probs)
    w_ref[...] = w_low

    def rows_of(features, mine):
        ones = jnp.broadcast_to(mine, (16, mine.shape[1]))
        return jnp.concatenate([low(features.astype(F32) * mine), low(ones)], 0)

    def compact(full):
        return jnp.concatenate([fold_blocks(full[:D]), full[D : D + ND_ROWS - DH]], 0)

    send_ref[...] = low(compact(dot_nt(rows_of(f_low, is_mesh(slot[...], info[0])), w_low)))

    nd_ref[...] = jnp.zeros_like(nd_ref)

    def value(place, part, mask):
        return compact(dot_nt(rows_of(f_ref[:, part], mask), w_ref[:, part]))

    def store(place, part, result):
        nd_ref[place] = nd_ref[place] + result

    each_window(info, slot, value, store)
    return copies


def back_half(w_in, slot, info, routed, routed_big, mix, hidden, vec, layer, mats):
    base = 9 * layer
    mix[...] = dot(routed_big[...], w_in[...]) * is_mesh(slot[...], info[0])

    def value(place, part, mask):
        return dot(routed[place], w_in[:, part]) * mask

    def store(place, part, result):
        mix[:, part] = mix[:, part] + result

    each_window(info, slot, value, store)
    y_low = low(mix[...])
    middle = hidden + dot(mats[5 * layer + 2], y_low) + columns_at(vec, base + 4)
    u2 = norm_apply(middle, columns_at(vec, base + 5), columns_at(vec, base + 6))
    pre = dot(mats[5 * layer + 3], u2) + columns_at(vec, base + 7)
    out = middle + dot(mats[5 * layer + 4], low(gelu(pre))) + columns_at(vec, base + 8)
    return y_low, middle, out


def head_half(grad, vec, layer, mats, middle, probs, y_low, slot, info, early_ref, late_ref, ds_ref, send_ref, acc, keep):
    base = 9 * layer
    grad_low = low(grad)
    centred, scale = norm_stats(middle)
    unit = centred * scale
    gain = columns_at(vec, base + 5)
    u2 = low(unit * gain + columns_at(vec, base + 6))
    activ, slope = gelu_both(dot(mats[5 * layer + 3], u2) + columns_at(vec, base + 7))
    d_pre = dot_tn(mats[5 * layer + 4], grad_low) * slope
    d_pre_low = low(d_pre)
    d_norm = dot_tn(mats[5 * layer + 3], d_pre_low)
    d_mid = norm_back(d_norm, unit, scale, gain) + grad
    d_mid_low = low(d_mid)
    d_y = low(dot_tn(mats[5 * layer + 2], d_mid_low))
    d_y_ref, d_mid_ref = keep
    d_y_ref[...] = d_y
    d_mid_ref[...] = d_mid
    put(early_ref, late_ref, 5 * layer + 4, dot_nt(grad_low, low(activ)))
    put(early_ref, late_ref, 5 * layer + 3, dot_nt(d_pre_low, u2))
    put(early_ref, late_ref, 5 * layer + 2, dot_nt(d_mid_low, y_low))
    own = low(d_y.astype(F32) * is_mesh(slot[...], info[0]))
    send_ref[...] = low(fold_blocks(dot_nt(own, low(probs[...]))))

    acc[...] = jnp.zeros_like(acc)

    def value(place, part, mask):
        mine = low(d_y_ref[:, part].astype(F32) * mask)
        return fold_blocks(dot_nt(mine, low(probs[:, part])))

    def store(place, part, result):
        acc[place] = acc[place] + result

    each_window(info, slot, value, store)
    ds_ref[...] = low(acc[...])
    return [(base + 4, lane_fold(d_mid)), (base + 5, lane_fold(d_norm * unit)),
            (base + 6, lane_fold(d_norm)), (base + 7, lane_fold(d_pre)), (base + 8, lane_fold(grad))]


def tail_half(vec, layer, mats, small, hidden, x_in, f_in, probs_in, d_y, d_mid, slot, info,
              back, back_big, route, mix, early_ref, late_ref):
    width = hidden.shape[1]
    base = 9 * layer
    both_big, num_big, den_big = back_big
    both, d_num, d_den = back
    mine = is_mesh(slot[...], info[0])
    pair = jnp.concatenate([d_y[...], f_in[...]], 0)
    route[...] = (dot(both_big, pair) + den_big) * mine
    mix[...] = dot(num_big, low(probs_in[...])) * mine

    def value(place, part, mask):
        piece = jnp.concatenate([d_y[:, part], f_in[:, part]], 0)
        through = (dot(both[place], piece) + d_den[place][:, :1]) * mask
        return through, dot(d_num[place], low(probs_in[:, part])) * mask

    def store(place, part, result):
        route[:, part] = route[:, part] + result[0]
        mix[:, part] = mix[:, part] + result[1]

    each_window(info, slot, value, store)
    d_probs = route[...].reshape(H, S, width)
    probs = probs_in[...].reshape(H, S, width)
    spread = jnp.sum(d_probs * probs, 1, keepdims=True)
    d_logits = low(probs * (d_probs - spread)).reshape(HS, width)
    d_x = dot(slice_matrix(small[layer]), d_logits)
    d_f = mix[...]
    slope = fold_blocks(dot_nt(x_in[...], d_logits))
    d_pair = jnp.concatenate([low(d_x), low(d_f)], 0)
    d_norm = dot_tn(mats[5 * layer : 5 * layer + 2].reshape(2 * D, D), d_pair)
    centred, scale = norm_stats(hidden)
    unit = centred * scale
    gain = columns_at(vec, base)
    u = low(unit * gain + columns_at(vec, base + 1))
    grads = dot_nt(d_pair, u)
    put(early_ref, late_ref, 5 * layer, grads[:D])
    put(early_ref, late_ref, 5 * layer + 1, grads[D:])
    sums = [(base, lane_fold(d_norm * unit)), (base + 1, lane_fold(d_norm)),
            (base + 2, lane_fold(d_x)), (base + 3, lane_fold(d_f))]
    return norm_back(d_norm, unit, scale, gain) + d_mid[...], sums, slope


def embed_kernel(info, feat, slot, vec, mats, small,
                 h_ref, w_ref, nd_ref, send_ref, h_far, x_far, f_far, probs_far,
                 x_ref, f_ref, probs_ref, sems):
    we1 = low(vec[:, BASE + 4 : BASE + 4 + F_IN])
    e1 = dot(we1, low(feat[...])) + columns_at(vec, BASE)
    hidden = dot(mats[5 * LAYERS], low(gelu(e1))) + columns_at(vec, BASE + 1)
    h_ref[...] = hidden
    copies = start_copies([h_ref], [h_far], sems, 3)
    copies = copies + front(hidden, vec, 0, mats, small, slot, info, w_ref, nd_ref, send_ref,
                            (x_ref, f_ref, probs_ref), (x_far, f_far, probs_far), sems)
    finish_copies(copies)


def small_kernel(layer, info, nd_ref, small, routed_ref, routed_far, attn_far, tokens_far, mixed_far,
                 attn_ref, tokens_ref, mixed_ref, sems):
    stage = (routed_ref, attn_ref, tokens_ref, mixed_ref)
    far = (routed_far, attn_far, tokens_far, mixed_far)

    def visit():
        results = slice_forward([nd_ref[place] for place in range(LOCALS)], small[layer])
        for place in range(LOCALS):
            for ref, value in zip(stage, results[place]):
                ref[place] = value
        finish_copies(start_copies(stage, far, sems, 0))

    any_local(info, visit)


def share_start(parts, small, stage, far, sems, first):
    total = sum_parts(parts)
    for ref, value in zip(stage, slice_forward([total], small)[0] + (total,)):
        ref[...] = value
    return start_copies(stage, far, sems, first)


def middle_kernel(npts, info, *refs):
    parts, refs = refs[:npts], refs[npts:]
    (routed, w_in, h_in, slot, vec, mats, small,
     h_ref, w_ref, nd_ref, send_ref, *refs) = refs
    share_far, (y_far, m_far, h_far, x_far, f_far, probs_far), refs = refs[:5], refs[5:11], refs[11:]
    share, (y_ref, m_ref, x_ref, f_ref, probs_ref, mix, sems) = refs[:5], refs[5:]
    copies = share_start(parts, small[0], share, share_far, sems, 6)
    y_low, middle, out = back_half(w_in, slot, info, routed, share[0], mix, h_in[...], vec, 0, mats)
    y_ref[...] = y_low
    m_ref[...] = middle
    h_ref[...] = out
    copies = copies + start_copies((h_ref, y_ref, m_ref), (h_far, y_far, m_far), sems, 3)
    copies = copies + front(out, vec, 1, mats, small, slot, info, w_ref, nd_ref, send_ref,
                            (x_ref, f_ref, probs_ref), (x_far, f_far, probs_far), sems)
    finish_copies(copies)


def head_kernel(npts, info, *refs):
    parts, refs = refs[:npts], refs[npts:]
    (routed, w_in, h_in, slot, target, vec, mats, small,
     y_ref, m_ref, h_ref, diff_ref, loss_ref, *refs) = refs
    share_far, share, (mix, sems) = refs[:5], refs[5:10], refs[10:]
    copies = share_start(parts, small[1], share, share_far, sems, 0)
    y_low, middle, out = back_half(w_in, slot, info, routed, share[0], mix, h_in[...], vec, 1, mats)
    y_ref[...] = y_low
    m_ref[...] = middle
    h_ref[...] = out
    uh = norm_apply(out, columns_at(vec, BASE + 2), columns_at(vec, BASE + 3))
    truth = target[...]
    whd = low(vec[:, BASE + 4 + F_IN : BASE + 4 + F_IN + F_OUT])
    differ = dot_tn(whd, uh) - truth
    diff_ref[...] = differ
    ids = lax.broadcasted_iota(I32, differ.shape, 0)
    member = (ids == slot[...]).astype(F32)
    squares = jnp.sum(differ * differ, 0, keepdims=True)
    sizes = jnp.sum(truth * truth, 0, keepdims=True)
    both = lane_fold(jnp.concatenate([member * squares, member * sizes], 0))
    loss_ref[...] = jnp.broadcast_to(jnp.sum(both, 1, keepdims=True), loss_ref.shape)
    finish_copies(copies)


def loss_kernel(npts, groups, info, *refs):
    parts, refs = refs[:npts], refs[npts:]
    diff, slot, h_in, vec, grad_ref, rel_ref, early_ref, late_ref = refs
    whd = low(vec[:, BASE + 4 + F_IN : BASE + 4 + F_IN + F_OUT])
    total = sum_parts(parts)
    err_root = jnp.sqrt(total[:MESH_GRP] + EPS_LOSS)
    tgt_root = jnp.sqrt(total[MESH_GRP:] + EPS_LOSS)
    rel_ref[...] = jnp.concatenate([err_root / tgt_root, jnp.zeros_like(err_root)], 0)
    coef = (1.0 / (err_root * tgt_root) * (1.0 / (MESH_GRP * groups)))[:, :1]
    ids = lax.broadcasted_iota(I32, diff.shape, 0)
    member = (ids == slot[...]).astype(F32)
    d_pred = low(diff[...] * jnp.sum(member * coef, 0, keepdims=True))
    d_head = dot(whd, d_pred)
    centred, scale = norm_stats(h_in[...])
    unit = centred * scale
    gain = columns_at(vec, BASE + 2)
    g_whd = dot_nt(low(unit * gain + columns_at(vec, BASE + 3)), d_pred)
    put_columns(late_ref, [(BASE + 2, lane_fold(d_head * unit)), (BASE + 3, lane_fold(d_head))]
                + [(BASE + 4 + F_IN + j, g_whd[:, j : j + 1]) for j in range(F_OUT)], True)
    grad_ref[...] = norm_back(d_head, unit, scale, gain)


def half_kernel(layer, info, grad, middle, probs, y_low, slot, vec, mats, early_ref, late_ref,
                ds_ref, send_ref, d_y_ref, d_mid_ref, acc):
    sums = head_half(grad[...], vec, layer, mats, middle[...], probs, y_low[...], slot, info, early_ref, late_ref,
                     ds_ref, send_ref, acc, (d_y_ref, d_mid_ref))
    put_columns(late_ref, sums)


def small_back_kernel(layer, info, ds_in, nd_ref, attn, tokens, mixed, routed, small,
                      both_ref, dn_ref, den_ref, dw_ref):
    dw_ref[...] = jnp.zeros_like(dw_ref)

    def visit():
        tables = [[ref[place] for place in range(LOCALS)] for ref in (ds_in, nd_ref, attn, tokens, mixed)]
        results = slice_backward(*tables, small[layer])
        for place, (dn, den, dw) in enumerate(results):
            both_ref[place] = jnp.concatenate([routed[place], dn], 0).T
            dn_ref[place] = dn
            den_ref[place] = jnp.broadcast_to(den, (128, HS)).T
        dw_ref[...] = results[0][2] + results[1][2] + results[2][2]

    any_local(info, visit)


def tail_start(npts, parts, small, ndb, attn, tokens, mixed, routed_big, dw_in):
    total = low(sum_parts(parts))
    ((d_num, d_den, d_weight),) = slice_backward(
        *[[value] for value in (total, ndb[...], attn[...], tokens[...], mixed[...])], small
    )
    d_weight = dw_in[...] + d_weight * (1.0 / npts)
    both = jnp.concatenate([routed_big[...], d_num], 0).T
    return (both, d_num, jnp.broadcast_to(d_den, (128, HS)).T[:, :1]), d_weight


def tail_kernel(npts, layer, info, *refs):
    parts, refs = refs[:npts], refs[npts:]
    (both_in, dn_in, den_in, dw_in, ndb, attn, tokens, mixed, routed_big, small,
     h_in, x_in, f_in, probs, d_y, d_mid, slot, vec, mats, early_ref, late_ref,
     grad_ref, small_ref, route, mix) = refs
    back_big, d_weight = tail_start(npts, parts, small[layer], ndb, attn, tokens, mixed, routed_big, dw_in)
    grad, sums, slope = tail_half(vec, layer, mats, small, h_in[...], x_in, f_in, probs, d_y, d_mid, slot, info,
                                  (both_in, dn_in, den_in), back_big, route, mix, early_ref, late_ref)
    grad_ref[...] = grad
    small_ref[...] = small_grad(slope, d_weight)
    put_columns(late_ref, sums)


def end_kernel(npts, info, *refs):
    parts, refs = refs[:npts], refs[npts:]
    (both_in, dn_in, den_in, dw_in, ndb, attn, tokens, mixed, routed_big, small,
     h_in, x_in, f_in, probs, d_y, d_mid, slot, vec, mats, feat, small_in, late_ref,
     small_ref, route, mix) = refs
    back_big, d_weight = tail_start(npts, parts, small[0], ndb, attn, tokens, mixed, routed_big, dw_in)
    grad, sums, slope = tail_half(vec, 0, mats, small, h_in[...], x_in, f_in, probs, d_y, d_mid, slot, info,
                                  (both_in, dn_in, den_in), back_big, route, mix, None, late_ref)
    feat_low = low(feat[...])
    we1 = low(vec[:, BASE + 4 : BASE + 4 + F_IN])
    activ, slope_in = gelu_both(dot(we1, feat_low) + columns_at(vec, BASE))
    grad_low = low(grad)
    d_embed = dot_tn(mats[5 * LAYERS], grad_low) * slope_in
    put(None, late_ref, 5 * LAYERS, dot_nt(grad_low, low(activ)))
    g_we1 = dot_nt(low(d_embed), feat_low)
    put_columns(late_ref, sums + [(BASE, lane_fold(d_embed)), (BASE + 1, lane_fold(grad))]
                + [(BASE + 4 + j, g_we1[:, j : j + 1]) for j in range(F_IN)])
    small_ref[0] = small_grad(slope, d_weight)
    small_ref[1] = small_in[...]
    cols = D // late_ref.shape[0]
    if cols * UNIT == 2 * (S + 3 * DH):
        for layer, column, row, lane, step in small_units(cols * UNIT // LAYERS, cols):
            late_ref[:, len(LATE) * cols + row, SMALL_AT + lane : SMALL_AT + lane + step] = (
                small_ref[layer, :, column : column + step]
            )


def pack_kernel(place, slot, mats, vecs, smalls, block_ref, info_ref):
    count, cols, _ = mats.shape
    points = slot.shape[1]
    block_ref[: count * cols] = low(mats[...].reshape(count * cols, D))
    block_ref[count * cols :] = jnp.zeros((cols, D), BF)
    block_ref[count * cols :, : vecs.shape[1]] = low(vecs[...])
    for layer, column, row, lane, step in small_units(smalls.shape[1], cols):
        block_ref[count * cols + row : count * cols + row + 1, SMALL_AT + lane : SMALL_AT + lane + step] = low(
            smalls[layer : layer + 1, column : column + step]
        )
    lanes = lax.broadcasted_iota(I32, (1, points), 1).astype(F32)
    ids = slot[...]
    edge = jnp.where(place[0] == 0, points - 1, 0).astype(F32)
    big = jnp.sum(jnp.where(lanes == edge, ids.astype(F32), 0.0)).astype(I32)
    info_ref[0] = big
    total = 0
    for j in range(LOCALS):
        mesh_id = j + jnp.where(big <= j, 1, 0)
        mine = ids == mesh_id
        first = jnp.min(jnp.where(mine, lanes, float(points))).astype(I32)
        last = jnp.max(jnp.where(mine, lanes, -1.0)).astype(I32)
        start = jnp.minimum((first >> 7) << 7, points - WINDOW)
        count_j = jnp.where(last >= 0, lax.div(jnp.maximum(last - start, 0), WINDOW) + 1, 0)
        info_ref[2 + j] = jnp.where(last >= 0, mesh_id, -1)
        info_ref[5 + j] = start
        info_ref[8 + j] = count_j
        total = total + count_j
    info_ref[1] = total


def unpack_kernel(masks, place, *refs):
    pieces, (mats_ref, vecs_ref, *rest) = refs[: len(masks)], refs[len(masks) :]
    count, _, cols, _ = mats_ref.shape
    for mask, piece in zip(masks, pieces):
        for i in range(piece.shape[0]):
            for k in range(piece.shape[1]):
                at = (place[1] ^ (mask | (i << 1))) * piece.shape[1] + (place[0] ^ k)
                for m in range(count):
                    mats_ref[m, at] = piece[i, k, m * cols : (m + 1) * cols, :]
                vecs_ref[at] = piece[i, k, count * cols :, :].astype(F32)
    if rest:
        for layer, column, row, lane, step in small_units(cols * UNIT // LAYERS, cols):
            rest[0][layer, :, column : column + step] = low(vecs_ref[:, row, SMALL_AT + lane : SMALL_AT + lane + step])


def split_kernel(place, grads, send_ref):
    send_ref[...] = grads[:, 1 - (place[1] & 1)]


def fold_kernel(first, shift, place, *refs):
    terms, outs = refs
    index = (place[1] >> shift) & (len(outs) - 1)
    for k, out in enumerate(outs):
        total = None
        for j, term in enumerate(terms):
            value = term[index ^ k, :, place[1] & 1] if first and j == 0 else term[index ^ k]
            total = value if total is None else total + value
        out[...] = total


def join_kernel(counts, *refs):
    out, row = refs[-1], 0
    at = 0
    for count in counts:
        total = refs[at][...]
        for ref in refs[at + 1 : at + count]:
            total = total + ref[...]
        out[:, row : row + total.shape[1]] = total
        row, at = row + total.shape[1], at + count


def square_kernel(devices, parts, rel, own_ref, sums_ref):
    own = parts[0]
    for j in range(1, parts.shape[0]):
        own = own + parts[j]
    own_ref[...] = own
    rows = lax.broadcasted_iota(I32, own.shape, 0)
    lanes = lax.broadcasted_iota(I32, own.shape, 1)
    edge = own.shape[0] // 12 * 11
    used = (rows < edge) | (lanes < BASE + 4 + F_IN + F_OUT) | ((lanes >= SMALL_AT) & (lanes < SMALL_AT + UNIT))
    squares = jnp.sum(jnp.where(used, own * own, 0.0))
    loss = jnp.sum(rel[:MESH_GRP, :1]) * (1.0 / (MESH_GRP * devices))
    which = lax.broadcasted_iota(I32, sums_ref.shape, 1)
    sums_ref[...] = jnp.where(which == 0, squares, loss)


def adamw(weight, moment, second, grad, factor):
    clipped = grad * factor
    moment = BETA_ONE * moment + (1.0 - BETA_ONE) * clipped
    second = BETA_TWO * second + (1.0 - BETA_TWO) * clipped * clipped
    moment_hat = moment / (1.0 - BETA_ONE**STEP)
    second_hat = second / (1.0 - BETA_TWO**STEP)
    updated = weight - LEARN * (moment_hat / (jnp.sqrt(second_hat) + EPS_ADAM) + DECAY * weight)
    return (moment, second, updated)


def update_kernel(sums, own, *refs):
    mats, vecs, smalls, outs = refs[:3], refs[3:6], refs[6:9], refs[9:]
    totals = jnp.sum(sums[...], 0)
    norm = jnp.sqrt(totals[:1, :1])
    factor = jnp.minimum(1.0, CLIP / norm)
    outs[0][0] = totals[1, 0]
    outs[1][0] = norm[0, 0]
    count, cols, _ = mats[0].shape
    for m in range(count):
        row = EARLY.index(m) if m in EARLY else len(EARLY) + LATE.index(m)
        for out, value in zip(outs[2:5], adamw(*[r[m] for r in mats], own[row * cols : (row + 1) * cols], factor)):
            out[m] = value
    grad = own[count * cols :, : vecs[0].shape[1]]
    for out, value in zip(outs[8:11], adamw(*[r[...] for r in vecs], grad, factor)):
        out[...] = value
    for layer, column, row, lane, step in small_units(smalls[0].shape[1], cols):
        grad = own[count * cols + row : count * cols + row + 1, SMALL_AT + lane : SMALL_AT + lane + step]
        old = [r[layer : layer + 1, column : column + step] for r in smalls]
        for out, value in zip(outs[5:8], adamw(*old, grad, factor)):
            out[layer : layer + 1, column : column + step] = value


LIMITS = dict(embed=16, small_fwd=5, middle=22, head=10, loss=8, half=20, small_bwd=4, tail=28, end=28,
              pack=3, unpack=3, split=3, fold=3, join=3, square=3, update=4)
WORK = dict(end=10**10)


def call(kernel, name, info, ins, outs, scratch=(), held=None, far=(), sems=0, nest=False):
    near = len(outs)
    outs = list(outs) + list(far)
    held = {} if held is None else held
    names = list(held)
    plain = [a for a in ins if not isinstance(a, str)]
    inside = pl.BlockSpec(memory_space=pltpu.VMEM)
    table = [] if info is None else [info]
    first, second = len(table) + len(plain), len(table) + len(plain) + len(names)

    def body(*refs):
        rest = iter(refs[len(table) : first])
        kept = dict(zip(names, refs[first:second]))
        order = [kept[a] if isinstance(a, str) else next(rest) for a in ins]
        results = refs[second : second + len(outs)]
        after = refs[second + len(outs) + len(names) :]
        if nest:
            kernel(*refs[: len(table)], order, results)
        else:
            kernel(*refs[: len(table)], *order, *results, *after)

    res = pl.pallas_call(
        body,
        in_specs=[pl.BlockSpec(memory_space=pltpu.SMEM)] * len(table) + [inside] * (second - len(table)),
        out_specs=[
            pl.BlockSpec(memory_space=pltpu.SMEM) if len(shape) == 1 else inside for shape, _ in outs[:near]
        ]
        + [pl.BlockSpec(memory_space=pltpu.HBM)] * len(far)
        + [inside] * len(names),
        out_shape=[jax.ShapeDtypeStruct(s, t) for s, t in outs]
        + [jax.ShapeDtypeStruct(held[n].shape, held[n].dtype) for n in names],
        input_output_aliases={first + j: len(outs) + j for j in range(len(names))},
        scratch_shapes=[pltpu.VMEM(s, t) for s, t in scratch]
        + ([pltpu.SemaphoreType.DMA((sems,))] if sems else []),
        compiler_params=pltpu.CompilerParams(vmem_limit_bytes=LIMITS[name] * 2**20),
        cost_estimate=pl.CostEstimate(flops=WORK.get(name, 1000), bytes_accessed=1000, transcendentals=0),
        name=name,
    )(*table, *plain, *[held[n] for n in names])
    held.update(zip(names, res[len(outs) :]))
    return res[: len(outs)]


def swap(value, axis, mask):
    size = lax.axis_size(axis)
    return lax.ppermute(value, axis, [(i, i ^ mask) for i in range(size)])


def bit_groups(size):
    bits = size.bit_length() - 1
    groups, low = [], 1
    while low < bits:
        width = min(2, bits - low)
        groups.append((low, width))
        low += width
    return groups


def gather_pieces(block):
    held = jnp.stack([block] + [swap(block, "pts", k) for k in range(1, lax.axis_size("pts"))])[None]
    masks, pieces = [0], [held]
    for low, width in bit_groups(lax.axis_size("mesh")):
        held = jnp.concatenate(pieces)
        masks = [k << low for k in range(1 << width)]
        pieces = [held] + [swap(held, "mesh", m) for m in masks[1:]]
    return masks + [m | 1 for m in masks], pieces + [swap(p, "mesh", 1) for p in pieces]


def scatter_start(place, grads, later):
    mesh_size, pts_size = lax.axis_size("mesh"), lax.axis_size("pts")
    rows = grads.shape[1]
    grads = grads.reshape(mesh_size // 2, 2, pts_size, rows, D)
    (send,) = call(split_kernel, "split", place, (grads,), [((mesh_size // 2, pts_size, rows, D), F32)])
    terms = [grads, swap(send, "mesh", 1)]
    left = mesh_size // 2
    for number, (low, width) in enumerate(reversed(bit_groups(mesh_size))):
        count = 1 << width
        left //= count
        shape = (count, left, pts_size, rows, D)
        views = [t.reshape(shape) for t in terms[1:]]
        views = [terms[0].reshape((count, left, 2) + shape[2:] if number == 0 else shape)] + views
        pieces = call(
            functools.partial(fold_kernel, number == 0, low), "fold", place, views, [(shape[1:], F32)] * count,
            nest=True,
        )
        if number == 0:
            *pieces, later = lax.optimization_barrier((*pieces, later))
        terms = [pieces[0]] + [swap(p, "mesh", k << low) for k, p in enumerate(pieces) if k]
    return [t.reshape(pts_size, rows, D) for t in terms], later


def per_device(
    features,
    targets,
    mesh_slot,
    matrices,
    matrices_moment,
    matrices_second,
    smalls,
    smalls_moment,
    smalls_second,
    vectors,
    vectors_moment,
    vectors_second,
):
    groups, npts = lax.axis_size("mesh"), lax.axis_size("pts")
    devices = groups * npts
    cols, width = matrices.shape[2], smalls.shape[1]
    points = mesh_slot.shape[0]
    count_mats, count_vecs = matrices.shape[0], vectors.shape[0]
    slot = mesh_slot[None]
    place = jnp.stack([lax.axis_index("pts"), lax.axis_index("mesh")]).astype(I32)
    turned = [a.transpose(0, 2, 1) for a in (matrices, matrices_moment, matrices_second)]
    vecs = [a.T for a in (vectors, vectors_moment, vectors_second)]
    block, info = call(
        pack_kernel, "pack", place, (slot, turned[0], vecs[0], smalls), [((12 * cols, D), BF), ((16,), I32)]
    )
    masks, pieces = gather_pieces(block)
    direct = cols * UNIT == 2 * (S + 3 * DH)
    mats, vec, *rest = call(
        functools.partial(unpack_kernel, masks), "unpack", place, pieces,
        [((count_mats, devices, cols, D), BF), ((devices, cols, D), F32)]
        + ([((LAYERS, DH, S + 3 * DH), BF)] if direct else []),
    )
    if direct:
        small = rest[0]
    else:
        small = vec[:, :, SMALL_AT : SMALL_AT + UNIT].reshape(devices, LAYERS, width).astype(BF)
        small = small.transpose(1, 0, 2).reshape(LAYERS, DH, S + 3 * DH)
    mats = mats.reshape(count_mats, D, D)
    vec = vec.reshape(D, D)

    wide = (D, points)
    tall = (HS, points)

    def exchange(value):
        return [value] + [swap(value, "pts", k) for k in range(1, npts)]

    held = {}

    def hold(**values):
        held.update(values)

    share = [((D, HS), BF), ((S, HS), F32), ((DH, HS), BF), ((3 * DH, HS), BF), ((ND_ROWS, HS), F32)]
    acts = [(wide, BF), (wide, BF), (tall, F32)]
    nears = [(wide, F32), (tall, BF), ((LOCALS, ND_ROWS, HS), F32), ((ND_ROWS, HS), BF)]
    few_out = [((LOCALS, D, HS), BF), ((LOCALS, S, HS), F32),
               ((LOCALS, DH, HS), BF), ((LOCALS, 3 * DH, HS), BF)]

    def small_call(nd, layer):
        routed, *rest = call(
            functools.partial(small_kernel, layer), "small_fwd", info, (nd, small),
            few_out[:1], few_out[1:], None, few_out, 4,
        )
        return routed, rest

    h0, w0, nd0, send, *acts0 = call(
        embed_kernel, "embed", info, (features, slot, vec, mats, small),
        nears, acts, None, [(wide, F32)] + acts, 4,
    )
    parts = exchange(send)
    routed, few0 = small_call(nd0, 0)
    h1, w1, nd1, send, *rest = call(
        functools.partial(middle_kernel, npts), "middle", info,
        (*parts, routed, w0, h0, slot, vec, mats, small),
        nears, share + [(wide, BF), (wide, F32)] + acts + [(wide, F32)], None,
        share + [(wide, BF), (wide, F32), (wide, F32)] + acts, 11,
    )
    share0, (y0, m0, *acts1) = rest[:5], rest[5:]

    parts = exchange(send)
    routed, few1 = small_call(nd1, 1)
    y1, m1, h2, diff, loss_part, *share1 = call(
        functools.partial(head_kernel, npts), "head", info,
        (*parts, routed, w1, h1, slot, targets, vec, mats, small),
        [(wide, BF), (wide, F32), (wide, F32), ((F_OUT, points), F32), ((8, 128), F32)],
        share + [(wide, F32)], None, share, 5,
    )
    hold(y1=y1, m1=m1)

    keeps = [(wide, BF), (wide, F32)]
    ds_out = [((LOCALS, DH, HS), BF), ((DH, HS), BF)]
    parts = exchange(loss_part)
    grad2, rel, early, late = call(
        functools.partial(loss_kernel, npts, groups), "loss", info,
        (*parts, diff, slot, h2, vec),
        [(wide, F32), ((8, 128), F32), ((devices, len(EARLY) * cols, D), F32),
         ((devices, (len(LATE) + 1) * cols, D), F32)], [], held,
    )
    hold(rel=rel, early=early, late=late)

    def half_call(layer, grad, middle, probs, y_low):
        res = call(
            functools.partial(half_kernel, layer), "half", info,
            (grad, middle, probs, y_low, slot, vec, mats, "early", "late"), ds_out + keeps, [((LOCALS, DH, HS), F32)], held,
        )
        return res[0], res[1], res[2:]

    def small_back(layer, ds, nd, few):
        return call(
            functools.partial(small_back_kernel, layer), "small_bwd", info,
            (ds, nd, few[1], few[2], few[3], few[0], small),
            [((LOCALS, HS, HS), BF), ((LOCALS, D, HS), BF),
             ((LOCALS, HS, 128), F32), ((DH, 3 * DH), F32)],
        )

    tail_scratch = [(tall, F32), (wide, F32)]
    def tail_ins(parts, back, keep, share, acts):
        return (*parts, *back, share[4], share[1], share[2], share[3], share[0], small, *acts, *keep, slot, vec, mats)

    ds, send, keep = half_call(1, grad2, held.pop("m1"), acts1[3], held.pop("y1"))
    parts = exchange(send)
    back = small_back(1, ds, nd1, few1)
    grad1, small1 = call(
        functools.partial(tail_kernel, npts, 1), "tail", info,
        (*tail_ins(parts, back, keep, share1, acts1), "early", "late"),
        [(wide, F32), ((DH, S + 3 * DH), F32)], tail_scratch, held,
    )
    ds, send, keep = half_call(0, grad1, m0, acts0[3], y0)
    parts = exchange(send)
    early_terms, after = scatter_start(place, held.pop("early"), small1)
    back = small_back(0, ds, nd0, few0)
    (small_out,) = call(
        functools.partial(end_kernel, npts), "end", info,
        (*tail_ins(parts, back, keep, share0, acts0), features, after, "late"),
        [((LAYERS, DH, S + 3 * DH), F32)], tail_scratch, held,
    )
    late = held.pop("late")
    if not direct:
        few = small_out.reshape(LAYERS, devices, width).transpose(1, 0, 2).reshape(devices, cols, UNIT)
        late = late.at[:, len(LATE) * cols :, SMALL_AT : SMALL_AT + UNIT].set(few)
    late_terms, _ = scatter_start(place, late, after)
    (joined,) = call(
        functools.partial(join_kernel, (len(early_terms), len(late_terms))), "join", None,
        (*early_terms, *late_terms), [((npts, 12 * cols, D), F32)],
    )
    own, sums = call(
        functools.partial(square_kernel, devices), "square", None,
        (lax.all_to_all(joined, "pts", 0, 0), held.pop("rel")), [((12 * cols, D), F32), ((devices, 2, 128), F32)],
    )
    sums = lax.all_to_all(sums, ALL, 0, 0)
    cube, flat = [((count_mats, cols, D), F32)] * 3, [((LAYERS, width), F32)] * 3
    loss, grad_norm, *new = call(
        update_kernel, "update", None,
        (sums, own, *turned, *vecs, smalls, smalls_moment, smalls_second),
        [((1,), F32)] * 2 + cube + flat + [((cols, count_vecs), F32)] * 3,
    )
    return (
        loss.reshape(()), grad_norm.reshape(()),
        *[a.transpose(0, 2, 1) for a in new[:3]], *new[3:6], *[a.T for a in new[6:]],
    )


def solution(mesh):
    both = ("mesh", "pts")
    cube, flat = P(None, None, both), P(None, both)
    return jax.shard_map(
        per_device,
        mesh=mesh,
        in_specs=(flat, flat, P(both), cube, cube, cube, flat, flat, flat, flat, flat, flat),
        out_specs=(P(), P(), cube, cube, cube, flat, flat, flat, flat, flat, flat),
        check_vma=False,
    )
```

```python
import functools
import jax
import jax.numpy as jnp
from jax import lax
from jax.experimental import pallas as pl
from jax.experimental.pallas import tpu as pltpu
from jax.sharding import PartitionSpec as P

D = 256
H = 8
DH = 32
S = 64
HS = H * S
F_IN = 7
F_OUT = 4
LAYERS = 2
MESH_GRP = 4
STEP = 5
LOCALS = MESH_GRP - 1
WINDOW = 640
PART = 512
ND_ROWS = 40


EPS_NORM = 1e-05
EPS_SLICE = 1e-05
EPS_LOSS = 1e-06
CLIP = 0.01
LEARN = 0.03
BETA_ONE = 0.9
BETA_TWO = 0.95
EPS_ADAM = 1e-08
DECAY = 0.1
BF = jnp.bfloat16
F32 = jnp.float32
I32 = jnp.int32
ALL = ("mesh", "pts")
BASE = 9 * LAYERS


def dot(left, right):
    return jnp.dot(left, right, preferred_element_type=F32)


def dot_nt(left, right):
    return lax.dot_general(left, right, (((1,), (1,)), ((), ())), preferred_element_type=F32)


def dot_tn(left, right):
    return lax.dot_general(left, right, (((0,), (0,)), ((), ())), preferred_element_type=F32)


def low(value):
    return value.astype(BF)


def block_mask():
    rows = lax.broadcasted_iota(I32, (D, HS), 0) // DH
    cols = lax.broadcasted_iota(I32, (D, HS), 1) // S
    return rows == cols


def spread_blocks(compact):
    tall = jnp.concatenate([compact] * H, 0)
    return jnp.where(block_mask(), tall, jnp.zeros_like(tall))


def fold_blocks(full):
    lanes = lax.broadcasted_iota(I32, (DH, HS), 1) // S
    total = jnp.zeros((DH, HS), F32)
    for head in range(H):
        total = jnp.where(lanes == head, full[head * DH : (head + 1) * DH], total)
    return total


def pick_matrix():
    rows = lax.broadcasted_iota(I32, (S, HS), 0)
    cols = lax.broadcasted_iota(I32, (S, HS), 1) % S
    return (rows == cols).astype(F32).astype(BF)


def norm_stats(hidden):
    row_mean = jnp.sum(hidden, 0, keepdims=True) * (1.0 / D)
    centred = hidden - row_mean
    row_var = jnp.sum(centred * centred, 0, keepdims=True) * (1.0 / D)
    return centred, lax.rsqrt(row_var + EPS_NORM)


def norm_apply(hidden, gain, shift):
    centred, scale = norm_stats(hidden)
    return low(centred * scale * gain + shift)


def norm_back(grad, unit, scale, gain):
    inner = grad * gain
    first = jnp.sum(inner, 0, keepdims=True) * (1.0 / D)
    second = jnp.sum(inner * unit, 0, keepdims=True) * (1.0 / D)
    return scale * (inner - first - unit * second)


ROOT = 0.7978845608028654
CUBIC = 0.044715


def gelu(value):
    return 0.5 * value * (1.0 + jnp.tanh(ROOT * (value + CUBIC * (value * value * value))))


def gelu_both(value):
    square = value * value
    bend = jnp.tanh(ROOT * (value + CUBIC * (square * value)))
    half = 0.5 * (1.0 + bend)
    slope = half + 0.5 * value * (1.0 - bend * bend) * (ROOT * (1.0 + 3.0 * CUBIC * square))
    return value * half, slope


def lane_fold(value):
    total = value[:, :128]
    for start in range(128, value.shape[1], 128):
        total = total + value[:, start : start + 128]
    return total


def columns(sums):
    lanes = lax.broadcasted_iota(I32, (D, 128), 1)
    total = jnp.zeros((D, 128), F32)
    for index, value in sums:
        total = jnp.where(lanes == index, jnp.sum(value, 1, keepdims=True), total)
    return total


def slice_matrix(small):
    wide = jnp.concatenate([small[:, :S], small[:, :S]], 1)
    return spread_blocks(jnp.concatenate([wide] * (HS // (2 * S)), 1))


def slice_forward(num_dens, small):
    pick, mask = pick_matrix(), block_mask()
    tokens = [low(nd[:DH] / (nd[DH : DH + 1] + EPS_SLICE)) for nd in num_dens]
    mixed = [low(dot_tn(small[:, S:], t)) for t in tokens]
    keys = [low(dot_nt(pick, spread_blocks(m[DH : 2 * DH]))) for m in mixed]
    values = [low(dot_nt(spread_blocks(m[2 * DH :]), pick)) for m in mixed]
    scores = [dot(k, spread_blocks(m[:DH])) * DH ** (-0.5) for k, m in zip(keys, mixed)]
    raised = [jnp.exp(s - jnp.max(s, 0, keepdims=True)) for s in scores]
    attn = [r * (1.0 / jnp.sum(r, 0, keepdims=True)) for r in raised]
    full = [dot(v, low(a)) for v, a in zip(values, attn)]
    routed = [low(jnp.where(mask, f, jnp.zeros_like(f))) for f in full]
    return list(zip(routed, attn, tokens, mixed))


def widen(tall):
    pair = jnp.concatenate([tall, tall], 1)
    return fold_blocks(jnp.concatenate([pair] * (HS // (2 * S)), 1))


def slice_backward(d_slices, num_dens, attns, tokens, mixed, small):
    pick = pick_matrix()
    scale = DH ** (-0.5)
    lows = [low(a) for a in attns]
    d_full = [spread_blocks(d) for d in d_slices]
    query_full = [spread_blocks(m[:DH]) for m in mixed]
    values = [low(dot_nt(pick, spread_blocks(m[2 * DH :]))) for m in mixed]
    keys = [low(dot_nt(spread_blocks(m[DH : 2 * DH]), pick)) for m in mixed]
    d_attn = [dot(v, d) for v, d in zip(values, d_full)]
    d_values = [low(widen(dot_nt(d, a))) for d, a in zip(d_full, lows)]
    d_scores = [low(a * (d - jnp.sum(d * a, 0, keepdims=True))) for a, d in zip(attns, d_attn)]
    d_queries = [low(fold_blocks(dot(k, d)) * scale) for k, d in zip(keys, d_scores)]
    d_keys = [low(widen(dot_nt(q, d)) * scale) for q, d in zip(query_full, d_scores)]
    d_mixed = [jnp.concatenate(group, 0) for group in zip(d_queries, d_keys, d_values)]
    d_tokens = [dot(small[:, S:], d) for d in d_mixed]
    d_weight = [dot_nt(t, d) for t, d in zip(tokens, d_mixed)]
    inverse = [1.0 / (nd[DH : DH + 1] + EPS_SLICE) for nd in num_dens]
    d_num = [spread_blocks(low(d * i)) for d, i in zip(d_tokens, inverse)]
    d_den = [
        -jnp.sum(d * nd[:DH], 0, keepdims=True) * i * i for d, nd, i in zip(d_tokens, num_dens, inverse)
    ]
    return list(zip(d_num, d_den, d_weight))


def is_mesh(slot, mesh_id):
    return (slot == mesh_id).astype(F32)


def columns_at(vec, index):
    return vec[:, index : index + 1]


def sum_parts(parts):
    terms = [part[...].astype(F32) for part in parts]
    while len(terms) > 1:
        terms = [terms[i] + terms[i + 1] for i in range(0, len(terms), 2)]
    return terms[0]


def window(info, place, index, width):
    start = info[5 + place] + index * WINDOW
    at = pl.multiple_of(jnp.minimum(start, width - WINDOW), 128)
    return start, pl.ds(at, WINDOW)


def inside_of(info, place, slot, start, part):
    lanes = lax.broadcasted_iota(I32, (1, WINDOW), 1) + part.start
    mesh_id = info[2 + place]
    first = jnp.where(start == info[5 + place], 0, start)
    return ((slot[:, part] == mesh_id) & (lanes >= first)).astype(F32)


def each_window(info, slot, value, store, side_by_side=True):
    width = slot.shape[1]

    @pl.when(info[1] != 0)
    def _():
        found = []
        for place in range(LOCALS if side_by_side else 0):
            start, part = window(info, place, 0, width)
            found.append((part, value(place, part, inside_of(info, place, slot, start, part))))
        for place, (part, result) in enumerate(found):
            store(place, part, result)

        def more(place, carry):
            def step(index, carry):
                start, part = window(info, place, index, width)
                store(place, part, value(place, part, inside_of(info, place, slot, start, part)))
                return carry

            return lax.fori_loop(1 if side_by_side else 0, info[8 + place], step, carry)

        lax.fori_loop(0, LOCALS, more, 0)


def any_local(info, visit):
    @pl.when(info[1] != 0)
    def _():
        visit()


LATE = (0, 1, 5 * LAYERS)
EARLY = tuple(m for m in range(5 * LAYERS + 1) if m not in LATE)
SMALL_AT = 64
UNIT = 40


def put(early_ref, late_ref, matrix, value):
    ref, row = (late_ref, LATE.index(matrix)) if matrix in LATE else (early_ref, EARLY.index(matrix))
    devices, cols = ref.shape[0], D // ref.shape[0]
    ref[:, row * cols : (row + 1) * cols, :] = value.reshape(devices, cols, D)


def put_columns(late_ref, sums, fresh=False):
    devices, cols = late_ref.shape[0], D // late_ref.shape[0]
    value = columns(sums).reshape(devices, cols, 128)
    if not fresh:
        value = value + late_ref[:, len(LATE) * cols :, :128]
    late_ref[:, len(LATE) * cols :, :128] = value


def small_grad(slope, mixed):
    total = slope[:, :S]
    for head in range(1, H):
        total = total + slope[:, head * S : (head + 1) * S]
    return jnp.concatenate([total, mixed], 1)


def small_units(width, rows):
    step = min(width, UNIT)
    for k in range(LAYERS * width // step):
        yield k * step // width, k * step % width, k * step // UNIT, k * step % UNIT, step


def start_copies(sources, targets, sems, first):
    copies = [
        pltpu.make_async_copy(a, b, sems.at[first + j]) for j, (a, b) in enumerate(zip(sources, targets))
    ]
    for copy in copies:
        copy.start()
    return copies


def finish_copies(copies):
    for copy in copies:
        copy.wait()


def front(hidden, vec, layer, mats, small, slot, info, w_ref, nd_ref, send_ref, stage, far, sems):
    x_ref, f_ref, probs_ref = stage
    base = 9 * layer
    width = hidden.shape[1]
    u = norm_apply(hidden, columns_at(vec, base), columns_at(vec, base + 1))
    pair = dot(mats[5 * layer : 5 * layer + 2].reshape(2 * D, D), u)
    x_low = low(pair[:D] + columns_at(vec, base + 2))
    f_low = low(pair[D:] + columns_at(vec, base + 3))
    x_ref[...] = x_low
    f_ref[...] = f_low
    copies = start_copies(stage[:2], far[:2], sems, 0)
    logits = dot(slice_matrix(small[layer]).T, x_low).reshape(H, S, width)
    raised = jnp.exp(logits - jnp.max(logits, 1, keepdims=True))
    valid = (slot[...] < MESH_GRP).astype(F32)
    probs = (raised * (valid[None] / jnp.sum(raised, 1, keepdims=True))).reshape(HS, width)
    probs_ref[...] = probs
    copies = copies + start_copies(stage[2:], far[2:], sems, 2)
    w_low = low(probs)
    w_ref[...] = w_low

    def rows_of(features, mine):
        ones = jnp.broadcast_to(mine, (16, mine.shape[1]))
        return jnp.concatenate([low(features.astype(F32) * mine), low(ones)], 0)

    def compact(full):
        return jnp.concatenate([fold_blocks(full[:D]), full[D : D + ND_ROWS - DH]], 0)

    send_ref[...] = low(compact(dot_nt(rows_of(f_low, is_mesh(slot[...], info[0])), w_low)))

    nd_ref[...] = jnp.zeros_like(nd_ref)

    def value(place, part, mask):
        return compact(dot_nt(rows_of(f_ref[:, part], mask), w_ref[:, part]))

    def store(place, part, result):
        nd_ref[place] = nd_ref[place] + result

    each_window(info, slot, value, store)
    return copies


def back_half(w_in, slot, info, routed, routed_big, mix, hidden, vec, layer, mats):
    base = 9 * layer
    mix[...] = dot(routed_big[...], w_in[...]) * is_mesh(slot[...], info[0])

    def value(place, part, mask):
        return dot(routed[place], w_in[:, part]) * mask

    def store(place, part, result):
        mix[:, part] = mix[:, part] + result

    each_window(info, slot, value, store)
    y_low = low(mix[...])
    middle = hidden + dot(mats[5 * layer + 2], y_low) + columns_at(vec, base + 4)
    u2 = norm_apply(middle, columns_at(vec, base + 5), columns_at(vec, base + 6))
    pre = dot(mats[5 * layer + 3], u2) + columns_at(vec, base + 7)
    out = middle + dot(mats[5 * layer + 4], low(gelu(pre))) + columns_at(vec, base + 8)
    return y_low, middle, out


def head_half(grad, vec, layer, mats, middle, probs, y_low, slot, info, early_ref, late_ref, ds_ref, send_ref, acc, keep):
    base = 9 * layer
    grad_low = low(grad)
    centred, scale = norm_stats(middle)
    unit = centred * scale
    gain = columns_at(vec, base + 5)
    u2 = low(unit * gain + columns_at(vec, base + 6))
    activ, slope = gelu_both(dot(mats[5 * layer + 3], u2) + columns_at(vec, base + 7))
    d_pre = dot_tn(mats[5 * layer + 4], grad_low) * slope
    d_pre_low = low(d_pre)
    d_norm = dot_tn(mats[5 * layer + 3], d_pre_low)
    d_mid = norm_back(d_norm, unit, scale, gain) + grad
    d_mid_low = low(d_mid)
    d_y = low(dot_tn(mats[5 * layer + 2], d_mid_low))
    d_y_ref, d_mid_ref = keep
    d_y_ref[...] = d_y
    d_mid_ref[...] = d_mid
    put(early_ref, late_ref, 5 * layer + 4, dot_nt(grad_low, low(activ)))
    put(early_ref, late_ref, 5 * layer + 3, dot_nt(d_pre_low, u2))
    put(early_ref, late_ref, 5 * layer + 2, dot_nt(d_mid_low, y_low))
    own = low(d_y.astype(F32) * is_mesh(slot[...], info[0]))
    send_ref[...] = low(fold_blocks(dot_nt(own, low(probs[...]))))

    acc[...] = jnp.zeros_like(acc)

    def value(place, part, mask):
        mine = low(d_y_ref[:, part].astype(F32) * mask)
        return fold_blocks(dot_nt(mine, low(probs[:, part])))

    def store(place, part, result):
        acc[place] = acc[place] + result

    each_window(info, slot, value, store)
    ds_ref[...] = low(acc[...])
    return [(base + 4, lane_fold(d_mid)), (base + 5, lane_fold(d_norm * unit)),
            (base + 6, lane_fold(d_norm)), (base + 7, lane_fold(d_pre)), (base + 8, lane_fold(grad))]


def tail_half(vec, layer, mats, small, hidden, x_in, f_in, probs_in, d_y, d_mid, slot, info,
              back, back_big, route, mix, grad_ref, early_ref, late_ref):
    width = hidden.shape[1]
    base = 9 * layer
    both_big, num_big, den_big = back_big
    both, d_num, d_den = back
    quarters = [slice(at, at + PART) for at in range(0, width, PART)]
    for part in quarters:
        mine = is_mesh(slot[:, part], info[0])
        pair = jnp.concatenate([d_y[:, part], f_in[:, part]], 0)
        route[:, part] = (dot(both_big, pair) + den_big) * mine
        mix[:, part] = dot(num_big, low(probs_in[:, part])) * mine

    def value(place, part, mask):
        piece = jnp.concatenate([d_y[:, part], f_in[:, part]], 0)
        through = (dot(both[place], piece) + d_den[place][:, :1]) * mask
        return through, dot(d_num[place], low(probs_in[:, part])) * mask

    def store(place, part, result):
        route[:, part] = route[:, part] + result[0]
        mix[:, part] = mix[:, part] + result[1]

    each_window(info, slot, value, store, False)
    gain, shift = columns_at(vec, base), columns_at(vec, base + 1)
    unslice = slice_matrix(small[layer])
    both_mats = mats[5 * layer : 5 * layer + 2].reshape(2 * D, D)
    totals = None
    for part in quarters:
        d_probs = route[:, part].reshape(H, S, PART)
        probs = probs_in[:, part].reshape(H, S, PART)
        spread = jnp.sum(d_probs * probs, 1, keepdims=True)
        d_logits = low(probs * (d_probs - spread)).reshape(HS, PART)
        d_x = dot(unslice, d_logits)
        d_f = mix[:, part]
        d_pair = jnp.concatenate([low(d_x), low(d_f)], 0)
        d_norm = dot_tn(both_mats, d_pair)
        centred, scale = norm_stats(hidden[:, part])
        unit = centred * scale
        u = low(unit * gain + shift)
        grad_ref[:, part] = norm_back(d_norm, unit, scale, gain) + d_mid[:, part]
        found = (
            dot_nt(x_in[:, part], d_logits), dot_nt(d_pair, u), lane_fold(d_norm * unit), lane_fold(d_norm),
            lane_fold(d_x), lane_fold(d_f),
        )
        totals = found if totals is None else tuple(t + f for t, f in zip(totals, found))
    slope, grads, *sums = totals
    put(early_ref, late_ref, 5 * layer, grads[:D])
    put(early_ref, late_ref, 5 * layer + 1, grads[D:])
    return [(base + j, value) for j, value in enumerate(sums)], fold_blocks(slope)


def embed_kernel(info, feat, slot, vec, mats, small,
                 h_ref, w_ref, nd_ref, send_ref, h_far, x_far, f_far, probs_far,
                 x_ref, f_ref, probs_ref, sems):
    we1 = low(vec[:, BASE + 4 : BASE + 4 + F_IN])
    e1 = dot(we1, low(feat[...])) + columns_at(vec, BASE)
    hidden = dot(mats[5 * LAYERS], low(gelu(e1))) + columns_at(vec, BASE + 1)
    h_ref[...] = hidden
    copies = start_copies([h_ref], [h_far], sems, 3)
    copies = copies + front(hidden, vec, 0, mats, small, slot, info, w_ref, nd_ref, send_ref,
                            (x_ref, f_ref, probs_ref), (x_far, f_far, probs_far), sems)
    finish_copies(copies)


def small_kernel(layer, info, nd_ref, small, routed_ref, routed_far, attn_far, tokens_far, mixed_far,
                 attn_ref, tokens_ref, mixed_ref, sems):
    stage = (routed_ref, attn_ref, tokens_ref, mixed_ref)
    far = (routed_far, attn_far, tokens_far, mixed_far)

    def visit():
        results = slice_forward([nd_ref[place] for place in range(LOCALS)], small[layer])
        for place in range(LOCALS):
            for ref, value in zip(stage, results[place]):
                ref[place] = value
        finish_copies(start_copies(stage, far, sems, 0))

    any_local(info, visit)


def share_start(parts, small, stage, far, sems, first):
    total = sum_parts(parts)
    for ref, value in zip(stage, slice_forward([total], small)[0] + (total,)):
        ref[...] = value
    return start_copies(stage, far, sems, first)


def middle_kernel(npts, info, *refs):
    parts, refs = refs[:npts], refs[npts:]
    (routed, w_in, h_in, slot, vec, mats, small,
     h_ref, w_ref, nd_ref, send_ref, *refs) = refs
    share_far, (y_far, m_far, h_far, x_far, f_far, probs_far), refs = refs[:5], refs[5:11], refs[11:]
    share, (y_ref, m_ref, x_ref, f_ref, probs_ref, mix, sems) = refs[:5], refs[5:]
    copies = share_start(parts, small[0], share, share_far, sems, 6)
    y_low, middle, out = back_half(w_in, slot, info, routed, share[0], mix, h_in[...], vec, 0, mats)
    y_ref[...] = y_low
    m_ref[...] = middle
    h_ref[...] = out
    copies = copies + start_copies((h_ref, y_ref, m_ref), (h_far, y_far, m_far), sems, 3)
    copies = copies + front(out, vec, 1, mats, small, slot, info, w_ref, nd_ref, send_ref,
                            (x_ref, f_ref, probs_ref), (x_far, f_far, probs_far), sems)
    finish_copies(copies)


def head_kernel(npts, info, *refs):
    parts, refs = refs[:npts], refs[npts:]
    (routed, w_in, h_in, slot, target, vec, mats, small,
     y_ref, m_ref, h_ref, diff_ref, loss_ref, *refs) = refs
    share_far, share, (mix, sems) = refs[:5], refs[5:10], refs[10:]
    copies = share_start(parts, small[1], share, share_far, sems, 0)
    y_low, middle, out = back_half(w_in, slot, info, routed, share[0], mix, h_in[...], vec, 1, mats)
    y_ref[...] = y_low
    m_ref[...] = middle
    h_ref[...] = out
    uh = norm_apply(out, columns_at(vec, BASE + 2), columns_at(vec, BASE + 3))
    truth = target[...]
    whd = low(vec[:, BASE + 4 + F_IN : BASE + 4 + F_IN + F_OUT])
    differ = dot_tn(whd, uh) - truth
    diff_ref[...] = differ
    ids = lax.broadcasted_iota(I32, differ.shape, 0)
    member = (ids == slot[...]).astype(F32)
    squares = jnp.sum(differ * differ, 0, keepdims=True)
    sizes = jnp.sum(truth * truth, 0, keepdims=True)
    both = lane_fold(jnp.concatenate([member * squares, member * sizes], 0))
    loss_ref[...] = jnp.broadcast_to(jnp.sum(both, 1, keepdims=True), loss_ref.shape)
    finish_copies(copies)


def loss_kernel(npts, groups, info, *refs):
    parts, refs = refs[:npts], refs[npts:]
    diff, slot, h_in, vec, grad_ref, rel_ref, early_ref, late_ref = refs
    whd = low(vec[:, BASE + 4 + F_IN : BASE + 4 + F_IN + F_OUT])
    total = sum_parts(parts)
    err_root = jnp.sqrt(total[:MESH_GRP] + EPS_LOSS)
    tgt_root = jnp.sqrt(total[MESH_GRP:] + EPS_LOSS)
    rel_ref[...] = jnp.concatenate([err_root / tgt_root, jnp.zeros_like(err_root)], 0)
    coef = (1.0 / (err_root * tgt_root) * (1.0 / (MESH_GRP * groups)))[:, :1]
    ids = lax.broadcasted_iota(I32, diff.shape, 0)
    member = (ids == slot[...]).astype(F32)
    d_pred = low(diff[...] * jnp.sum(member * coef, 0, keepdims=True))
    d_head = dot(whd, d_pred)
    centred, scale = norm_stats(h_in[...])
    unit = centred * scale
    gain = columns_at(vec, BASE + 2)
    g_whd = dot_nt(low(unit * gain + columns_at(vec, BASE + 3)), d_pred)
    put_columns(late_ref, [(BASE + 2, lane_fold(d_head * unit)), (BASE + 3, lane_fold(d_head))]
                + [(BASE + 4 + F_IN + j, g_whd[:, j : j + 1]) for j in range(F_OUT)], True)
    grad_ref[...] = norm_back(d_head, unit, scale, gain)


def half_kernel(layer, info, grad, middle, probs, y_low, slot, vec, mats, early_ref, late_ref,
                ds_ref, send_ref, d_y_ref, d_mid_ref, acc):
    sums = head_half(grad[...], vec, layer, mats, middle[...], probs, y_low[...], slot, info, early_ref, late_ref,
                     ds_ref, send_ref, acc, (d_y_ref, d_mid_ref))
    put_columns(late_ref, sums)


def small_back_kernel(layer, info, ds_in, nd_ref, attn, tokens, mixed, routed, small,
                      both_ref, dn_ref, den_ref, dw_ref):
    dw_ref[...] = jnp.zeros_like(dw_ref)

    def visit():
        tables = [[ref[place] for place in range(LOCALS)] for ref in (ds_in, nd_ref, attn, tokens, mixed)]
        results = slice_backward(*tables, small[layer])
        for place, (dn, den, dw) in enumerate(results):
            both_ref[place] = jnp.concatenate([routed[place], dn], 0).T
            dn_ref[place] = dn
            den_ref[place] = jnp.broadcast_to(den, (128, HS)).T
        dw_ref[...] = results[0][2] + results[1][2] + results[2][2]

    any_local(info, visit)


def tail_start(npts, parts, small, ndb, attn, tokens, mixed, routed_big, dw_in):
    total = low(sum_parts(parts))
    ((d_num, d_den, d_weight),) = slice_backward(
        *[[value] for value in (total, ndb[...], attn[...], tokens[...], mixed[...])], small
    )
    d_weight = dw_in[...] + d_weight * (1.0 / npts)
    both = jnp.concatenate([routed_big[...], d_num], 0).T
    return (both, d_num, jnp.broadcast_to(d_den, (128, HS)).T[:, :1]), d_weight


def tail_kernel(npts, layer, info, *refs):
    parts, refs = refs[:npts], refs[npts:]
    (both_in, dn_in, den_in, dw_in, ndb, attn, tokens, mixed, routed_big, small,
     h_in, x_in, f_in, probs, d_y, d_mid, slot, vec, mats, late_ref, *early,
     grad_ref, small_ref, route, mix) = refs
    back_big, d_weight = tail_start(npts, parts, small[layer], ndb, attn, tokens, mixed, routed_big, dw_in)
    sums, slope = tail_half(vec, layer, mats, small, h_in, x_in, f_in, probs, d_y, d_mid, slot, info,
                            (both_in, dn_in, den_in), back_big, route, mix, grad_ref,
                            early[0] if early else None, late_ref)
    small_ref[...] = small_grad(slope, d_weight)
    put_columns(late_ref, sums)


def last_kernel(grad_in, feat, vec, mats, small0, small1, late_ref, small_ref):
    feat_low = low(feat[...])
    we1 = low(vec[:, BASE + 4 : BASE + 4 + F_IN])
    activ, slope = gelu_both(dot(we1, feat_low) + columns_at(vec, BASE))
    grad = grad_in[...]
    grad_low = low(grad)
    d_embed = dot_tn(mats[5 * LAYERS], grad_low) * slope
    put(None, late_ref, 5 * LAYERS, dot_nt(grad_low, low(activ)))
    g_we1 = dot_nt(low(d_embed), feat_low)
    put_columns(late_ref, [(BASE, lane_fold(d_embed)), (BASE + 1, lane_fold(grad))]
                + [(BASE + 4 + j, g_we1[:, j : j + 1]) for j in range(F_IN)])
    small_ref[0] = small0[...]
    small_ref[1] = small1[...]
    cols = D // late_ref.shape[0]
    if cols * UNIT == 2 * (S + 3 * DH):
        for layer, column, row, lane, step in small_units(cols * UNIT // LAYERS, cols):
            late_ref[:, len(LATE) * cols + row, SMALL_AT + lane : SMALL_AT + lane + step] = (
                small_ref[layer, :, column : column + step]
            )


def pack_kernel(place, slot, mats, vecs, smalls, block_ref, info_ref):
    count, cols, _ = mats.shape
    points = slot.shape[1]
    block_ref[: count * cols] = low(mats[...].reshape(count * cols, D))
    block_ref[count * cols :] = jnp.zeros((cols, D), BF)
    block_ref[count * cols :, : vecs.shape[1]] = low(vecs[...])
    for layer, column, row, lane, step in small_units(smalls.shape[1], cols):
        block_ref[count * cols + row : count * cols + row + 1, SMALL_AT + lane : SMALL_AT + lane + step] = low(
            smalls[layer : layer + 1, column : column + step]
        )
    lanes = lax.broadcasted_iota(I32, (1, points), 1).astype(F32)
    ids = slot[...]
    edge = jnp.where(place[0] == 0, points - 1, 0).astype(F32)
    big = jnp.sum(jnp.where(lanes == edge, ids.astype(F32), 0.0)).astype(I32)
    info_ref[0] = big
    total = 0
    for j in range(LOCALS):
        mesh_id = j + jnp.where(big <= j, 1, 0)
        mine = ids == mesh_id
        first = jnp.min(jnp.where(mine, lanes, float(points))).astype(I32)
        last = jnp.max(jnp.where(mine, lanes, -1.0)).astype(I32)
        start = jnp.minimum((first >> 7) << 7, points - WINDOW)
        count_j = jnp.where(last >= 0, lax.div(jnp.maximum(last - start, 0), WINDOW) + 1, 0)
        info_ref[2 + j] = jnp.where(last >= 0, mesh_id, -1)
        info_ref[5 + j] = start
        info_ref[8 + j] = count_j
        total = total + count_j
    info_ref[1] = total


def unpack_kernel(masks, place, *refs):
    pieces, (mats_ref, vecs_ref, *rest) = refs[: len(masks)], refs[len(masks) :]
    count, _, cols, _ = mats_ref.shape
    for mask, piece in zip(masks, pieces):
        for i in range(piece.shape[0]):
            for k in range(piece.shape[1]):
                at = (place[1] ^ (mask | (i << 1))) * piece.shape[1] + (place[0] ^ k)
                for m in range(count):
                    mats_ref[m, at] = piece[i, k, m * cols : (m + 1) * cols, :]
                vecs_ref[at] = piece[i, k, count * cols :, :].astype(F32)
    if rest:
        for layer, column, row, lane, step in small_units(cols * UNIT // LAYERS, cols):
            rest[0][layer, :, column : column + step] = low(vecs_ref[:, row, SMALL_AT + lane : SMALL_AT + lane + step])


def split_kernel(place, grads, send_ref):
    send_ref[...] = grads[:, 1 - (place[1] & 1)]


def fold_kernel(first, shift, place, *refs):
    terms, outs = refs
    index = (place[1] >> shift) & (len(outs) - 1)
    for k, out in enumerate(outs):
        total = None
        for j, term in enumerate(terms):
            value = term[index ^ k, :, place[1] & 1] if first and j == 0 else term[index ^ k]
            total = value if total is None else total + value
        out[...] = total


def join_kernel(counts, *refs):
    out, row = refs[-1], 0
    at = 0
    for count in counts:
        total = refs[at][...]
        for ref in refs[at + 1 : at + count]:
            total = total + ref[...]
        out[:, row : row + total.shape[1]] = total
        row, at = row + total.shape[1], at + count


def square_kernel(devices, early, late, rel, own_ref, sums_ref):
    wholes = []
    for parts in (early, late):
        total = parts[0]
        for j in range(1, parts.shape[0]):
            total = total + parts[j]
        wholes.append(total)
    own = jnp.concatenate(wholes, 0)
    own_ref[...] = own
    rows = lax.broadcasted_iota(I32, own.shape, 0)
    lanes = lax.broadcasted_iota(I32, own.shape, 1)
    edge = own.shape[0] // 12 * 11
    used = (rows < edge) | (lanes < BASE + 4 + F_IN + F_OUT) | ((lanes >= SMALL_AT) & (lanes < SMALL_AT + UNIT))
    squares = jnp.sum(jnp.where(used, own * own, 0.0))
    loss = jnp.sum(rel[:MESH_GRP, :1]) * (1.0 / (MESH_GRP * devices))
    which = lax.broadcasted_iota(I32, sums_ref.shape, 1)
    sums_ref[...] = jnp.where(which == 0, squares, loss)


def adamw(weight, moment, second, grad, factor):
    clipped = grad * factor
    moment = BETA_ONE * moment + (1.0 - BETA_ONE) * clipped
    second = BETA_TWO * second + (1.0 - BETA_TWO) * clipped * clipped
    moment_hat = moment / (1.0 - BETA_ONE**STEP)
    second_hat = second / (1.0 - BETA_TWO**STEP)
    updated = weight - LEARN * (moment_hat / (jnp.sqrt(second_hat) + EPS_ADAM) + DECAY * weight)
    return (moment, second, updated)


def update_kernel(sums, own, *refs):
    mats, vecs, smalls, outs = refs[:3], refs[3:6], refs[6:9], refs[9:]
    totals = jnp.sum(sums[...], 0)
    norm = jnp.sqrt(totals[:1, :1])
    factor = jnp.minimum(1.0, CLIP / norm)
    outs[0][0] = totals[1, 0]
    outs[1][0] = norm[0, 0]
    count, cols, _ = mats[0].shape
    for m in range(count):
        row = EARLY.index(m) if m in EARLY else len(EARLY) + LATE.index(m)
        for out, value in zip(outs[2:5], adamw(*[r[m] for r in mats], own[row * cols : (row + 1) * cols], factor)):
            out[m] = value
    grad = own[count * cols :, : vecs[0].shape[1]]
    for out, value in zip(outs[8:11], adamw(*[r[...] for r in vecs], grad, factor)):
        out[...] = value
    for layer, column, row, lane, step in small_units(smalls[0].shape[1], cols):
        grad = own[count * cols + row : count * cols + row + 1, SMALL_AT + lane : SMALL_AT + lane + step]
        old = [r[layer : layer + 1, column : column + step] for r in smalls]
        for out, value in zip(outs[5:8], adamw(*old, grad, factor)):
            out[layer : layer + 1, column : column + step] = value


LIMITS = dict(embed=14, small_fwd=5, middle=20, head=10, loss=8, half=20, small_bwd=4, tail=17, last=12,
              pack=3, unpack=3, split=3, fold=3, join=3, square=3, update=4)
WORK = {}


def call(kernel, name, info, ins, outs, scratch=(), held=None, far=(), sems=0, nest=False):
    near = len(outs)
    outs = list(outs) + list(far)
    held = {} if held is None else held
    names = list(held)
    plain = [a for a in ins if not isinstance(a, str)]
    inside = pl.BlockSpec(memory_space=pltpu.VMEM)
    table = [] if info is None else [info]
    first, second = len(table) + len(plain), len(table) + len(plain) + len(names)

    def body(*refs):
        rest = iter(refs[len(table) : first])
        kept = dict(zip(names, refs[first:second]))
        order = [kept[a] if isinstance(a, str) else next(rest) for a in ins]
        results = refs[second : second + len(outs)]
        after = refs[second + len(outs) + len(names) :]
        if nest:
            kernel(*refs[: len(table)], order, results)
        else:
            kernel(*refs[: len(table)], *order, *results, *after)

    res = pl.pallas_call(
        body,
        in_specs=[pl.BlockSpec(memory_space=pltpu.SMEM)] * len(table) + [inside] * (second - len(table)),
        out_specs=[
            pl.BlockSpec(memory_space=pltpu.SMEM) if len(shape) == 1 else inside for shape, _ in outs[:near]
        ]
        + [pl.BlockSpec(memory_space=pltpu.HBM)] * len(far)
        + [inside] * len(names),
        out_shape=[jax.ShapeDtypeStruct(s, t) for s, t in outs]
        + [jax.ShapeDtypeStruct(held[n].shape, held[n].dtype) for n in names],
        input_output_aliases={first + j: len(outs) + j for j in range(len(names))},
        scratch_shapes=[pltpu.VMEM(s, t) for s, t in scratch]
        + ([pltpu.SemaphoreType.DMA((sems,))] if sems else []),
        compiler_params=pltpu.CompilerParams(vmem_limit_bytes=LIMITS[name] * 2**20),
        cost_estimate=pl.CostEstimate(flops=WORK.get(name, 1000), bytes_accessed=1000, transcendentals=0),
        name=name,
    )(*table, *plain, *[held[n] for n in names])
    held.update(zip(names, res[len(outs) :]))
    return res[: len(outs)]


def swap(value, axis, mask):
    size = lax.axis_size(axis)
    return lax.ppermute(value, axis, [(i, i ^ mask) for i in range(size)])


def bit_groups(size):
    bits = size.bit_length() - 1
    groups, low = [], 1
    while low < bits:
        width = min(2, bits - low)
        groups.append((low, width))
        low += width
    return groups


def gather_pieces(block):
    held = jnp.stack([block] + [swap(block, "pts", k) for k in range(1, lax.axis_size("pts"))])[None]
    masks, pieces = [0], [held]
    for low, width in bit_groups(lax.axis_size("mesh")):
        held = jnp.concatenate(pieces)
        masks = [k << low for k in range(1 << width)]
        pieces = [held] + [swap(held, "mesh", m) for m in masks[1:]]
    return masks + [m | 1 for m in masks], pieces + [swap(p, "mesh", 1) for p in pieces]


def scatter_start(place, grads, later, gate=()):
    mesh_size, pts_size = lax.axis_size("mesh"), lax.axis_size("pts")
    rows = grads.shape[1]
    grads = grads.reshape(mesh_size // 2, 2, pts_size, rows, D)
    (send,) = call(split_kernel, "split", place, (grads,), [((mesh_size // 2, pts_size, rows, D), F32)])
    terms = [grads, swap(send, "mesh", 1)]
    terms[1], *gate = lax.optimization_barrier((terms[1], *gate))
    left = mesh_size // 2
    for number, (low, width) in enumerate(reversed(bit_groups(mesh_size))):
        count = 1 << width
        left //= count
        shape = (count, left, pts_size, rows, D)
        views = [t.reshape(shape) for t in terms[1:]]
        views = [terms[0].reshape((count, left, 2) + shape[2:] if number == 0 else shape)] + views
        pieces = call(
            functools.partial(fold_kernel, number == 0, low), "fold", place, views, [(shape[1:], F32)] * count,
            nest=True,
        )
        if number == 0:
            *pieces, later = lax.optimization_barrier((*pieces, later))
        terms = [pieces[0]] + [swap(p, "mesh", k << low) for k, p in enumerate(pieces) if k]
    return [t.reshape(pts_size, rows, D) for t in terms], later, gate


def per_device(
    features,
    targets,
    mesh_slot,
    matrices,
    matrices_moment,
    matrices_second,
    smalls,
    smalls_moment,
    smalls_second,
    vectors,
    vectors_moment,
    vectors_second,
):
    groups, npts = lax.axis_size("mesh"), lax.axis_size("pts")
    devices = groups * npts
    cols, width = matrices.shape[2], smalls.shape[1]
    points = mesh_slot.shape[0]
    count_mats, count_vecs = matrices.shape[0], vectors.shape[0]
    slot = mesh_slot[None]
    place = jnp.stack([lax.axis_index("pts"), lax.axis_index("mesh")]).astype(I32)
    turned = [a.transpose(0, 2, 1) for a in (matrices, matrices_moment, matrices_second)]
    vecs = [a.T for a in (vectors, vectors_moment, vectors_second)]
    block, info = call(
        pack_kernel, "pack", place, (slot, turned[0], vecs[0], smalls), [((12 * cols, D), BF), ((16,), I32)]
    )
    masks, pieces = gather_pieces(block)
    direct = cols * UNIT == 2 * (S + 3 * DH)
    mats, vec, *rest = call(
        functools.partial(unpack_kernel, masks), "unpack", place, pieces,
        [((count_mats, devices, cols, D), BF), ((devices, cols, D), F32)]
        + ([((LAYERS, DH, S + 3 * DH), BF)] if direct else []),
    )
    if direct:
        small = rest[0]
    else:
        small = vec[:, :, SMALL_AT : SMALL_AT + UNIT].reshape(devices, LAYERS, width).astype(BF)
        small = small.transpose(1, 0, 2).reshape(LAYERS, DH, S + 3 * DH)
    mats = mats.reshape(count_mats, D, D)
    vec = vec.reshape(D, D)

    wide = (D, points)
    tall = (HS, points)

    def exchange(value):
        return [value] + [swap(value, "pts", k) for k in range(1, npts)]

    held = {}

    def hold(**values):
        held.update(values)

    share = [((D, HS), BF), ((S, HS), F32), ((DH, HS), BF), ((3 * DH, HS), BF), ((ND_ROWS, HS), F32)]
    acts = [(wide, BF), (wide, BF), (tall, F32)]
    nears = [(wide, F32), (tall, BF), ((LOCALS, ND_ROWS, HS), F32), ((ND_ROWS, HS), BF)]
    few_out = [((LOCALS, D, HS), BF), ((LOCALS, S, HS), F32),
               ((LOCALS, DH, HS), BF), ((LOCALS, 3 * DH, HS), BF)]

    def small_call(nd, layer):
        routed, *rest = call(
            functools.partial(small_kernel, layer), "small_fwd", info, (nd, small),
            few_out[:1], few_out[1:], None, few_out, 4,
        )
        return routed, rest

    h0, w0, nd0, send, *acts0 = call(
        embed_kernel, "embed", info, (features, slot, vec, mats, small),
        nears, acts, None, [(wide, F32)] + acts, 4,
    )
    parts = exchange(send)
    routed, few0 = small_call(nd0, 0)
    h1, w1, nd1, send, *rest = call(
        functools.partial(middle_kernel, npts), "middle", info,
        (*parts, routed, w0, h0, slot, vec, mats, small),
        nears, share + [(wide, BF), (wide, F32)] + acts + [(wide, F32)], None,
        share + [(wide, BF), (wide, F32), (wide, F32)] + acts, 11,
    )
    share0, (y0, m0, *acts1) = rest[:5], rest[5:]

    parts = exchange(send)
    routed, few1 = small_call(nd1, 1)
    y1, m1, h2, diff, loss_part, *share1 = call(
        functools.partial(head_kernel, npts), "head", info,
        (*parts, routed, w1, h1, slot, targets, vec, mats, small),
        [(wide, BF), (wide, F32), (wide, F32), ((F_OUT, points), F32), ((8, 128), F32)],
        share + [(wide, F32)], None, share, 5,
    )
    hold(y1=y1, m1=m1)

    keeps = [(wide, BF), (wide, F32)]
    ds_out = [((LOCALS, DH, HS), BF), ((DH, HS), BF)]
    parts = exchange(loss_part)
    grad2, rel, early, late = call(
        functools.partial(loss_kernel, npts, groups), "loss", info,
        (*parts, diff, slot, h2, vec),
        [(wide, F32), ((8, 128), F32), ((devices, len(EARLY) * cols, D), F32),
         ((devices, (len(LATE) + 1) * cols, D), F32)], [], held,
    )
    hold(rel=rel, early=early, late=late)

    def half_call(layer, grad, middle, probs, y_low):
        res = call(
            functools.partial(half_kernel, layer), "half", info,
            (grad, middle, probs, y_low, slot, vec, mats, "early", "late"), ds_out + keeps, [((LOCALS, DH, HS), F32)], held,
        )
        return res[0], res[1], res[2:]

    def small_back(layer, ds, nd, few):
        return call(
            functools.partial(small_back_kernel, layer), "small_bwd", info,
            (ds, nd, few[1], few[2], few[3], few[0], small),
            [((LOCALS, HS, HS), BF), ((LOCALS, D, HS), BF),
             ((LOCALS, HS, 128), F32), ((DH, 3 * DH), F32)],
        )

    tail_scratch = [(tall, F32), (wide, F32)]

    def tail_ins(parts, back, keep, share, acts):
        return (*parts, *back, share[4], share[1], share[2], share[3], share[0], small, *acts, *keep, slot, vec, mats)

    ds, send, keep = half_call(1, grad2, held.pop("m1"), acts1[3], held.pop("y1"))
    parts = exchange(send)
    back = small_back(1, ds, nd1, few1)
    grad1, small1 = call(
        functools.partial(tail_kernel, npts, 1), "tail", info,
        (*tail_ins(parts, back, keep, share1, acts1), "late", "early"),
        [(wide, F32), ((DH, S + 3 * DH), F32)], tail_scratch, held,
    )
    ds, send, keep = half_call(0, grad1, m0, acts0[3], y0)
    parts = exchange(send)
    back = small_back(0, ds, nd0, few0)
    early_terms, after, gate = scatter_start(place, held.pop("early"), features, (*parts[1:], back[3]))
    parts, back = parts[:1] + gate[:-1], [*back[:3], gate[-1]]
    grad0, small0 = call(
        functools.partial(tail_kernel, npts, 0), "tail", info,
        (*tail_ins(parts, back, keep, share0, acts0), "late"),
        [(wide, F32), ((DH, S + 3 * DH), F32)], tail_scratch, held,
    )
    (joined,) = call(
        functools.partial(join_kernel, (len(early_terms),)), "join", None, early_terms,
        [((npts, len(EARLY) * cols, D), F32)],
    )
    joined, after = lax.optimization_barrier((joined, after))
    early_own = lax.all_to_all(joined, "pts", 0, 0)
    (small_out,) = call(
        last_kernel, "last", None, (grad0, after, vec, mats, small0, small1, "late"),
        [((LAYERS, DH, S + 3 * DH), F32)], (), held,
    )
    late = held.pop("late")
    if not direct:
        few = small_out.reshape(LAYERS, devices, width).transpose(1, 0, 2).reshape(devices, cols, UNIT)
        late = late.at[:, len(LATE) * cols :, SMALL_AT : SMALL_AT + UNIT].set(few)
    late_terms, *_ = scatter_start(place, late, after)
    (joined,) = call(
        functools.partial(join_kernel, (len(late_terms),)), "join", None, late_terms,
        [((npts, (len(LATE) + 1) * cols, D), F32)],
    )
    own, sums = call(
        functools.partial(square_kernel, devices), "square", None,
        (early_own, lax.all_to_all(joined, "pts", 0, 0), held.pop("rel")),
        [((12 * cols, D), F32), ((devices, 2, 128), F32)],
    )
    sums = lax.all_to_all(sums, ALL, 0, 0)
    cube, flat = [((count_mats, cols, D), F32)] * 3, [((LAYERS, width), F32)] * 3
    loss, grad_norm, *new = call(
        update_kernel, "update", None,
        (sums, own, *turned, *vecs, smalls, smalls_moment, smalls_second),
        [((1,), F32)] * 2 + cube + flat + [((cols, count_vecs), F32)] * 3,
    )
    return (
        loss.reshape(()), grad_norm.reshape(()),
        *[a.transpose(0, 2, 1) for a in new[:3]], *new[3:6], *[a.T for a in new[6:]],
    )


def solution(mesh):
    both = ("mesh", "pts")
    cube, flat = P(None, None, both), P(None, both)
    return jax.shard_map(
        per_device,
        mesh=mesh,
        in_specs=(flat, flat, P(both), cube, cube, cube, flat, flat, flat, flat, flat, flat),
        out_specs=(P(), P(), cube, cube, cube, flat, flat, flat, flat, flat, flat),
        check_vma=False,
    )
```

```python
import functools
import jax
import jax.numpy as jnp
from jax import lax
from jax.experimental import pallas as pl
from jax.experimental.pallas import tpu as pltpu
from jax.sharding import PartitionSpec as P

D = 256
H = 8
DH = 32
S = 64
HS = H * S
F_IN = 7
F_OUT = 4
LAYERS = 2
MESH_GRP = 4
STEP = 5
LOCALS = MESH_GRP - 1
WINDOW = 640
PART = 512
ND_ROWS = 40


EPS_NORM = 1e-05
EPS_SLICE = 1e-05
EPS_LOSS = 1e-06
CLIP = 0.01
LEARN = 0.03
BETA_ONE = 0.9
BETA_TWO = 0.95
EPS_ADAM = 1e-08
DECAY = 0.1
BF = jnp.bfloat16
F32 = jnp.float32
I32 = jnp.int32
ALL = ("mesh", "pts")
BASE = 9 * LAYERS


def dot(left, right):
    return jnp.dot(left, right, preferred_element_type=F32)


def dot_nt(left, right):
    return lax.dot_general(left, right, (((1,), (1,)), ((), ())), preferred_element_type=F32)


def dot_tn(left, right):
    return lax.dot_general(left, right, (((0,), (0,)), ((), ())), preferred_element_type=F32)


def low(value):
    return value.astype(BF)


def block_mask():
    rows = lax.broadcasted_iota(I32, (D, HS), 0) // DH
    cols = lax.broadcasted_iota(I32, (D, HS), 1) // S
    return rows == cols


def spread_blocks(compact):
    tall = jnp.concatenate([compact] * H, 0)
    return jnp.where(block_mask(), tall, jnp.zeros_like(tall))


def fold_blocks(full):
    lanes = lax.broadcasted_iota(I32, (DH, HS), 1) // S
    total = jnp.zeros((DH, HS), F32)
    for head in range(H):
        total = jnp.where(lanes == head, full[head * DH : (head + 1) * DH], total)
    return total


def pick_matrix():
    rows = lax.broadcasted_iota(I32, (S, HS), 0)
    cols = lax.broadcasted_iota(I32, (S, HS), 1) % S
    return (rows == cols).astype(F32).astype(BF)


def norm_stats(hidden):
    row_mean = jnp.sum(hidden, 0, keepdims=True) * (1.0 / D)
    centred = hidden - row_mean
    row_var = jnp.sum(centred * centred, 0, keepdims=True) * (1.0 / D)
    return centred, lax.rsqrt(row_var + EPS_NORM)


def norm_apply(hidden, gain, shift):
    centred, scale = norm_stats(hidden)
    return low(centred * scale * gain + shift)


def norm_back(grad, unit, scale, gain):
    inner = grad * gain
    first = jnp.sum(inner, 0, keepdims=True) * (1.0 / D)
    second = jnp.sum(inner * unit, 0, keepdims=True) * (1.0 / D)
    return scale * (inner - first - unit * second)


ROOT = 0.7978845608028654
CUBIC = 0.044715


def gelu(value):
    return 0.5 * value * (1.0 + jnp.tanh(ROOT * (value + CUBIC * (value * value * value))))


def gelu_both(value):
    square = value * value
    bend = jnp.tanh(ROOT * (value + CUBIC * (square * value)))
    half = 0.5 * (1.0 + bend)
    slope = half + 0.5 * value * (1.0 - bend * bend) * (ROOT * (1.0 + 3.0 * CUBIC * square))
    return value * half, slope


def lane_fold(value):
    total = value[:, :128]
    for start in range(128, value.shape[1], 128):
        total = total + value[:, start : start + 128]
    return total


def columns(sums):
    lanes = lax.broadcasted_iota(I32, (D, 128), 1)
    total = jnp.zeros((D, 128), F32)
    for index, value in sums:
        total = jnp.where(lanes == index, jnp.sum(value, 1, keepdims=True), total)
    return total


def slice_matrix(small):
    wide = jnp.concatenate([small[:, :S], small[:, :S]], 1)
    return spread_blocks(jnp.concatenate([wide] * (HS // (2 * S)), 1))


def slice_forward(num_dens, small):
    pick, mask = pick_matrix(), block_mask()
    tokens = [low(nd[:DH] / (nd[DH : DH + 1] + EPS_SLICE)) for nd in num_dens]
    mixed = [low(dot_tn(small[:, S:], t)) for t in tokens]
    keys = [low(dot_nt(pick, spread_blocks(m[DH : 2 * DH]))) for m in mixed]
    values = [low(dot_nt(spread_blocks(m[2 * DH :]), pick)) for m in mixed]
    scores = [dot(k, spread_blocks(m[:DH])) * DH ** (-0.5) for k, m in zip(keys, mixed)]
    raised = [jnp.exp(s - jnp.max(s, 0, keepdims=True)) for s in scores]
    attn = [r * (1.0 / jnp.sum(r, 0, keepdims=True)) for r in raised]
    full = [dot(v, low(a)) for v, a in zip(values, attn)]
    routed = [low(jnp.where(mask, f, jnp.zeros_like(f))) for f in full]
    return list(zip(routed, attn, tokens, mixed))


def widen(tall):
    pair = jnp.concatenate([tall, tall], 1)
    return fold_blocks(jnp.concatenate([pair] * (HS // (2 * S)), 1))


def slice_backward(d_slices, num_dens, attns, tokens, mixed, small):
    pick = pick_matrix()
    scale = DH ** (-0.5)
    lows = [low(a) for a in attns]
    d_full = [spread_blocks(d) for d in d_slices]
    query_full = [spread_blocks(m[:DH]) for m in mixed]
    values = [low(dot_nt(pick, spread_blocks(m[2 * DH :]))) for m in mixed]
    keys = [low(dot_nt(spread_blocks(m[DH : 2 * DH]), pick)) for m in mixed]
    d_attn = [dot(v, d) for v, d in zip(values, d_full)]
    d_values = [low(widen(dot_nt(d, a))) for d, a in zip(d_full, lows)]
    d_scores = [low(a * (d - jnp.sum(d * a, 0, keepdims=True))) for a, d in zip(attns, d_attn)]
    d_queries = [low(fold_blocks(dot(k, d)) * scale) for k, d in zip(keys, d_scores)]
    d_keys = [low(widen(dot_nt(q, d)) * scale) for q, d in zip(query_full, d_scores)]
    d_mixed = [jnp.concatenate(group, 0) for group in zip(d_queries, d_keys, d_values)]
    d_tokens = [dot(small[:, S:], d) for d in d_mixed]
    d_weight = [dot_nt(t, d) for t, d in zip(tokens, d_mixed)]
    inverse = [1.0 / (nd[DH : DH + 1] + EPS_SLICE) for nd in num_dens]
    d_num = [spread_blocks(low(d * i)) for d, i in zip(d_tokens, inverse)]
    d_den = [
        -jnp.sum(d * nd[:DH], 0, keepdims=True) * i * i for d, nd, i in zip(d_tokens, num_dens, inverse)
    ]
    return list(zip(d_num, d_den, d_weight))


def is_mesh(slot, mesh_id):
    return (slot == mesh_id).astype(F32)


def columns_at(vec, index):
    return vec[:, index : index + 1]


def sum_parts(parts):
    terms = [part[...].astype(F32) for part in parts]
    while len(terms) > 1:
        terms = [terms[i] + terms[i + 1] for i in range(0, len(terms), 2)]
    return terms[0]


def window(info, place, index, width):
    start = info[5 + place] + index * WINDOW
    at = pl.multiple_of(jnp.minimum(start, width - WINDOW), 128)
    return start, pl.ds(at, WINDOW)


def inside_of(info, place, slot, start, part):
    lanes = lax.broadcasted_iota(I32, (1, WINDOW), 1) + part.start
    mesh_id = info[2 + place]
    first = jnp.where(start == info[5 + place], 0, start)
    return ((slot[:, part] == mesh_id) & (lanes >= first)).astype(F32)


def each_window(info, slot, value, store, side_by_side=True):
    width = slot.shape[1]

    @pl.when(info[1] != 0)
    def _():
        found = []
        for place in range(LOCALS if side_by_side else 0):
            start, part = window(info, place, 0, width)
            found.append((part, value(place, part, inside_of(info, place, slot, start, part))))
        for place, (part, result) in enumerate(found):
            store(place, part, result)

        def more(place, carry):
            def step(index, carry):
                start, part = window(info, place, index, width)
                store(place, part, value(place, part, inside_of(info, place, slot, start, part)))
                return carry

            return lax.fori_loop(1 if side_by_side else 0, info[8 + place], step, carry)

        lax.fori_loop(0, LOCALS, more, 0)


def any_local(info, visit):
    @pl.when(info[1] != 0)
    def _():
        visit()


LATE = (0, 1, 5 * LAYERS)
EARLY = tuple(m for m in range(5 * LAYERS + 1) if m not in LATE)
SMALL_AT = 64
UNIT = 40


def put(early_ref, late_ref, matrix, value):
    ref, row = (late_ref, LATE.index(matrix)) if matrix in LATE else (early_ref, EARLY.index(matrix))
    devices, cols = ref.shape[0], D // ref.shape[0]
    ref[:, row * cols : (row + 1) * cols, :] = value.reshape(devices, cols, D)


def put_columns(late_ref, sums, fresh=False):
    devices, cols = late_ref.shape[0], D // late_ref.shape[0]
    value = columns(sums).reshape(devices, cols, 128)
    if not fresh:
        value = value + late_ref[:, len(LATE) * cols :, :128]
    late_ref[:, len(LATE) * cols :, :128] = value


def small_grad(slope, mixed):
    total = slope[:, :S]
    for head in range(1, H):
        total = total + slope[:, head * S : (head + 1) * S]
    return jnp.concatenate([total, mixed], 1)


def small_units(width, rows):
    step = min(width, UNIT)
    for k in range(LAYERS * width // step):
        yield k * step // width, k * step % width, k * step // UNIT, k * step % UNIT, step


def start_copies(sources, targets, sems, first):
    copies = [
        pltpu.make_async_copy(a, b, sems.at[first + j]) for j, (a, b) in enumerate(zip(sources, targets))
    ]
    for copy in copies:
        copy.start()
    return copies


def finish_copies(copies):
    for copy in copies:
        copy.wait()


def front(hidden, vec, layer, mats, small, slot, info, w_ref, nd_ref, send_ref, stage, far, sems):
    x_ref, f_ref, probs_ref = stage
    base = 9 * layer
    width = hidden.shape[1]
    u = norm_apply(hidden, columns_at(vec, base), columns_at(vec, base + 1))
    pair = dot(mats[5 * layer : 5 * layer + 2].reshape(2 * D, D), u)
    x_low = low(pair[:D] + columns_at(vec, base + 2))
    f_low = low(pair[D:] + columns_at(vec, base + 3))
    x_ref[...] = x_low
    f_ref[...] = f_low
    copies = start_copies(stage[:2], far[:2], sems, 0)
    logits = dot(slice_matrix(small[layer]).T, x_low).reshape(H, S, width)
    raised = jnp.exp(logits - jnp.max(logits, 1, keepdims=True))
    valid = (slot[...] < MESH_GRP).astype(F32)
    probs = (raised * (valid[None] / jnp.sum(raised, 1, keepdims=True))).reshape(HS, width)
    probs_ref[...] = probs
    copies = copies + start_copies(stage[2:], far[2:], sems, 2)
    w_low = low(probs)
    w_ref[...] = w_low

    def rows_of(features, mine):
        ones = jnp.broadcast_to(mine, (16, mine.shape[1]))
        return jnp.concatenate([low(features.astype(F32) * mine), low(ones)], 0)

    def compact(full):
        return jnp.concatenate([fold_blocks(full[:D]), full[D : D + ND_ROWS - DH]], 0)

    send_ref[...] = low(compact(dot_nt(rows_of(f_low, is_mesh(slot[...], info[0])), w_low)))

    nd_ref[...] = jnp.zeros_like(nd_ref)

    def value(place, part, mask):
        return compact(dot_nt(rows_of(f_ref[:, part], mask), w_ref[:, part]))

    def store(place, part, result):
        nd_ref[place] = nd_ref[place] + result

    each_window(info, slot, value, store)
    return copies


def back_half(w_in, slot, info, routed, routed_big, mix, hidden, vec, layer, mats):
    base = 9 * layer
    mix[...] = dot(routed_big[...], w_in[...]) * is_mesh(slot[...], info[0])

    def value(place, part, mask):
        return dot(routed[place], w_in[:, part]) * mask

    def store(place, part, result):
        mix[:, part] = mix[:, part] + result

    each_window(info, slot, value, store)
    y_low = low(mix[...])
    middle = hidden + dot(mats[5 * layer + 2], y_low) + columns_at(vec, base + 4)
    u2 = norm_apply(middle, columns_at(vec, base + 5), columns_at(vec, base + 6))
    pre = dot(mats[5 * layer + 3], u2) + columns_at(vec, base + 7)
    out = middle + dot(mats[5 * layer + 4], low(gelu(pre))) + columns_at(vec, base + 8)
    return y_low, middle, out


def head_half(grad, vec, layer, mats, middle, probs, y_low, slot, info, early_ref, late_ref, ds_ref, send_ref, acc, keep):
    base = 9 * layer
    d_y_ref, d_mid_ref = keep
    grad_low = low(grad)
    d_activ = dot_tn(mats[5 * layer + 4], grad_low)
    centred, scale = norm_stats(middle)
    unit = centred * scale
    gain = columns_at(vec, base + 5)
    u2 = low(unit * gain + columns_at(vec, base + 6))
    pre = dot(mats[5 * layer + 3], u2) + columns_at(vec, base + 7)
    sum_grad = lane_fold(grad)
    activ, slope = gelu_both(pre)
    d_pre = d_activ * slope
    d_pre_low = low(d_pre)
    d_norm = dot_tn(mats[5 * layer + 3], d_pre_low)
    put(early_ref, late_ref, 5 * layer + 4, dot_nt(grad_low, low(activ)))
    sum_pre = lane_fold(d_pre)
    d_mid = norm_back(d_norm, unit, scale, gain) + grad
    d_mid_low = low(d_mid)
    put(early_ref, late_ref, 5 * layer + 3, dot_nt(d_pre_low, u2))
    sum_unit = lane_fold(d_norm * unit)
    d_y = low(dot_tn(mats[5 * layer + 2], d_mid_low))
    sum_norm = lane_fold(d_norm)
    d_y_ref[...] = d_y
    put(early_ref, late_ref, 5 * layer + 2, dot_nt(d_mid_low, y_low))
    sum_mid = lane_fold(d_mid)
    d_mid_ref[...] = d_mid
    own = low(d_y.astype(F32) * is_mesh(slot[...], info[0]))
    send_ref[...] = low(fold_blocks(dot_nt(own, low(probs[...]))))

    acc[...] = jnp.zeros_like(acc)

    def value(place, part, mask):
        mine = low(d_y_ref[:, part].astype(F32) * mask)
        return fold_blocks(dot_nt(mine, low(probs[:, part])))

    def store(place, part, result):
        acc[place] = acc[place] + result

    each_window(info, slot, value, store)
    ds_ref[...] = low(acc[...])
    return [(base + 4, sum_mid), (base + 5, sum_unit), (base + 6, sum_norm), (base + 7, sum_pre), (base + 8, sum_grad)]


def tail_half(vec, layer, mats, small, hidden, x_in, f_in, probs_in, d_y, d_mid, slot, info,
              back, back_big, route, mix, grad_ref, early_ref, late_ref):
    width = hidden.shape[1]
    base = 9 * layer
    both_big, num_big, den_big = back_big
    both, d_num, d_den = back
    quarters = [slice(at, at + PART) for at in range(0, width, PART)]
    for part in quarters:
        mine = is_mesh(slot[:, part], info[0])
        pair = jnp.concatenate([d_y[:, part], f_in[:, part]], 0)
        route[:, part] = (dot(both_big, pair) + den_big) * mine
        mix[:, part] = dot(num_big, low(probs_in[:, part])) * mine

    def value(place, part, mask):
        piece = jnp.concatenate([d_y[:, part], f_in[:, part]], 0)
        through = (dot(both[place], piece) + d_den[place][:, :1]) * mask
        return through, dot(d_num[place], low(probs_in[:, part])) * mask

    def store(place, part, result):
        route[:, part] = route[:, part] + result[0]
        mix[:, part] = mix[:, part] + result[1]

    each_window(info, slot, value, store, False)
    gain, shift = columns_at(vec, base), columns_at(vec, base + 1)
    unslice = slice_matrix(small[layer])
    both_mats = mats[5 * layer : 5 * layer + 2].reshape(2 * D, D)
    totals = None
    for part in quarters:
        d_probs = route[:, part].reshape(H, S, PART)
        probs = probs_in[:, part].reshape(H, S, PART)
        spread = jnp.sum(d_probs * probs, 1, keepdims=True)
        d_logits = low(probs * (d_probs - spread)).reshape(HS, PART)
        d_x = dot(unslice, d_logits)
        d_f = mix[:, part]
        d_pair = jnp.concatenate([low(d_x), low(d_f)], 0)
        d_norm = dot_tn(both_mats, d_pair)
        centred, scale = norm_stats(hidden[:, part])
        unit = centred * scale
        u = low(unit * gain + shift)
        grad_ref[:, part] = norm_back(d_norm, unit, scale, gain) + d_mid[:, part]
        found = (
            dot_nt(x_in[:, part], d_logits), dot_nt(d_pair, u), lane_fold(d_norm * unit), lane_fold(d_norm),
            lane_fold(d_x), lane_fold(d_f),
        )
        totals = found if totals is None else tuple(t + f for t, f in zip(totals, found))
    slope, grads, *sums = totals
    put(early_ref, late_ref, 5 * layer, grads[:D])
    put(early_ref, late_ref, 5 * layer + 1, grads[D:])
    return [(base + j, value) for j, value in enumerate(sums)], fold_blocks(slope)


def embed_kernel(info, feat, slot, vec, mats, small,
                 h_ref, w_ref, nd_ref, send_ref, h_far, x_far, f_far, probs_far,
                 x_ref, f_ref, probs_ref, sems):
    we1 = low(vec[:, BASE + 4 : BASE + 4 + F_IN])
    e1 = dot(we1, low(feat[...])) + columns_at(vec, BASE)
    hidden = dot(mats[5 * LAYERS], low(gelu(e1))) + columns_at(vec, BASE + 1)
    h_ref[...] = hidden
    copies = start_copies([h_ref], [h_far], sems, 3)
    copies = copies + front(hidden, vec, 0, mats, small, slot, info, w_ref, nd_ref, send_ref,
                            (x_ref, f_ref, probs_ref), (x_far, f_far, probs_far), sems)
    finish_copies(copies)


def small_kernel(layer, info, nd_ref, small, routed_ref, routed_far, attn_far, tokens_far, mixed_far,
                 attn_ref, tokens_ref, mixed_ref, sems):
    stage = (routed_ref, attn_ref, tokens_ref, mixed_ref)
    far = (routed_far, attn_far, tokens_far, mixed_far)

    def visit():
        results = slice_forward([nd_ref[place] for place in range(LOCALS)], small[layer])
        for place in range(LOCALS):
            for ref, value in zip(stage, results[place]):
                ref[place] = value
        finish_copies(start_copies(stage, far, sems, 0))

    any_local(info, visit)


def share_start(parts, small, stage, far, sems, first):
    total = sum_parts(parts)
    for ref, value in zip(stage, slice_forward([total], small)[0] + (total,)):
        ref[...] = value
    return start_copies(stage, far, sems, first)


def middle_kernel(npts, info, *refs):
    parts, refs = refs[:npts], refs[npts:]
    (routed, w_in, h_in, slot, vec, mats, small,
     h_ref, w_ref, nd_ref, send_ref, *refs) = refs
    share_far, (y_far, m_far, h_far, x_far, f_far, probs_far), refs = refs[:5], refs[5:11], refs[11:]
    share, (y_ref, m_ref, x_ref, f_ref, probs_ref, mix, sems) = refs[:5], refs[5:]
    copies = share_start(parts, small[0], share, share_far, sems, 6)
    y_low, middle, out = back_half(w_in, slot, info, routed, share[0], mix, h_in[...], vec, 0, mats)
    y_ref[...] = y_low
    m_ref[...] = middle
    h_ref[...] = out
    copies = copies + start_copies((h_ref, y_ref, m_ref), (h_far, y_far, m_far), sems, 3)
    copies = copies + front(out, vec, 1, mats, small, slot, info, w_ref, nd_ref, send_ref,
                            (x_ref, f_ref, probs_ref), (x_far, f_far, probs_far), sems)
    finish_copies(copies)


def head_kernel(npts, info, *refs):
    parts, refs = refs[:npts], refs[npts:]
    (routed, w_in, h_in, slot, target, vec, mats, small,
     y_ref, m_ref, h_ref, diff_ref, loss_ref, *refs) = refs
    share_far, share, (mix, sems) = refs[:5], refs[5:10], refs[10:]
    copies = share_start(parts, small[1], share, share_far, sems, 0)
    y_low, middle, out = back_half(w_in, slot, info, routed, share[0], mix, h_in[...], vec, 1, mats)
    y_ref[...] = y_low
    m_ref[...] = middle
    h_ref[...] = out
    uh = norm_apply(out, columns_at(vec, BASE + 2), columns_at(vec, BASE + 3))
    truth = target[...]
    whd = low(vec[:, BASE + 4 + F_IN : BASE + 4 + F_IN + F_OUT])
    differ = dot_tn(whd, uh) - truth
    diff_ref[...] = differ
    ids = lax.broadcasted_iota(I32, differ.shape, 0)
    member = (ids == slot[...]).astype(F32)
    squares = jnp.sum(differ * differ, 0, keepdims=True)
    sizes = jnp.sum(truth * truth, 0, keepdims=True)
    both = lane_fold(jnp.concatenate([member * squares, member * sizes], 0))
    loss_ref[...] = jnp.broadcast_to(jnp.sum(both, 1, keepdims=True), loss_ref.shape)
    finish_copies(copies)


def loss_kernel(npts, groups, info, *refs):
    parts, refs = refs[:npts], refs[npts:]
    diff, slot, h_in, vec, grad_ref, rel_ref, early_ref, late_ref = refs
    whd = low(vec[:, BASE + 4 + F_IN : BASE + 4 + F_IN + F_OUT])
    total = sum_parts(parts)
    err_root = jnp.sqrt(total[:MESH_GRP] + EPS_LOSS)
    tgt_root = jnp.sqrt(total[MESH_GRP:] + EPS_LOSS)
    rel_ref[...] = jnp.concatenate([err_root / tgt_root, jnp.zeros_like(err_root)], 0)
    coef = (1.0 / (err_root * tgt_root) * (1.0 / (MESH_GRP * groups)))[:, :1]
    ids = lax.broadcasted_iota(I32, diff.shape, 0)
    member = (ids == slot[...]).astype(F32)
    d_pred = low(diff[...] * jnp.sum(member * coef, 0, keepdims=True))
    d_head = dot(whd, d_pred)
    centred, scale = norm_stats(h_in[...])
    unit = centred * scale
    gain = columns_at(vec, BASE + 2)
    g_whd = dot_nt(low(unit * gain + columns_at(vec, BASE + 3)), d_pred)
    put_columns(late_ref, [(BASE + 2, lane_fold(d_head * unit)), (BASE + 3, lane_fold(d_head))]
                + [(BASE + 4 + F_IN + j, g_whd[:, j : j + 1]) for j in range(F_OUT)], True)
    grad_ref[...] = norm_back(d_head, unit, scale, gain)


def half_kernel(layer, info, grad, middle, probs, y_low, slot, vec, mats, early_ref, late_ref,
                ds_ref, send_ref, d_y_ref, d_mid_ref, acc):
    sums = head_half(grad[...], vec, layer, mats, middle[...], probs, y_low[...], slot, info, early_ref, late_ref,
                     ds_ref, send_ref, acc, (d_y_ref, d_mid_ref))
    put_columns(late_ref, sums)


def small_back_kernel(layer, info, ds_in, nd_ref, attn, tokens, mixed, routed, small,
                      both_ref, dn_ref, den_ref, dw_ref):
    dw_ref[...] = jnp.zeros_like(dw_ref)

    def visit():
        tables = [[ref[place] for place in range(LOCALS)] for ref in (ds_in, nd_ref, attn, tokens, mixed)]
        results = slice_backward(*tables, small[layer])
        for place, (dn, den, dw) in enumerate(results):
            both_ref[place] = jnp.concatenate([routed[place], dn], 0).T
            dn_ref[place] = dn
            den_ref[place] = jnp.broadcast_to(den, (128, HS)).T
        dw_ref[...] = results[0][2] + results[1][2] + results[2][2]

    any_local(info, visit)


def tail_start(npts, parts, small, ndb, attn, tokens, mixed, routed_big, dw_in):
    total = low(sum_parts(parts))
    ((d_num, d_den, d_weight),) = slice_backward(
        *[[value] for value in (total, ndb[...], attn[...], tokens[...], mixed[...])], small
    )
    d_weight = dw_in[...] + d_weight * (1.0 / npts)
    both = jnp.concatenate([routed_big[...], d_num], 0).T
    return (both, d_num, jnp.broadcast_to(d_den, (128, HS)).T[:, :1]), d_weight


def tail_kernel(npts, layer, info, *refs):
    parts, refs = refs[:npts], refs[npts:]
    (both_in, dn_in, den_in, dw_in, ndb, attn, tokens, mixed, routed_big, small,
     h_in, x_in, f_in, probs, d_y, d_mid, slot, vec, mats, late_ref, *early,
     grad_ref, small_ref, route, mix) = refs
    back_big, d_weight = tail_start(npts, parts, small[layer], ndb, attn, tokens, mixed, routed_big, dw_in)
    sums, slope = tail_half(vec, layer, mats, small, h_in, x_in, f_in, probs, d_y, d_mid, slot, info,
                            (both_in, dn_in, den_in), back_big, route, mix, grad_ref,
                            early[0] if early else None, late_ref)
    small_ref[...] = small_grad(slope, d_weight)
    put_columns(late_ref, sums)


def last_kernel(grad_in, feat, vec, mats, small0, small1, late_ref, small_ref):
    feat_low = low(feat[...])
    we1 = low(vec[:, BASE + 4 : BASE + 4 + F_IN])
    activ, slope = gelu_both(dot(we1, feat_low) + columns_at(vec, BASE))
    grad = grad_in[...]
    grad_low = low(grad)
    d_embed = dot_tn(mats[5 * LAYERS], grad_low) * slope
    put(None, late_ref, 5 * LAYERS, dot_nt(grad_low, low(activ)))
    g_we1 = dot_nt(low(d_embed), feat_low)
    put_columns(late_ref, [(BASE, lane_fold(d_embed)), (BASE + 1, lane_fold(grad))]
                + [(BASE + 4 + j, g_we1[:, j : j + 1]) for j in range(F_IN)])
    small_ref[0] = small0[...]
    small_ref[1] = small1[...]
    cols = D // late_ref.shape[0]
    if cols * UNIT == 2 * (S + 3 * DH):
        for layer, column, row, lane, step in small_units(cols * UNIT // LAYERS, cols):
            late_ref[:, len(LATE) * cols + row, SMALL_AT + lane : SMALL_AT + lane + step] = (
                small_ref[layer, :, column : column + step]
            )


def pack_kernel(mats_in, vecs_in, smalls_in, block_ref, mats, vecs, smalls, sems):
    finish_copies(start_copies((mats_in, vecs_in, smalls_in), (mats, vecs, smalls), sems, 0))
    count, cols, _ = mats.shape
    block_ref[: count * cols] = low(mats[...].reshape(count * cols, D))
    block_ref[count * cols :] = jnp.zeros((cols, D), BF)
    block_ref[count * cols :, : vecs.shape[1]] = low(vecs[...])
    for layer, column, row, lane, step in small_units(smalls.shape[1], cols):
        block_ref[count * cols + row : count * cols + row + 1, SMALL_AT + lane : SMALL_AT + lane + step] = low(
            smalls[layer : layer + 1, column : column + step]
        )


def locals_kernel(place, slot, info_ref):
    points = slot.shape[1]
    lanes = lax.broadcasted_iota(I32, (1, points), 1).astype(F32)
    ids = slot[...]
    edge = jnp.where(place[0] == 0, points - 1, 0).astype(F32)
    big = jnp.sum(jnp.where(lanes == edge, ids.astype(F32), 0.0)).astype(I32)
    info_ref[0] = big
    total = 0
    for j in range(LOCALS):
        mesh_id = j + jnp.where(big <= j, 1, 0)
        mine = ids == mesh_id
        first = jnp.min(jnp.where(mine, lanes, float(points))).astype(I32)
        last = jnp.max(jnp.where(mine, lanes, -1.0)).astype(I32)
        start = jnp.minimum((first >> 7) << 7, points - WINDOW)
        count_j = jnp.where(last >= 0, lax.div(jnp.maximum(last - start, 0), WINDOW) + 1, 0)
        info_ref[2 + j] = jnp.where(last >= 0, mesh_id, -1)
        info_ref[5 + j] = start
        info_ref[8 + j] = count_j
        total = total + count_j
    info_ref[1] = total


def unpack_kernel(masks, place, *refs):
    pieces, (mats_ref, vecs_ref, *rest) = refs[: len(masks)], refs[len(masks) :]
    count, _, cols, _ = mats_ref.shape
    for mask, piece in zip(masks, pieces):
        for i in range(piece.shape[0]):
            for k in range(piece.shape[1]):
                at = (place[1] ^ (mask | (i << 1))) * piece.shape[1] + (place[0] ^ k)
                for m in range(count):
                    mats_ref[m, at] = piece[i, k, m * cols : (m + 1) * cols, :]
                vecs_ref[at] = piece[i, k, count * cols :, :].astype(F32)
    if rest:
        for layer, column, row, lane, step in small_units(cols * UNIT // LAYERS, cols):
            rest[0][layer, :, column : column + step] = low(vecs_ref[:, row, SMALL_AT + lane : SMALL_AT + lane + step])


def split_kernel(place, grads, send_ref):
    send_ref[...] = grads[:, 1 - (place[1] & 1)]


def fold_kernel(first, shift, place, *refs):
    terms, outs = refs
    index = (place[1] >> shift) & (len(outs) - 1)
    for k, out in enumerate(outs):
        total = None
        for j, term in enumerate(terms):
            value = term[index ^ k, :, place[1] & 1] if first and j == 0 else term[index ^ k]
            total = value if total is None else total + value
        out[...] = total


def join_kernel(counts, *refs):
    out, row = refs[-1], 0
    at = 0
    for count in counts:
        total = refs[at][...]
        for ref in refs[at + 1 : at + count]:
            total = total + ref[...]
        out[:, row : row + total.shape[1]] = total
        row, at = row + total.shape[1], at + count


def square_kernel(devices, early, late, rel, own_ref, sums_ref):
    wholes = []
    for parts in (early, late):
        total = parts[0]
        for j in range(1, parts.shape[0]):
            total = total + parts[j]
        wholes.append(total)
    own = jnp.concatenate(wholes, 0)
    own_ref[...] = own
    rows = lax.broadcasted_iota(I32, own.shape, 0)
    lanes = lax.broadcasted_iota(I32, own.shape, 1)
    edge = own.shape[0] // 12 * 11
    used = (rows < edge) | (lanes < BASE + 4 + F_IN + F_OUT) | ((lanes >= SMALL_AT) & (lanes < SMALL_AT + UNIT))
    squares = jnp.sum(jnp.where(used, own * own, 0.0))
    loss = jnp.sum(rel[:MESH_GRP, :1]) * (1.0 / (MESH_GRP * devices))
    which = lax.broadcasted_iota(I32, sums_ref.shape, 1)
    sums_ref[...] = jnp.where(which == 0, squares, loss)


def adamw(weight, moment, second, grad, factor):
    clipped = grad * factor
    moment = BETA_ONE * moment + (1.0 - BETA_ONE) * clipped
    second = BETA_TWO * second + (1.0 - BETA_TWO) * clipped * clipped
    moment_hat = moment / (1.0 - BETA_ONE**STEP)
    second_hat = second / (1.0 - BETA_TWO**STEP)
    updated = weight - LEARN * (moment_hat / (jnp.sqrt(second_hat) + EPS_ADAM) + DECAY * weight)
    return (moment, second, updated)


def update_kernel(sums, own, *refs):
    mats, vecs, smalls, outs = refs[:3], refs[3:6], refs[6:9], refs[9:]
    totals = jnp.sum(sums[...], 0)
    norm = jnp.sqrt(totals[:1, :1])
    factor = jnp.minimum(1.0, CLIP / norm)
    outs[0][0] = totals[1, 0]
    outs[1][0] = norm[0, 0]
    count, cols, _ = mats[0].shape
    for m in range(count):
        row = EARLY.index(m) if m in EARLY else len(EARLY) + LATE.index(m)
        for out, value in zip(outs[2:5], adamw(*[r[m] for r in mats], own[row * cols : (row + 1) * cols], factor)):
            out[m] = value
    grad = own[count * cols :, : vecs[0].shape[1]]
    for out, value in zip(outs[8:11], adamw(*[r[...] for r in vecs], grad, factor)):
        out[...] = value
    for layer, column, row, lane, step in small_units(smalls[0].shape[1], cols):
        grad = own[count * cols + row : count * cols + row + 1, SMALL_AT + lane : SMALL_AT + lane + step]
        old = [r[layer : layer + 1, column : column + step] for r in smalls]
        for out, value in zip(outs[5:8], adamw(*old, grad, factor)):
            out[layer : layer + 1, column : column + step] = value


LIMITS = dict(embed=14, small_fwd=5, middle=20, head=10, loss=8, half=20, small_bwd=4, tail=17, last=12,
              pack=3, locals=2, unpack=3, split=3, fold=3, join=3, square=3, update=4)
WORK = {}


def call(kernel, name, info, ins, outs, scratch=(), held=None, far=(), sems=0, nest=False, distant=False):
    near = len(outs)
    outs = list(outs) + list(far)
    held = {} if held is None else held
    names = list(held)
    plain = [a for a in ins if not isinstance(a, str)]
    inside = pl.BlockSpec(memory_space=pltpu.VMEM)
    table = [] if info is None else [info]
    first, second = len(table) + len(plain), len(table) + len(plain) + len(names)

    def body(*refs):
        rest = iter(refs[len(table) : first])
        kept = dict(zip(names, refs[first:second]))
        order = [kept[a] if isinstance(a, str) else next(rest) for a in ins]
        results = refs[second : second + len(outs)]
        after = refs[second + len(outs) + len(names) :]
        if nest:
            kernel(*refs[: len(table)], order, results)
        else:
            kernel(*refs[: len(table)], *order, *results, *after)

    res = pl.pallas_call(
        body,
        in_specs=[pl.BlockSpec(memory_space=pltpu.SMEM)] * len(table)
        + [pl.BlockSpec(memory_space=pltpu.HBM) if distant else inside] * (second - len(table)),
        out_specs=[
            pl.BlockSpec(memory_space=pltpu.SMEM) if len(shape) == 1 else inside for shape, _ in outs[:near]
        ]
        + [pl.BlockSpec(memory_space=pltpu.HBM)] * len(far)
        + [inside] * len(names),
        out_shape=[jax.ShapeDtypeStruct(s, t) for s, t in outs]
        + [jax.ShapeDtypeStruct(held[n].shape, held[n].dtype) for n in names],
        input_output_aliases={first + j: len(outs) + j for j in range(len(names))},
        scratch_shapes=[pltpu.VMEM(s, t) for s, t in scratch]
        + ([pltpu.SemaphoreType.DMA((sems,))] if sems else []),
        compiler_params=pltpu.CompilerParams(vmem_limit_bytes=LIMITS[name] * 2**20),
        cost_estimate=pl.CostEstimate(flops=WORK.get(name, 1000), bytes_accessed=1000, transcendentals=0),
        name=name,
    )(*table, *plain, *[held[n] for n in names])
    held.update(zip(names, res[len(outs) :]))
    return res[: len(outs)]


def swap(value, axis, mask):
    size = lax.axis_size(axis)
    return lax.ppermute(value, axis, [(i, i ^ mask) for i in range(size)])


def bit_groups(size):
    bits = size.bit_length() - 1
    groups, low = [], 1
    while low < bits:
        width = min(2, bits - low)
        groups.append((low, width))
        low += width
    return groups


def gather_pieces(block, beside):
    held = jnp.stack([block] + [swap(block, "pts", k) for k in range(1, lax.axis_size("pts"))])[None]
    held, beside = lax.optimization_barrier((held, beside))
    masks, pieces = [0], [held]
    for low, width in bit_groups(lax.axis_size("mesh")):
        held = jnp.concatenate(pieces)
        masks = [k << low for k in range(1 << width)]
        pieces = [held] + [swap(held, "mesh", m) for m in masks[1:]]
    return masks + [m | 1 for m in masks], pieces + [swap(p, "mesh", 1) for p in pieces], beside


def scatter_start(place, grads, later, gate=()):
    mesh_size, pts_size = lax.axis_size("mesh"), lax.axis_size("pts")
    rows = grads.shape[1]
    grads = grads.reshape(mesh_size // 2, 2, pts_size, rows, D)
    (send,) = call(split_kernel, "split", place, (grads,), [((mesh_size // 2, pts_size, rows, D), F32)])
    terms = [grads, swap(send, "mesh", 1)]
    terms[1], *gate = lax.optimization_barrier((terms[1], *gate))
    left = mesh_size // 2
    for number, (low, width) in enumerate(reversed(bit_groups(mesh_size))):
        count = 1 << width
        left //= count
        shape = (count, left, pts_size, rows, D)
        views = [t.reshape(shape) for t in terms[1:]]
        views = [terms[0].reshape((count, left, 2) + shape[2:] if number == 0 else shape)] + views
        pieces = call(
            functools.partial(fold_kernel, number == 0, low), "fold", place, views, [(shape[1:], F32)] * count,
            nest=True,
        )
        if number == 0:
            *pieces, later = lax.optimization_barrier((*pieces, later))
        terms = [pieces[0]] + [swap(p, "mesh", k << low) for k, p in enumerate(pieces) if k]
    return [t.reshape(pts_size, rows, D) for t in terms], later, gate


def per_device(
    features,
    targets,
    mesh_slot,
    matrices,
    matrices_moment,
    matrices_second,
    smalls,
    smalls_moment,
    smalls_second,
    vectors,
    vectors_moment,
    vectors_second,
):
    groups, npts = lax.axis_size("mesh"), lax.axis_size("pts")
    devices = groups * npts
    cols, width = matrices.shape[2], smalls.shape[1]
    points = mesh_slot.shape[0]
    count_mats, count_vecs = matrices.shape[0], vectors.shape[0]
    slot = mesh_slot[None]
    place = jnp.stack([lax.axis_index("pts"), lax.axis_index("mesh")]).astype(I32)
    turned = [a.transpose(0, 2, 1) for a in (matrices, matrices_moment, matrices_second)]
    vecs = [a.T for a in (vectors, vectors_moment, vectors_second)]
    sources = (turned[0], vecs[0], smalls)
    (block,) = call(
        pack_kernel, "pack", None, sources, [((12 * cols, D), BF)], [(a.shape, F32) for a in sources],
        sems=3, distant=True,
    )
    (info,) = call(locals_kernel, "locals", place, (slot,), [((16,), I32)])
    masks, pieces, info = gather_pieces(block, info)
    direct = cols * UNIT == 2 * (S + 3 * DH)
    mats, vec, *rest = call(
        functools.partial(unpack_kernel, masks), "unpack", place, pieces,
        [((count_mats, devices, cols, D), BF), ((devices, cols, D), F32)]
        + ([((LAYERS, DH, S + 3 * DH), BF)] if direct else []),
    )
    if direct:
        small = rest[0]
    else:
        small = vec[:, :, SMALL_AT : SMALL_AT + UNIT].reshape(devices, LAYERS, width).astype(BF)
        small = small.transpose(1, 0, 2).reshape(LAYERS, DH, S + 3 * DH)
    mats = mats.reshape(count_mats, D, D)
    vec = vec.reshape(D, D)

    wide = (D, points)
    tall = (HS, points)

    def exchange(value):
        return [value] + [swap(value, "pts", k) for k in range(1, npts)]

    held = {}

    def hold(**values):
        held.update(values)

    share = [((D, HS), BF), ((S, HS), F32), ((DH, HS), BF), ((3 * DH, HS), BF), ((ND_ROWS, HS), F32)]
    acts = [(wide, BF), (wide, BF), (tall, F32)]
    nears = [(wide, F32), (tall, BF), ((LOCALS, ND_ROWS, HS), F32), ((ND_ROWS, HS), BF)]
    few_out = [((LOCALS, D, HS), BF), ((LOCALS, S, HS), F32),
               ((LOCALS, DH, HS), BF), ((LOCALS, 3 * DH, HS), BF)]

    def small_call(nd, layer):
        routed, *rest = call(
            functools.partial(small_kernel, layer), "small_fwd", info, (nd, small),
            few_out[:1], few_out[1:], None, few_out, 4,
        )
        return routed, rest

    h0, w0, nd0, send, *acts0 = call(
        embed_kernel, "embed", info, (features, slot, vec, mats, small),
        nears, acts, None, [(wide, F32)] + acts, 4,
    )
    parts = exchange(send)
    routed, few0 = small_call(nd0, 0)
    h1, w1, nd1, send, *rest = call(
        functools.partial(middle_kernel, npts), "middle", info,
        (*parts, routed, w0, h0, slot, vec, mats, small),
        nears, share + [(wide, BF), (wide, F32)] + acts + [(wide, F32)], None,
        share + [(wide, BF), (wide, F32), (wide, F32)] + acts, 11,
    )
    share0, (y0, m0, *acts1) = rest[:5], rest[5:]

    parts = exchange(send)
    routed, few1 = small_call(nd1, 1)
    y1, m1, h2, diff, loss_part, *share1 = call(
        functools.partial(head_kernel, npts), "head", info,
        (*parts, routed, w1, h1, slot, targets, vec, mats, small),
        [(wide, BF), (wide, F32), (wide, F32), ((F_OUT, points), F32), ((8, 128), F32)],
        share + [(wide, F32)], None, share, 5,
    )
    hold(y1=y1, m1=m1)

    keeps = [(wide, BF), (wide, F32)]
    ds_out = [((LOCALS, DH, HS), BF), ((DH, HS), BF)]
    parts = exchange(loss_part)
    grad2, rel, early, late = call(
        functools.partial(loss_kernel, npts, groups), "loss", info,
        (*parts, diff, slot, h2, vec),
        [(wide, F32), ((8, 128), F32), ((devices, len(EARLY) * cols, D), F32),
         ((devices, (len(LATE) + 1) * cols, D), F32)], [], held,
    )
    hold(rel=rel, early=early, late=late)

    def half_call(layer, grad, middle, probs, y_low):
        res = call(
            functools.partial(half_kernel, layer), "half", info,
            (grad, middle, probs, y_low, slot, vec, mats, "early", "late"), ds_out + keeps, [((LOCALS, DH, HS), F32)], held,
        )
        return res[0], res[1], res[2:]

    def small_back(layer, ds, nd, few):
        return call(
            functools.partial(small_back_kernel, layer), "small_bwd", info,
            (ds, nd, few[1], few[2], few[3], few[0], small),
            [((LOCALS, HS, HS), BF), ((LOCALS, D, HS), BF),
             ((LOCALS, HS, 128), F32), ((DH, 3 * DH), F32)],
        )

    tail_scratch = [(tall, F32), (wide, F32)]

    def tail_ins(parts, back, keep, share, acts):
        return (*parts, *back, share[4], share[1], share[2], share[3], share[0], small, *acts, *keep, slot, vec, mats)

    ds, send, keep = half_call(1, grad2, held.pop("m1"), acts1[3], held.pop("y1"))
    parts = exchange(send)
    back = small_back(1, ds, nd1, few1)
    grad1, small1 = call(
        functools.partial(tail_kernel, npts, 1), "tail", info,
        (*tail_ins(parts, back, keep, share1, acts1), "late", "early"),
        [(wide, F32), ((DH, S + 3 * DH), F32)], tail_scratch, held,
    )
    ds, send, keep = half_call(0, grad1, m0, acts0[3], y0)
    parts = exchange(send)
    back = small_back(0, ds, nd0, few0)
    early_terms, after, gate = scatter_start(place, held.pop("early"), features, (*parts[1:], back[3]))
    parts, back = parts[:1] + gate[:-1], [*back[:3], gate[-1]]
    grad0, small0 = call(
        functools.partial(tail_kernel, npts, 0), "tail", info,
        (*tail_ins(parts, back, keep, share0, acts0), "late"),
        [(wide, F32), ((DH, S + 3 * DH), F32)], tail_scratch, held,
    )
    (joined,) = call(
        functools.partial(join_kernel, (len(early_terms),)), "join", None, early_terms,
        [((npts, len(EARLY) * cols, D), F32)],
    )
    joined, after = lax.optimization_barrier((joined, after))
    early_own = lax.all_to_all(joined, "pts", 0, 0)
    (small_out,) = call(
        last_kernel, "last", None, (grad0, after, vec, mats, small0, small1, "late"),
        [((LAYERS, DH, S + 3 * DH), F32)], (), held,
    )
    late = held.pop("late")
    if not direct:
        few = small_out.reshape(LAYERS, devices, width).transpose(1, 0, 2).reshape(devices, cols, UNIT)
        late = late.at[:, len(LATE) * cols :, SMALL_AT : SMALL_AT + UNIT].set(few)
    late_terms, *_ = scatter_start(place, late, after)
    (joined,) = call(
        functools.partial(join_kernel, (len(late_terms),)), "join", None, late_terms,
        [((npts, (len(LATE) + 1) * cols, D), F32)],
    )
    own, sums = call(
        functools.partial(square_kernel, devices), "square", None,
        (early_own, lax.all_to_all(joined, "pts", 0, 0), held.pop("rel")),
        [((12 * cols, D), F32), ((devices, 2, 128), F32)],
    )
    sums = lax.all_to_all(sums, ALL, 0, 0)
    cube, flat = [((count_mats, cols, D), F32)] * 3, [((LAYERS, width), F32)] * 3
    loss, grad_norm, *new = call(
        update_kernel, "update", None,
        (sums, own, *turned, *vecs, smalls, smalls_moment, smalls_second),
        [((1,), F32)] * 2 + cube + flat + [((cols, count_vecs), F32)] * 3,
    )
    return (
        loss.reshape(()), grad_norm.reshape(()),
        *[a.transpose(0, 2, 1) for a in new[:3]], *new[3:6], *[a.T for a in new[6:]],
    )


def solution(mesh):
    both = ("mesh", "pts")
    cube, flat = P(None, None, both), P(None, both)
    return jax.shard_map(
        per_device,
        mesh=mesh,
        in_specs=(flat, flat, P(both), cube, cube, cube, flat, flat, flat, flat, flat, flat),
        out_specs=(P(), P(), cube, cube, cube, flat, flat, flat, flat, flat, flat),
        check_vma=False,
    )
```

```python
import functools
import jax
import jax.numpy as jnp
from jax import lax
from jax.experimental import pallas as pl
from jax.experimental.pallas import tpu as pltpu
from jax.sharding import PartitionSpec as P

D = 256
H = 8
DH = 32
S = 64
HS = H * S
F_IN = 7
F_OUT = 4
LAYERS = 2
MESH_GRP = 4
STEP = 5
LOCALS = MESH_GRP - 1
WINDOW = 640
PART = 512
ND_ROWS = 40


EPS_NORM = 1e-05
EPS_SLICE = 1e-05
EPS_LOSS = 1e-06
CLIP = 0.01
LEARN = 0.03
BETA_ONE = 0.9
BETA_TWO = 0.95
EPS_ADAM = 1e-08
DECAY = 0.1
BF = jnp.bfloat16
F32 = jnp.float32
I32 = jnp.int32
ALL = ("mesh", "pts")
BASE = 9 * LAYERS


def dot(left, right):
    return jnp.dot(left, right, preferred_element_type=F32)


def dot_nt(left, right):
    return lax.dot_general(left, right, (((1,), (1,)), ((), ())), preferred_element_type=F32)


def dot_tn(left, right):
    return lax.dot_general(left, right, (((0,), (0,)), ((), ())), preferred_element_type=F32)


def low(value):
    return value.astype(BF)


def block_mask():
    rows = lax.broadcasted_iota(I32, (D, HS), 0) // DH
    cols = lax.broadcasted_iota(I32, (D, HS), 1) // S
    return rows == cols


def spread_blocks(compact):
    tall = jnp.concatenate([compact] * H, 0)
    return jnp.where(block_mask(), tall, jnp.zeros_like(tall))


def fold_blocks(full):
    lanes = lax.broadcasted_iota(I32, (DH, HS), 1) // S
    total = jnp.zeros((DH, HS), F32)
    for head in range(H):
        total = jnp.where(lanes == head, full[head * DH : (head + 1) * DH], total)
    return total


def pick_matrix():
    rows = lax.broadcasted_iota(I32, (S, HS), 0)
    cols = lax.broadcasted_iota(I32, (S, HS), 1) % S
    return (rows == cols).astype(F32).astype(BF)


def norm_stats(hidden):
    row_mean = jnp.sum(hidden, 0, keepdims=True) * (1.0 / D)
    centred = hidden - row_mean
    row_var = jnp.sum(centred * centred, 0, keepdims=True) * (1.0 / D)
    return centred, lax.rsqrt(row_var + EPS_NORM)


def norm_apply(hidden, gain, shift):
    centred, scale = norm_stats(hidden)
    return low(centred * scale * gain + shift)


def norm_back(grad, unit, scale, gain):
    inner = grad * gain
    first = jnp.sum(inner, 0, keepdims=True) * (1.0 / D)
    second = jnp.sum(inner * unit, 0, keepdims=True) * (1.0 / D)
    return scale * (inner - first - unit * second)


ROOT = 0.7978845608028654
CUBIC = 0.044715


def gelu(value):
    return 0.5 * value * (1.0 + jnp.tanh(ROOT * (value + CUBIC * (value * value * value))))


def gelu_both(value):
    square = value * value
    bend = jnp.tanh(ROOT * (value + CUBIC * (square * value)))
    half = 0.5 * (1.0 + bend)
    slope = half + 0.5 * value * (1.0 - bend * bend) * (ROOT * (1.0 + 3.0 * CUBIC * square))
    return value * half, slope


def lane_fold(value):
    total = value[:, :128]
    for start in range(128, value.shape[1], 128):
        total = total + value[:, start : start + 128]
    return total


def columns(sums):
    lanes = lax.broadcasted_iota(I32, (D, 128), 1)
    total = jnp.zeros((D, 128), F32)
    for index, value in sums:
        total = jnp.where(lanes == index, jnp.sum(value, 1, keepdims=True), total)
    return total


def slice_matrix(small):
    wide = jnp.concatenate([small[:, :S], small[:, :S]], 1)
    return spread_blocks(jnp.concatenate([wide] * (HS // (2 * S)), 1))


def slice_forward(num_dens, small):
    pick, mask = pick_matrix(), block_mask()
    tokens = [low(nd[:DH] / (nd[DH : DH + 1] + EPS_SLICE)) for nd in num_dens]
    mixed = [low(dot_tn(small[:, S:], t)) for t in tokens]
    keys = [low(dot_nt(pick, spread_blocks(m[DH : 2 * DH]))) for m in mixed]
    values = [low(dot_nt(spread_blocks(m[2 * DH :]), pick)) for m in mixed]
    scores = [dot(k, spread_blocks(m[:DH])) * DH ** (-0.5) for k, m in zip(keys, mixed)]
    raised = [jnp.exp(s - jnp.max(s, 0, keepdims=True)) for s in scores]
    attn = [r * (1.0 / jnp.sum(r, 0, keepdims=True)) for r in raised]
    full = [dot(v, low(a)) for v, a in zip(values, attn)]
    routed = [low(jnp.where(mask, f, jnp.zeros_like(f))) for f in full]
    return list(zip(routed, attn, tokens, mixed))


def widen(tall):
    pair = jnp.concatenate([tall, tall], 1)
    return fold_blocks(jnp.concatenate([pair] * (HS // (2 * S)), 1))


def slice_backward(d_slices, num_dens, attns, tokens, mixed, small):
    pick = pick_matrix()
    scale = DH ** (-0.5)
    lows = [low(a) for a in attns]
    d_full = [spread_blocks(d) for d in d_slices]
    query_full = [spread_blocks(m[:DH]) for m in mixed]
    values = [low(dot_nt(pick, spread_blocks(m[2 * DH :]))) for m in mixed]
    keys = [low(dot_nt(spread_blocks(m[DH : 2 * DH]), pick)) for m in mixed]
    d_attn = [dot(v, d) for v, d in zip(values, d_full)]
    d_values = [low(widen(dot_nt(d, a))) for d, a in zip(d_full, lows)]
    d_scores = [low(a * (d - jnp.sum(d * a, 0, keepdims=True))) for a, d in zip(attns, d_attn)]
    d_queries = [low(fold_blocks(dot(k, d)) * scale) for k, d in zip(keys, d_scores)]
    d_keys = [low(widen(dot_nt(q, d)) * scale) for q, d in zip(query_full, d_scores)]
    d_mixed = [jnp.concatenate(group, 0) for group in zip(d_queries, d_keys, d_values)]
    d_tokens = [dot(small[:, S:], d) for d in d_mixed]
    d_weight = [dot_nt(t, d) for t, d in zip(tokens, d_mixed)]
    inverse = [1.0 / (nd[DH : DH + 1] + EPS_SLICE) for nd in num_dens]
    d_num = [spread_blocks(low(d * i)) for d, i in zip(d_tokens, inverse)]
    d_den = [
        -jnp.sum(d * nd[:DH], 0, keepdims=True) * i * i for d, nd, i in zip(d_tokens, num_dens, inverse)
    ]
    return list(zip(d_num, d_den, d_weight))


def is_mesh(slot, mesh_id):
    return (slot == mesh_id).astype(F32)


def columns_at(vec, index):
    return vec[:, index : index + 1]


def sum_parts(parts):
    terms = [part[...].astype(F32) for part in parts]
    while len(terms) > 1:
        terms = [terms[i] + terms[i + 1] for i in range(0, len(terms), 2)]
    return terms[0]


def window(info, place, index, width):
    start = info[5 + place] + index * WINDOW
    at = pl.multiple_of(jnp.minimum(start, width - WINDOW), 128)
    return start, pl.ds(at, WINDOW)


def inside_of(info, place, slot, start, part):
    lanes = lax.broadcasted_iota(I32, (1, WINDOW), 1) + part.start
    mesh_id = info[2 + place]
    first = jnp.where(start == info[5 + place], 0, start)
    return ((slot[:, part] == mesh_id) & (lanes >= first)).astype(F32)


def each_window(info, slot, value, store, side_by_side=True):
    width = slot.shape[1]

    @pl.when(info[1] != 0)
    def _():
        found = []
        for place in range(LOCALS if side_by_side else 0):
            start, part = window(info, place, 0, width)
            found.append((part, value(place, part, inside_of(info, place, slot, start, part))))
        for place, (part, result) in enumerate(found):
            store(place, part, result)

        def more(place, carry):
            def step(index, carry):
                start, part = window(info, place, index, width)
                store(place, part, value(place, part, inside_of(info, place, slot, start, part)))
                return carry

            return lax.fori_loop(1 if side_by_side else 0, info[8 + place], step, carry)

        lax.fori_loop(0, LOCALS, more, 0)


def any_local(info, visit):
    @pl.when(info[1] != 0)
    def _():
        visit()


LATE = (0, 1, 5 * LAYERS)
EARLY = tuple(m for m in range(5 * LAYERS + 1) if m not in LATE)
SMALL_AT = 64
UNIT = 40


def put(early_ref, late_ref, matrix, value):
    ref, row = (late_ref, LATE.index(matrix)) if matrix in LATE else (early_ref, EARLY.index(matrix))
    devices, cols = ref.shape[0], D // ref.shape[0]
    ref[:, row * cols : (row + 1) * cols, :] = value.reshape(devices, cols, D)


def put_columns(late_ref, sums, fresh=False):
    devices, cols = late_ref.shape[0], D // late_ref.shape[0]
    value = columns(sums).reshape(devices, cols, 128)
    if not fresh:
        value = value + late_ref[:, len(LATE) * cols :, :128]
    late_ref[:, len(LATE) * cols :, :128] = value


def small_grad(slope, mixed):
    total = slope[:, :S]
    for head in range(1, H):
        total = total + slope[:, head * S : (head + 1) * S]
    return jnp.concatenate([total, mixed], 1)


def small_units(width, rows):
    step = min(width, UNIT)
    for k in range(LAYERS * width // step):
        yield k * step // width, k * step % width, k * step // UNIT, k * step % UNIT, step


def start_copies(sources, targets, sems, first):
    copies = [
        pltpu.make_async_copy(a, b, sems.at[first + j]) for j, (a, b) in enumerate(zip(sources, targets))
    ]
    for copy in copies:
        copy.start()
    return copies


def finish_copies(copies):
    for copy in copies:
        copy.wait()


def front(hidden, vec, layer, mats, small, slot, info, w_ref, nd_ref, send_ref, stage, far, sems):
    x_ref, f_ref, probs_ref = stage
    base = 9 * layer
    width = hidden.shape[1]
    u = norm_apply(hidden, columns_at(vec, base), columns_at(vec, base + 1))
    pair = dot(mats[5 * layer : 5 * layer + 2].reshape(2 * D, D), u)
    x_low = low(pair[:D] + columns_at(vec, base + 2))
    f_low = low(pair[D:] + columns_at(vec, base + 3))
    x_ref[...] = x_low
    f_ref[...] = f_low
    copies = start_copies(stage[:2], far[:2], sems, 0)
    logits = dot(slice_matrix(small[layer]).T, x_low).reshape(H, S, width)
    raised = jnp.exp(logits - jnp.max(logits, 1, keepdims=True))
    valid = (slot[...] < MESH_GRP).astype(F32)
    probs = (raised * (valid[None] / jnp.sum(raised, 1, keepdims=True))).reshape(HS, width)
    probs_ref[...] = probs
    w_low = low(probs)
    w_ref[...] = w_low

    def rows_of(features, mine):
        ones = jnp.broadcast_to(mine, (16, mine.shape[1]))
        return jnp.concatenate([low(features.astype(F32) * mine), low(ones)], 0)

    def compact(full):
        return jnp.concatenate([fold_blocks(full[:D]), full[D : D + ND_ROWS - DH]], 0)

    send_ref[...] = low(compact(dot_nt(rows_of(f_low, is_mesh(slot[...], info[0])), w_low)))

    nd_ref[...] = jnp.zeros_like(nd_ref)

    def value(place, part, mask):
        return compact(dot_nt(rows_of(f_ref[:, part], mask), w_ref[:, part]))

    def store(place, part, result):
        nd_ref[place] = nd_ref[place] + result

    each_window(info, slot, value, store)
    return copies


def back_half(w_in, slot, info, routed, routed_big, mix, hidden, vec, layer, mats):
    base = 9 * layer
    mix[...] = dot(routed_big[...], w_in[...]) * is_mesh(slot[...], info[0])

    def value(place, part, mask):
        return dot(routed[place], w_in[:, part]) * mask

    def store(place, part, result):
        mix[:, part] = mix[:, part] + result

    each_window(info, slot, value, store)
    y_low = low(mix[...])
    middle = hidden + dot(mats[5 * layer + 2], y_low) + columns_at(vec, base + 4)
    u2 = norm_apply(middle, columns_at(vec, base + 5), columns_at(vec, base + 6))
    pre = dot(mats[5 * layer + 3], u2) + columns_at(vec, base + 7)
    out = middle + dot(mats[5 * layer + 4], low(gelu(pre))) + columns_at(vec, base + 8)
    return y_low, middle, out


def head_half(grad, vec, layer, mats, middle, probs, y_low, slot, info, early_ref, late_ref, ds_ref, send_ref, acc, keep):
    base = 9 * layer
    d_y_ref, d_mid_ref = keep
    grad_low = low(grad)
    d_activ = dot_tn(mats[5 * layer + 4], grad_low)
    centred, scale = norm_stats(middle)
    unit = centred * scale
    gain = columns_at(vec, base + 5)
    u2 = low(unit * gain + columns_at(vec, base + 6))
    pre = dot(mats[5 * layer + 3], u2) + columns_at(vec, base + 7)
    sum_grad = lane_fold(grad)
    activ, slope = gelu_both(pre)
    d_pre = d_activ * slope
    d_pre_low = low(d_pre)
    d_norm = dot_tn(mats[5 * layer + 3], d_pre_low)
    put(early_ref, late_ref, 5 * layer + 4, dot_nt(grad_low, low(activ)))
    sum_pre = lane_fold(d_pre)
    d_mid = norm_back(d_norm, unit, scale, gain) + grad
    d_mid_low = low(d_mid)
    put(early_ref, late_ref, 5 * layer + 3, dot_nt(d_pre_low, u2))
    sum_unit = lane_fold(d_norm * unit)
    d_y = low(dot_tn(mats[5 * layer + 2], d_mid_low))
    sum_norm = lane_fold(d_norm)
    d_y_ref[...] = d_y
    put(early_ref, late_ref, 5 * layer + 2, dot_nt(d_mid_low, y_low))
    sum_mid = lane_fold(d_mid)
    d_mid_ref[...] = d_mid
    own = low(d_y.astype(F32) * is_mesh(slot[...], info[0]))
    send_ref[...] = low(fold_blocks(dot_nt(own, low(probs[...]))))

    acc[...] = jnp.zeros_like(acc)

    def value(place, part, mask):
        mine = low(d_y_ref[:, part].astype(F32) * mask)
        return fold_blocks(dot_nt(mine, low(probs[:, part])))

    def store(place, part, result):
        acc[place] = acc[place] + result

    each_window(info, slot, value, store)
    ds_ref[...] = low(acc[...])
    return [(base + 4, sum_mid), (base + 5, sum_unit), (base + 6, sum_norm), (base + 7, sum_pre), (base + 8, sum_grad)]


def tail_half(vec, layer, mats, small, hidden, x_in, f_in, probs_in, d_y, d_mid, slot, info,
              back, back_big, route, mix, grad_ref, early_ref, late_ref):
    width = hidden.shape[1]
    base = 9 * layer
    both_big, num_big, den_big = back_big
    both, d_num, d_den = back
    quarters = [slice(at, at + PART) for at in range(0, width, PART)]
    for part in quarters:
        mine = is_mesh(slot[:, part], info[0])
        pair = jnp.concatenate([d_y[:, part], f_in[:, part]], 0)
        route[:, part] = (dot(both_big, pair) + den_big) * mine
        mix[:, part] = dot(num_big, low(probs_in[:, part])) * mine

    def value(place, part, mask):
        piece = jnp.concatenate([d_y[:, part], f_in[:, part]], 0)
        through = (dot(both[place], piece) + d_den[place][:, :1]) * mask
        return through, dot(d_num[place], low(probs_in[:, part])) * mask

    def store(place, part, result):
        route[:, part] = route[:, part] + result[0]
        mix[:, part] = mix[:, part] + result[1]

    each_window(info, slot, value, store, False)
    gain, shift = columns_at(vec, base), columns_at(vec, base + 1)
    unslice = slice_matrix(small[layer])
    both_mats = mats[5 * layer : 5 * layer + 2].reshape(2 * D, D)
    totals = None
    for part in quarters:
        d_probs = route[:, part].reshape(H, S, PART)
        probs = probs_in[:, part].reshape(H, S, PART)
        spread = jnp.sum(d_probs * probs, 1, keepdims=True)
        d_logits = low(probs * (d_probs - spread)).reshape(HS, PART)
        d_x = dot(unslice, d_logits)
        d_f = mix[:, part]
        d_pair = jnp.concatenate([low(d_x), low(d_f)], 0)
        d_norm = dot_tn(both_mats, d_pair)
        centred, scale = norm_stats(hidden[:, part])
        unit = centred * scale
        u = low(unit * gain + shift)
        grad_ref[:, part] = norm_back(d_norm, unit, scale, gain) + d_mid[:, part]
        found = (
            dot_nt(x_in[:, part], d_logits), dot_nt(d_pair, u), lane_fold(d_norm * unit), lane_fold(d_norm),
            lane_fold(d_x), lane_fold(d_f),
        )
        totals = found if totals is None else tuple(t + f for t, f in zip(totals, found))
    slope, grads, *sums = totals
    put(early_ref, late_ref, 5 * layer, grads[:D])
    put(early_ref, late_ref, 5 * layer + 1, grads[D:])
    return [(base + j, value) for j, value in enumerate(sums)], fold_blocks(slope)


def embed_kernel(info, feat, slot, vec, mats, small,
                 h_ref, w_ref, nd_ref, send_ref, probs_ref, h_far, x_far, f_far, x_ref, f_ref, sems):
    we1 = low(vec[:, BASE + 4 : BASE + 4 + F_IN])
    e1 = dot(we1, low(feat[...])) + columns_at(vec, BASE)
    hidden = dot(mats[5 * LAYERS], low(gelu(e1))) + columns_at(vec, BASE + 1)
    h_ref[...] = hidden
    copies = start_copies([h_ref], [h_far], sems, 3)
    copies = copies + front(hidden, vec, 0, mats, small, slot, info, w_ref, nd_ref, send_ref,
                            (x_ref, f_ref, probs_ref), (x_far, f_far), sems)
    finish_copies(copies)


def small_kernel(layer, info, nd_ref, small, routed_ref, routed_far, attn_far, tokens_far, mixed_far,
                 attn_ref, tokens_ref, mixed_ref, sems):
    stage = (routed_ref, attn_ref, tokens_ref, mixed_ref)
    far = (routed_far, attn_far, tokens_far, mixed_far)

    def visit():
        results = slice_forward([nd_ref[place] for place in range(LOCALS)], small[layer])
        for place in range(LOCALS):
            for ref, value in zip(stage, results[place]):
                ref[place] = value
        finish_copies(start_copies(stage, far, sems, 0))

    any_local(info, visit)


def share_start(parts, small, stage, far, sems, first):
    total = sum_parts(parts)
    for ref, value in zip(stage, slice_forward([total], small)[0] + (total,)):
        ref[...] = value
    return start_copies(stage, far, sems, first)


def middle_kernel(npts, info, *refs):
    parts, refs = refs[:npts], refs[npts:]
    (routed, w_in, h_in, probs_in, slot, vec, mats, small,
     h_ref, w_ref, nd_ref, send_ref, probs_ref, *refs) = refs
    share_far, (y_far, m_far, h_far, x_far, f_far, probs_far), refs = refs[:5], refs[5:11], refs[11:]
    share, (y_ref, m_ref, x_ref, f_ref, mix, sems) = refs[:5], refs[5:]
    copies = start_copies([probs_in], [probs_far], sems, 2)
    copies = copies + share_start(parts, small[0], share, share_far, sems, 6)
    y_low, middle, out = back_half(w_in, slot, info, routed, share[0], mix, h_in[...], vec, 0, mats)
    y_ref[...] = y_low
    m_ref[...] = middle
    h_ref[...] = out
    copies = copies + start_copies((h_ref, y_ref, m_ref), (h_far, y_far, m_far), sems, 3)
    copies = copies + front(out, vec, 1, mats, small, slot, info, w_ref, nd_ref, send_ref,
                            (x_ref, f_ref, probs_ref), (x_far, f_far), sems)
    finish_copies(copies)


def head_kernel(npts, info, *refs):
    parts, refs = refs[:npts], refs[npts:]
    (routed, w_in, h_in, probs_in, slot, target, vec, mats, small,
     y_ref, m_ref, h_ref, diff_ref, loss_ref, *refs) = refs
    probs_far, share_far, share, (mix, sems) = refs[0], refs[1:6], refs[6:11], refs[11:]
    copies = start_copies([probs_in], [probs_far], sems, 5)
    copies = copies + share_start(parts, small[1], share, share_far, sems, 0)
    y_low, middle, out = back_half(w_in, slot, info, routed, share[0], mix, h_in[...], vec, 1, mats)
    y_ref[...] = y_low
    m_ref[...] = middle
    h_ref[...] = out
    uh = norm_apply(out, columns_at(vec, BASE + 2), columns_at(vec, BASE + 3))
    truth = target[...]
    whd = low(vec[:, BASE + 4 + F_IN : BASE + 4 + F_IN + F_OUT])
    differ = dot_tn(whd, uh) - truth
    diff_ref[...] = differ
    ids = lax.broadcasted_iota(I32, differ.shape, 0)
    member = (ids == slot[...]).astype(F32)
    squares = jnp.sum(differ * differ, 0, keepdims=True)
    sizes = jnp.sum(truth * truth, 0, keepdims=True)
    both = lane_fold(jnp.concatenate([member * squares, member * sizes], 0))
    loss_ref[...] = jnp.broadcast_to(jnp.sum(both, 1, keepdims=True), loss_ref.shape)
    finish_copies(copies)


def loss_kernel(npts, groups, info, *refs):
    parts, refs = refs[:npts], refs[npts:]
    diff, slot, h_in, vec, grad_ref, rel_ref, early_ref, late_ref = refs
    whd = low(vec[:, BASE + 4 + F_IN : BASE + 4 + F_IN + F_OUT])
    total = sum_parts(parts)
    err_root = jnp.sqrt(total[:MESH_GRP] + EPS_LOSS)
    tgt_root = jnp.sqrt(total[MESH_GRP:] + EPS_LOSS)
    rel_ref[...] = jnp.concatenate([err_root / tgt_root, jnp.zeros_like(err_root)], 0)
    coef = (1.0 / (err_root * tgt_root) * (1.0 / (MESH_GRP * groups)))[:, :1]
    ids = lax.broadcasted_iota(I32, diff.shape, 0)
    member = (ids == slot[...]).astype(F32)
    d_pred = low(diff[...] * jnp.sum(member * coef, 0, keepdims=True))
    d_head = dot(whd, d_pred)
    centred, scale = norm_stats(h_in[...])
    unit = centred * scale
    gain = columns_at(vec, BASE + 2)
    g_whd = dot_nt(low(unit * gain + columns_at(vec, BASE + 3)), d_pred)
    put_columns(late_ref, [(BASE + 2, lane_fold(d_head * unit)), (BASE + 3, lane_fold(d_head))]
                + [(BASE + 4 + F_IN + j, g_whd[:, j : j + 1]) for j in range(F_OUT)], True)
    grad_ref[...] = norm_back(d_head, unit, scale, gain)


def hand_other(info, grads_ref, out_ref):
    npts = out_ref.shape[1]
    for i in range(out_ref.shape[0]):
        out_ref[i] = grads_ref[pl.ds((2 * i + 1 - info[13]) * npts, npts)]


def half_kernel(layer, info, grad, middle, probs, y_low, slot, vec, mats, early_ref, late_ref,
                ds_ref, send_ref, d_y_ref, d_mid_ref, *rest):
    *other, acc = rest
    sums = head_half(grad[...], vec, layer, mats, middle[...], probs, y_low[...], slot, info, early_ref, late_ref,
                     ds_ref, send_ref, acc, (d_y_ref, d_mid_ref))
    put_columns(late_ref, sums)
    for ref in other:
        hand_other(info, early_ref, ref)


def small_back_kernel(layer, info, ds_in, nd_ref, attn, tokens, mixed, routed, small,
                      both_ref, dn_ref, den_ref, dw_ref):
    dw_ref[...] = jnp.zeros_like(dw_ref)

    def visit():
        tables = [[ref[place] for place in range(LOCALS)] for ref in (ds_in, nd_ref, attn, tokens, mixed)]
        results = slice_backward(*tables, small[layer])
        for place, (dn, den, dw) in enumerate(results):
            both_ref[place] = jnp.concatenate([routed[place], dn], 0).T
            dn_ref[place] = dn
            den_ref[place] = jnp.broadcast_to(den, (128, HS)).T
        dw_ref[...] = results[0][2] + results[1][2] + results[2][2]

    any_local(info, visit)


def tail_start(npts, parts, small, ndb, attn, tokens, mixed, routed_big, dw_in):
    total = low(sum_parts(parts))
    ((d_num, d_den, d_weight),) = slice_backward(
        *[[value] for value in (total, ndb[...], attn[...], tokens[...], mixed[...])], small
    )
    d_weight = dw_in[...] + d_weight * (1.0 / npts)
    both = jnp.concatenate([routed_big[...], d_num], 0).T
    return (both, d_num, jnp.broadcast_to(d_den, (128, HS)).T[:, :1]), d_weight


def tail_kernel(npts, layer, info, *refs):
    parts, refs = refs[:npts], refs[npts:]
    (both_in, dn_in, den_in, dw_in, ndb, attn, tokens, mixed, routed_big, small,
     h_in, x_in, f_in, probs, d_y, d_mid, slot, vec, mats, late_ref, *early,
     grad_ref, small_ref, route, mix) = refs
    back_big, d_weight = tail_start(npts, parts, small[layer], ndb, attn, tokens, mixed, routed_big, dw_in)
    sums, slope = tail_half(vec, layer, mats, small, h_in, x_in, f_in, probs, d_y, d_mid, slot, info,
                            (both_in, dn_in, den_in), back_big, route, mix, grad_ref,
                            early[0] if early else None, late_ref)
    small_ref[...] = small_grad(slope, d_weight)
    put_columns(late_ref, sums)


def last_kernel(info, grad_in, feat, vec, mats, small0, small1, late_ref, small_ref, *other):
    feat_low = low(feat[...])
    we1 = low(vec[:, BASE + 4 : BASE + 4 + F_IN])
    activ, slope = gelu_both(dot(we1, feat_low) + columns_at(vec, BASE))
    grad = grad_in[...]
    grad_low = low(grad)
    d_embed = dot_tn(mats[5 * LAYERS], grad_low) * slope
    put(None, late_ref, 5 * LAYERS, dot_nt(grad_low, low(activ)))
    g_we1 = dot_nt(low(d_embed), feat_low)
    put_columns(late_ref, [(BASE, lane_fold(d_embed)), (BASE + 1, lane_fold(grad))]
                + [(BASE + 4 + j, g_we1[:, j : j + 1]) for j in range(F_IN)])
    small_ref[0] = small0[...]
    small_ref[1] = small1[...]
    cols = D // late_ref.shape[0]
    if cols * UNIT == 2 * (S + 3 * DH):
        for layer, column, row, lane, step in small_units(cols * UNIT // LAYERS, cols):
            late_ref[:, len(LATE) * cols + row, SMALL_AT + lane : SMALL_AT + lane + step] = (
                small_ref[layer, :, column : column + step]
            )
    for ref in other:
        hand_other(info, late_ref, ref)


def pack_kernel(mats_in, vecs_in, smalls_in, block_ref, mats, vecs, smalls, sems):
    finish_copies(start_copies((mats_in, vecs_in, smalls_in), (mats, vecs, smalls), sems, 0))
    count, cols, _ = mats.shape
    block_ref[: count * cols] = low(mats[...].reshape(count * cols, D))
    block_ref[count * cols :] = jnp.zeros((cols, D), BF)
    block_ref[count * cols :, : vecs.shape[1]] = low(vecs[...])
    for layer, column, row, lane, step in small_units(smalls.shape[1], cols):
        block_ref[count * cols + row : count * cols + row + 1, SMALL_AT + lane : SMALL_AT + lane + step] = low(
            smalls[layer : layer + 1, column : column + step]
        )


def locals_kernel(place, slot, info_ref):
    points = slot.shape[1]
    lanes = lax.broadcasted_iota(I32, (1, points), 1).astype(F32)
    ids = slot[...]
    edge = jnp.where(place[0] == 0, points - 1, 0).astype(F32)
    big = jnp.sum(jnp.where(lanes == edge, ids.astype(F32), 0.0)).astype(I32)
    info_ref[0] = big
    total = 0
    for j in range(LOCALS):
        mesh_id = j + jnp.where(big <= j, 1, 0)
        mine = ids == mesh_id
        first = jnp.min(jnp.where(mine, lanes, float(points))).astype(I32)
        last = jnp.max(jnp.where(mine, lanes, -1.0)).astype(I32)
        start = jnp.minimum((first >> 7) << 7, points - WINDOW)
        count_j = jnp.where(last >= 0, lax.div(jnp.maximum(last - start, 0), WINDOW) + 1, 0)
        info_ref[2 + j] = jnp.where(last >= 0, mesh_id, -1)
        info_ref[5 + j] = start
        info_ref[8 + j] = count_j
        total = total + count_j
    info_ref[1] = total
    info_ref[13] = place[1] & 1


def unpack_kernel(masks, place, *refs):
    pieces, (mats_ref, vecs_ref, *rest) = refs[: len(masks)], refs[len(masks) :]
    count, _, cols, _ = mats_ref.shape
    for mask, piece in zip(masks, pieces):
        for i in range(piece.shape[0]):
            for k in range(piece.shape[1]):
                at = (place[1] ^ (mask | (i << 1))) * piece.shape[1] + (place[0] ^ k)
                for m in range(count):
                    mats_ref[m, at] = piece[i, k, m * cols : (m + 1) * cols, :]
                vecs_ref[at] = piece[i, k, count * cols :, :].astype(F32)
    if rest:
        for layer, column, row, lane, step in small_units(cols * UNIT // LAYERS, cols):
            rest[0][layer, :, column : column + step] = low(vecs_ref[:, row, SMALL_AT + lane : SMALL_AT + lane + step])


def split_kernel(place, grads, send_ref):
    send_ref[...] = grads[:, 1 - (place[1] & 1)]


def fold_kernel(first, shift, place, *refs):
    terms, outs = refs
    index = (place[1] >> shift) & (len(outs) - 1)
    for k, out in enumerate(outs):
        total = None
        for j, term in enumerate(terms):
            value = term[index ^ k, :, place[1] & 1] if first and j == 0 else term[index ^ k]
            total = value if total is None else total + value
        out[...] = total


def join_kernel(counts, *refs):
    out, row = refs[-1], 0
    at = 0
    for count in counts:
        total = refs[at][...]
        for ref in refs[at + 1 : at + count]:
            total = total + ref[...]
        out[:, row : row + total.shape[1]] = total
        row, at = row + total.shape[1], at + count


def square_kernel(devices, early, late, rel, own_ref, sums_ref):
    wholes = []
    for parts in (early, late):
        total = parts[0]
        for j in range(1, parts.shape[0]):
            total = total + parts[j]
        wholes.append(total)
    own = jnp.concatenate(wholes, 0)
    own_ref[...] = own
    rows = lax.broadcasted_iota(I32, own.shape, 0)
    lanes = lax.broadcasted_iota(I32, own.shape, 1)
    edge = own.shape[0] // 12 * 11
    used = (rows < edge) | (lanes < BASE + 4 + F_IN + F_OUT) | ((lanes >= SMALL_AT) & (lanes < SMALL_AT + UNIT))
    squares = jnp.sum(jnp.where(used, own * own, 0.0))
    loss = jnp.sum(rel[:MESH_GRP, :1]) * (1.0 / (MESH_GRP * devices))
    which = lax.broadcasted_iota(I32, sums_ref.shape, 1)
    sums_ref[...] = jnp.where(which == 0, squares, loss)


def adamw(weight, moment, second, grad, factor):
    clipped = grad * factor
    moment = BETA_ONE * moment + (1.0 - BETA_ONE) * clipped
    second = BETA_TWO * second + (1.0 - BETA_TWO) * clipped * clipped
    moment_hat = moment / (1.0 - BETA_ONE**STEP)
    second_hat = second / (1.0 - BETA_TWO**STEP)
    updated = weight - LEARN * (moment_hat / (jnp.sqrt(second_hat) + EPS_ADAM) + DECAY * weight)
    return (moment, second, updated)


def update_kernel(sums, own, *refs):
    mats, vecs, smalls, outs = refs[:3], refs[3:6], refs[6:9], refs[9:]
    totals = jnp.sum(sums[...], 0)
    norm = jnp.sqrt(totals[:1, :1])
    factor = jnp.minimum(1.0, CLIP / norm)
    outs[0][0] = totals[1, 0]
    outs[1][0] = norm[0, 0]
    count, cols, _ = mats[0].shape
    for m in range(count):
        row = EARLY.index(m) if m in EARLY else len(EARLY) + LATE.index(m)
        for out, value in zip(outs[2:5], adamw(*[r[m] for r in mats], own[row * cols : (row + 1) * cols], factor)):
            out[m] = value
    grad = own[count * cols :, : vecs[0].shape[1]]
    for out, value in zip(outs[8:11], adamw(*[r[...] for r in vecs], grad, factor)):
        out[...] = value
    for layer, column, row, lane, step in small_units(smalls[0].shape[1], cols):
        grad = own[count * cols + row : count * cols + row + 1, SMALL_AT + lane : SMALL_AT + lane + step]
        old = [r[layer : layer + 1, column : column + step] for r in smalls]
        for out, value in zip(outs[5:8], adamw(*old, grad, factor)):
            out[layer : layer + 1, column : column + step] = value


LIMITS = dict(embed=9, small_fwd=8, middle=20, head=14, loss=8, half=20, small_bwd=4, tail=17, last=12,
              pack=3, locals=2, unpack=3, split=3, fold=3, join=3, square=3, update=4)
WORK = {}


def call(kernel, name, info, ins, outs, scratch=(), held=None, far=(), sems=0, nest=False, distant=False):
    near = len(outs)
    outs = list(outs) + list(far)
    held = {} if held is None else held
    names = list(held)
    plain = [a for a in ins if not isinstance(a, str)]
    inside = pl.BlockSpec(memory_space=pltpu.VMEM)
    table = [] if info is None else [info]
    first, second = len(table) + len(plain), len(table) + len(plain) + len(names)

    def body(*refs):
        rest = iter(refs[len(table) : first])
        kept = dict(zip(names, refs[first:second]))
        order = [kept[a] if isinstance(a, str) else next(rest) for a in ins]
        results = refs[second : second + len(outs)]
        after = refs[second + len(outs) + len(names) :]
        if nest:
            kernel(*refs[: len(table)], order, results)
        else:
            kernel(*refs[: len(table)], *order, *results, *after)

    res = pl.pallas_call(
        body,
        in_specs=[pl.BlockSpec(memory_space=pltpu.SMEM)] * len(table)
        + [pl.BlockSpec(memory_space=pltpu.HBM) if distant else inside] * (second - len(table)),
        out_specs=[
            pl.BlockSpec(memory_space=pltpu.SMEM) if len(shape) == 1 else inside for shape, _ in outs[:near]
        ]
        + [pl.BlockSpec(memory_space=pltpu.HBM)] * len(far)
        + [inside] * len(names),
        out_shape=[jax.ShapeDtypeStruct(s, t) for s, t in outs]
        + [jax.ShapeDtypeStruct(held[n].shape, held[n].dtype) for n in names],
        input_output_aliases={first + j: len(outs) + j for j in range(len(names))},
        scratch_shapes=[pltpu.VMEM(s, t) for s, t in scratch]
        + ([pltpu.SemaphoreType.DMA((sems,))] if sems else []),
        compiler_params=pltpu.CompilerParams(vmem_limit_bytes=LIMITS[name] * 2**20),
        cost_estimate=pl.CostEstimate(flops=WORK.get(name, 1000), bytes_accessed=1000, transcendentals=0),
        name=name,
    )(*table, *plain, *[held[n] for n in names])
    held.update(zip(names, res[len(outs) :]))
    return res[: len(outs)]


def swap(value, axis, mask):
    size = lax.axis_size(axis)
    return lax.ppermute(value, axis, [(i, i ^ mask) for i in range(size)])


def bit_groups(size):
    bits = size.bit_length() - 1
    groups, low = [], 1
    while low < bits:
        width = min(2, bits - low)
        groups.append((low, width))
        low += width
    return groups


def gather_pieces(block, beside):
    held = jnp.stack([block] + [swap(block, "pts", k) for k in range(1, lax.axis_size("pts"))])[None]
    held, beside = lax.optimization_barrier((held, beside))
    masks, pieces = [0], [held]
    for low, width in bit_groups(lax.axis_size("mesh")):
        held = jnp.concatenate(pieces)
        masks = [k << low for k in range(1 << width)]
        pieces = [held] + [swap(held, "mesh", m) for m in masks[1:]]
    return masks + [m | 1 for m in masks], pieces + [swap(p, "mesh", 1) for p in pieces], beside


def scatter_start(place, grads, later, gate=(), send=None):
    mesh_size, pts_size = lax.axis_size("mesh"), lax.axis_size("pts")
    rows = grads.shape[1]
    grads = grads.reshape(mesh_size // 2, 2, pts_size, rows, D)
    if send is None:
        (send,) = call(split_kernel, "split", place, (grads,), [((mesh_size // 2, pts_size, rows, D), F32)])
    terms = [grads, swap(send, "mesh", 1)]
    terms[1], *gate = lax.optimization_barrier((terms[1], *gate))
    left = mesh_size // 2
    for number, (low, width) in enumerate(reversed(bit_groups(mesh_size))):
        count = 1 << width
        left //= count
        shape = (count, left, pts_size, rows, D)
        views = [t.reshape(shape) for t in terms[1:]]
        views = [terms[0].reshape((count, left, 2) + shape[2:] if number == 0 else shape)] + views
        pieces = call(
            functools.partial(fold_kernel, number == 0, low), "fold", place, views, [(shape[1:], F32)] * count,
            nest=True,
        )
        if number == 0:
            *pieces, later = lax.optimization_barrier((*pieces, later))
        terms = [pieces[0]] + [swap(p, "mesh", k << low) for k, p in enumerate(pieces) if k]
    return [t.reshape(pts_size, rows, D) for t in terms], later, gate


def per_device(
    features,
    targets,
    mesh_slot,
    matrices,
    matrices_moment,
    matrices_second,
    smalls,
    smalls_moment,
    smalls_second,
    vectors,
    vectors_moment,
    vectors_second,
):
    groups, npts = lax.axis_size("mesh"), lax.axis_size("pts")
    devices = groups * npts
    cols, width = matrices.shape[2], smalls.shape[1]
    points = mesh_slot.shape[0]
    count_mats, count_vecs = matrices.shape[0], vectors.shape[0]
    slot = mesh_slot[None]
    place = jnp.stack([lax.axis_index("pts"), lax.axis_index("mesh")]).astype(I32)
    turned = [a.transpose(0, 2, 1) for a in (matrices, matrices_moment, matrices_second)]
    vecs = [a.T for a in (vectors, vectors_moment, vectors_second)]
    sources = (turned[0], vecs[0], smalls)
    (block,) = call(
        pack_kernel, "pack", None, sources, [((12 * cols, D), BF)], [(a.shape, F32) for a in sources],
        sems=3, distant=True,
    )
    (info,) = call(locals_kernel, "locals", place, (slot,), [((16,), I32)])
    masks, pieces, info = gather_pieces(block, info)
    direct = cols * UNIT == 2 * (S + 3 * DH)
    mats, vec, *rest = call(
        functools.partial(unpack_kernel, masks), "unpack", place, pieces,
        [((count_mats, devices, cols, D), BF), ((devices, cols, D), F32)]
        + ([((LAYERS, DH, S + 3 * DH), BF)] if direct else []),
    )
    if direct:
        small = rest[0]
    else:
        small = vec[:, :, SMALL_AT : SMALL_AT + UNIT].reshape(devices, LAYERS, width).astype(BF)
        small = small.transpose(1, 0, 2).reshape(LAYERS, DH, S + 3 * DH)
    mats = mats.reshape(count_mats, D, D)
    vec = vec.reshape(D, D)

    wide = (D, points)
    tall = (HS, points)

    def exchange(value):
        return [value] + [swap(value, "pts", k) for k in range(1, npts)]

    held = {}

    def hold(**values):
        held.update(values)

    share = [((D, HS), BF), ((S, HS), F32), ((DH, HS), BF), ((3 * DH, HS), BF), ((ND_ROWS, HS), F32)]
    acts = [(wide, BF), (wide, BF), (tall, F32)]
    nears = [(wide, F32), (tall, BF), ((LOCALS, ND_ROWS, HS), F32), ((ND_ROWS, HS), BF)]
    few_out = [((LOCALS, D, HS), BF), ((LOCALS, S, HS), F32),
               ((LOCALS, DH, HS), BF), ((LOCALS, 3 * DH, HS), BF)]

    def small_call(nd, layer):
        routed, *rest = call(
            functools.partial(small_kernel, layer), "small_fwd", info, (nd, small),
            few_out[:1], few_out[1:], None, few_out, 4,
        )
        return routed, rest

    probs_out = [(tall, F32)]
    h0, w0, nd0, send, probs0, *acts0 = call(
        embed_kernel, "embed", info, (features, slot, vec, mats, small),
        nears + probs_out, acts[:2], None, [(wide, F32)] + acts[:2], 4,
    )
    parts = exchange(send)
    routed, few0 = small_call(nd0, 0)
    h1, w1, nd1, send, probs1, *rest = call(
        functools.partial(middle_kernel, npts), "middle", info,
        (*parts, routed, w0, h0, probs0, slot, vec, mats, small),
        nears + probs_out, share + [(wide, BF), (wide, F32)] + acts[:2] + [(wide, F32)], None,
        share + [(wide, BF), (wide, F32), (wide, F32)] + acts, 11,
    )
    share0, (y0, m0, *acts1, probs0) = rest[:5], rest[5:]

    parts = exchange(send)
    routed, few1 = small_call(nd1, 1)
    y1, m1, h2, diff, loss_part, probs1, *share1 = call(
        functools.partial(head_kernel, npts), "head", info,
        (*parts, routed, w1, h1, probs1, slot, targets, vec, mats, small),
        [(wide, BF), (wide, F32), (wide, F32), ((F_OUT, points), F32), ((8, 128), F32)],
        share + [(wide, F32)], None, probs_out + share, 6,
    )
    acts0, acts1 = [*acts0, probs0], [*acts1, probs1]
    hold(y1=y1, m1=m1)

    keeps = [(wide, BF), (wide, F32)]
    ds_out = [((LOCALS, DH, HS), BF), ((DH, HS), BF)]
    parts = exchange(loss_part)
    grad2, rel, early, late = call(
        functools.partial(loss_kernel, npts, groups), "loss", info,
        (*parts, diff, slot, h2, vec),
        [(wide, F32), ((8, 128), F32), ((devices, len(EARLY) * cols, D), F32),
         ((devices, (len(LATE) + 1) * cols, D), F32)], [], held,
    )
    hold(rel=rel, early=early, late=late)

    def other_half(rows):
        return ((groups // 2, npts, rows * cols, D), F32)

    def half_call(layer, grad, middle, probs, y_low):
        other = [] if layer else [other_half(len(EARLY))]
        res = call(
            functools.partial(half_kernel, layer), "half", info,
            (grad, middle, probs, y_low, slot, vec, mats, "early", "late"), ds_out + keeps + other, [((LOCALS, DH, HS), F32)], held,
        )
        return res[0], res[1], res[2:4], res[4:]

    def small_back(layer, ds, nd, few):
        return call(
            functools.partial(small_back_kernel, layer), "small_bwd", info,
            (ds, nd, few[1], few[2], few[3], few[0], small),
            [((LOCALS, HS, HS), BF), ((LOCALS, D, HS), BF),
             ((LOCALS, HS, 128), F32), ((DH, 3 * DH), F32)],
        )

    tail_scratch = [(tall, F32), (wide, F32)]

    def tail_ins(parts, back, keep, share, acts):
        return (*parts, *back, share[4], share[1], share[2], share[3], share[0], small, *acts, *keep, slot, vec, mats)

    ds, send, keep, _ = half_call(1, grad2, held.pop("m1"), acts1[3], held.pop("y1"))
    parts = exchange(send)
    back = small_back(1, ds, nd1, few1)
    grad1, small1 = call(
        functools.partial(tail_kernel, npts, 1), "tail", info,
        (*tail_ins(parts, back, keep, share1, acts1), "late", "early"),
        [(wide, F32), ((DH, S + 3 * DH), F32)], tail_scratch, held,
    )
    ds, send, keep, other = half_call(0, grad1, m0, acts0[3], y0)
    parts = exchange(send)
    back = small_back(0, ds, nd0, few0)
    early_terms, after, gate = scatter_start(place, held.pop("early"), features, (*parts[1:], back[3]), other[0])
    parts, back = parts[:1] + gate[:-1], [*back[:3], gate[-1]]
    grad0, small0 = call(
        functools.partial(tail_kernel, npts, 0), "tail", info,
        (*tail_ins(parts, back, keep, share0, acts0), "late"),
        [(wide, F32), ((DH, S + 3 * DH), F32)], tail_scratch, held,
    )
    (joined,) = call(
        functools.partial(join_kernel, (len(early_terms),)), "join", None, early_terms,
        [((npts, len(EARLY) * cols, D), F32)],
    )
    joined, after = lax.optimization_barrier((joined, after))
    early_own = lax.all_to_all(joined, "pts", 0, 0)
    small_out, *other = call(
        last_kernel, "last", info, (grad0, after, vec, mats, small0, small1, "late"),
        [((LAYERS, DH, S + 3 * DH), F32)] + ([other_half(len(LATE) + 1)] if direct else []), (), held,
    )
    late = held.pop("late")
    if not direct:
        few = small_out.reshape(LAYERS, devices, width).transpose(1, 0, 2).reshape(devices, cols, UNIT)
        late = late.at[:, len(LATE) * cols :, SMALL_AT : SMALL_AT + UNIT].set(few)
    late_terms, *_ = scatter_start(place, late, after, (), other[0] if direct else None)
    (joined,) = call(
        functools.partial(join_kernel, (len(late_terms),)), "join", None, late_terms,
        [((npts, (len(LATE) + 1) * cols, D), F32)],
    )
    own, sums = call(
        functools.partial(square_kernel, devices), "square", None,
        (early_own, lax.all_to_all(joined, "pts", 0, 0), held.pop("rel")),
        [((12 * cols, D), F32), ((devices, 2, 128), F32)],
    )
    sums = lax.all_to_all(sums, ALL, 0, 0)
    cube, flat = [((count_mats, cols, D), F32)] * 3, [((LAYERS, width), F32)] * 3
    loss, grad_norm, *new = call(
        update_kernel, "update", None,
        (sums, own, *turned, *vecs, smalls, smalls_moment, smalls_second),
        [((1,), F32)] * 2 + cube + flat + [((cols, count_vecs), F32)] * 3,
    )
    return (
        loss.reshape(()), grad_norm.reshape(()),
        *[a.transpose(0, 2, 1) for a in new[:3]], *new[3:6], *[a.T for a in new[6:]],
    )


def solution(mesh):
    both = ("mesh", "pts")
    cube, flat = P(None, None, both), P(None, both)
    return jax.shard_map(
        per_device,
        mesh=mesh,
        in_specs=(flat, flat, P(both), cube, cube, cube, flat, flat, flat, flat, flat, flat),
        out_specs=(P(), P(), cube, cube, cube, flat, flat, flat, flat, flat, flat),
        check_vma=False,
    )
```
